32 devices in a mesh: rep: 4 (over y, x), fsdp: 8 (over z, core).
Axes of the slice: x: 2, y: 2, z: 4, core: 2. Of those that a mesh axis runs over, the one named last changes fastest.
Arguments:
- inputs: float32 [4, 1024, 768], P('rep', 'fsdp'), may hold values from -6 to 6
- encoder: float32 [4, 128, 768], P('rep', 'fsdp'), may hold values from -6 to 6
- self_gain: float32 [768], P('fsdp'), may hold values from 0.5 to 1.5
- cross_gain: float32 [768], P('fsdp'), may hold values from 0.5 to 1.5
- ffn_gain: float32 [768], P('fsdp'), may hold values from 0.5 to 1.5
- self_query: float32 [768, 768], P('fsdp')
- self_key: float32 [768, 768], P('fsdp'), may hold values from -0.21875 to 0.21875
- self_value: float32 [768, 768], P('fsdp'), may hold values from -0.21875 to 0.21875
- self_output: float32 [768, 768], P('fsdp'), may hold values from -1.25 to 1.25
- position_bias: float32 [32, 12], replicated, may hold values from -4 to 4
- bucket_table: int32 [1024], replicated, may hold values from 0 to 31, as said below
- cross_query: float32 [768, 768], P('fsdp')
- cross_key: float32 [768, 768], P('fsdp'), may hold values from -0.21875 to 0.21875
- cross_value: float32 [768, 768], P('fsdp'), may hold values from -0.21875 to 0.21875
- cross_output: float32 [768, 768], P('fsdp'), may hold values from -0.875 to 0.875
- ffn_gate: float32 [768, 2048], P(None, 'fsdp'), may hold values from -0.21875 to 0.21875
- ffn_up: float32 [768, 2048], P(None, 'fsdp'), may hold values from -0.21875 to 0.21875
- ffn_down: float32 [2048, 768], P('fsdp'), may hold values from -0.125 to 0.125
- cotangent: float32 [4, 1024, 768], P('rep', 'fsdp'), may hold values from -6 to 6
Outputs:
- outputs: float32 [4, 1024, 768], P('rep', 'fsdp')
- grad_inputs: float32 [4, 1024, 768], P('rep', 'fsdp')
- grad_encoder: float32 [4, 128, 768], P('rep', 'fsdp')
- grad_self_gain: float32 [768], P('fsdp')
- grad_cross_gain: float32 [768], P('fsdp')
- grad_ffn_gain: float32 [768], P('fsdp')
- grad_self_query: float32 [768, 768], P('fsdp')
- grad_self_key: float32 [768, 768], P('fsdp')
- grad_self_value: float32 [768, 768], P('fsdp')
- grad_self_output: float32 [768, 768], P('fsdp')
- grad_position_bias: float32 [32, 12], P('fsdp')
- grad_cross_query: float32 [768, 768], P('fsdp')
- grad_cross_key: float32 [768, 768], P('fsdp')
- grad_cross_value: float32 [768, 768], P('fsdp')
- grad_cross_output: float32 [768, 768], P('fsdp')
- grad_ffn_gate: float32 [768, 2048], P(None, 'fsdp')
- grad_ffn_up: float32 [768, 2048], P(None, 'fsdp')
- grad_ffn_down: float32 [2048, 768], P('fsdp')
The draws below stay inside these ranges and needn't reach their ends.
Inputs may be any that keep to these rules, and one draw needn't show every extreme that they name: bucket_table[d] is the bucket of a key d positions before its query: d for d < 16, never falling as d grows, and 31 for every d >= 127.
All inputs are finite; a program needn't handle non-finite values.
Results may differ from the reference program's by a relative error of at most 0.0003.
Values sent between devices are 32-bit elements; how exact they have to be, the bound alone decides.
A program may use at most 256 MiB of HBM per device.

```python
import math
import jax
import jax.numpy as jnp
from jax import lax

D = 768
H = 12
DH = 64
FF = 2048
NB = 32
MAXDIST = 128
SEQ_LEN = 1024
ENC = 128
SEQS = 4


def query_weight(key):
    return jax.random.normal(jax.random.fold_in(key, 3), (D, D), jnp.float32) / math.sqrt(D * DH)


def draw_self_query(key, part):
    return query_weight(jax.random.fold_in(key, 21))


def draw_cross_query(key, part):
    return query_weight(jax.random.fold_in(key, 22))


def draw_bucket_table(key, part):
    half_count = NB // 2
    distance = jnp.arange(SEQ_LEN, dtype=jnp.int32)
    spread_count = MAXDIST - half_count - 1
    thresholds = jax.random.permutation(jax.random.fold_in(key, 31), spread_count)[:half_count - 1] + half_count + 1
    above = jnp.sum((thresholds[None, :] <= distance[:, None]).astype(jnp.int32), axis=1)
    middle_ids = half_count + above
    return jnp.where(distance < half_count, distance, jnp.where(distance >= MAXDIST - 1, NB - 1, middle_ids)).astype(jnp.int32)


def steps_of(rng, dims, split, low, high):
    def one(position, parts):
        steps = jax.random.uniform(jax.random.fold_in(jax.random.fold_in(rng, 6), position), (parts,), jnp.float32, low / len(split), high / len(split))
        return jnp.repeat(jnp.exp(steps), dims[position] // parts).reshape((-1,) + (1,) * (len(dims) - position - 1))

    factor_of = one(*split[0])
    for cut in split[1:]:
        factor_of = factor_of * one(*cut)
    return factor_of


def bell_draw(own_key, dims, spread, limit, pieces=(), kind=jnp.bfloat16):
    array = jax.random.normal(own_key, dims, jnp.float32) * spread
    if len(pieces) > 0:
        array = steps_of(own_key, dims, pieces, -0.22, 0.18) * array
    return jnp.clip(array, min=-limit, max=limit).astype(kind)


def setup_inputs(seed: int = 0) -> dict:
    key_list = jax.random.split(jax.random.key(seed), 20)
    return {
        "inputs": bell_draw(key_list[0], (SEQS, SEQ_LEN, D), 1.0, 6.0, ((0, 4), (1, 8)), jnp.float32),
        "encoder": bell_draw(key_list[1], (SEQS, ENC, D), 1.0, 6.0, ((0, 4), (1, 8)), jnp.float32),
        "self_gain": jnp.clip(1.0 + 0.1 * jax.random.normal(key_list[2], (D,), jnp.float32), 0.5, 1.5),
        "cross_gain": jnp.clip(1.0 + 0.1 * jax.random.normal(key_list[3], (D,), jnp.float32), 0.5, 1.5),
        "ffn_gain": jnp.clip(1.0 + 0.1 * jax.random.normal(key_list[4], (D,), jnp.float32), 0.5, 1.5),
        "self_query": draw_self_query(jax.random.fold_in(key_list[19], 71), 0),
        "self_key": bell_draw(key_list[6], (D, D), D ** -0.5, 0.21875, ((0, 8),), jnp.float32),
        "self_value": bell_draw(key_list[7], (D, D), D ** -0.5, 0.21875, ((0, 8),), jnp.float32),
        "self_output": bell_draw(key_list[8], (D, D), (D // 32) ** -0.5, 1.25, ((0, 8),), jnp.float32),
        "position_bias": bell_draw(key_list[9], (NB, H), 1.0, 4.0, (), jnp.float32),
        "bucket_table": draw_bucket_table(jax.random.fold_in(key_list[19], 71), 0),
        "cross_query": draw_cross_query(jax.random.fold_in(key_list[19], 71), 0),
        "cross_key": bell_draw(key_list[12], (D, D), D ** -0.5, 0.21875, ((0, 8),), jnp.float32),
        "cross_value": bell_draw(key_list[13], (D, D), D ** -0.5, 0.21875, ((0, 8),), jnp.float32),
        "cross_output": bell_draw(key_list[14], (D, D), (D // 16) ** -0.5, 0.875, ((0, 8),), jnp.float32),
        "ffn_gate": bell_draw(key_list[15], (D, FF), D ** -0.5, 0.21875, ((1, 8),), jnp.float32),
        "ffn_up": bell_draw(key_list[16], (D, FF), D ** -0.5, 0.21875, ((1, 8),), jnp.float32),
        "ffn_down": bell_draw(key_list[17], (FF, D), FF ** -0.5, 0.125, ((0, 8),), jnp.float32),
        "cotangent": bell_draw(key_list[18], (SEQS, SEQ_LEN, D), 1.0, 6.0, ((0, 4), (1, 8)), jnp.float32),
    }


PRECISE = lax.Precision.HIGHEST
eps_norm = 1e-06

def matmul(matrix_a, matrix_b):
    return jnp.dot(matrix_a, matrix_b, precision=PRECISE, preferred_element_type=jnp.float32)

def rms_norm(hidden_state, gain_full):
    return hidden_state * lax.rsqrt(lax.optimization_barrier(jnp.mean(hidden_state * hidden_state, axis=-1, keepdims=True)) + eps_norm) * gain_full

def self_block(query_block, block_start, keys_heads, values_heads, position_bias, bucket_table):
    query_pos = block_start + jnp.arange(query_block.shape[0], dtype=jnp.int32)
    key_pos = jnp.arange(keys_heads.shape[0], dtype=jnp.int32)
    distance = query_pos[:, None] - key_pos[None, :]
    bucket_ids = jnp.take(bucket_table, jnp.maximum(distance, 0).astype(jnp.int32), axis=0)
    score_bias = jnp.take(position_bias, bucket_ids, axis=0)
    scores = jnp.einsum('qhd,khd->hqk', query_block, keys_heads, precision=PRECISE) + jnp.transpose(score_bias, (2, 0, 1))
    scores = jnp.where((distance >= 0)[None], scores, -jnp.inf)
    attn_probs = jax.nn.softmax(scores, axis=-1)
    return jnp.einsum('hqk,khd->qhd', attn_probs, values_heads, precision=PRECISE)

def layer(params, block_in, enc_rows, bucket_table):
    self_gain, cross_gain, ffn_gain, self_query, self_key, self_value, self_output, position_bias, cross_query, cross_key, cross_value, cross_output, ffn_gate, ffn_up, ffn_down = params
    seq_rows, model_width = block_in.shape
    head_count = position_bias.shape[1]
    head_dim = model_width // head_count
    normed_one = rms_norm(block_in, self_gain)
    query_heads = matmul(normed_one, self_query).reshape(seq_rows, head_count, head_dim)
    keys_heads = matmul(normed_one, self_key).reshape(seq_rows, head_count, head_dim)
    values_heads = matmul(normed_one, self_value).reshape(seq_rows, head_count, head_dim)
    block_rows = min(512, seq_rows)
    block_count = seq_rows // block_rows
    starts = (jnp.arange(block_count, dtype=jnp.int32) * block_rows).astype(jnp.int32)
    blocks = query_heads.reshape(block_count, block_rows, head_count, head_dim)

    def one_block(block_pair):
        return self_block(block_pair[0], block_pair[1], keys_heads, values_heads, position_bias, bucket_table)
    attended = lax.map(jax.checkpoint(one_block), (blocks, starts)).reshape(seq_rows, model_width)
    after = block_in + matmul(attended, self_output)
    normed_two = rms_norm(after, cross_gain)
    enc_count = enc_rows.shape[0]
    cross_q = matmul(normed_two, cross_query).reshape(seq_rows, head_count, head_dim)
    cross_k = matmul(enc_rows, cross_key).reshape(enc_count, head_count, head_dim)
    cross_v = matmul(enc_rows, cross_value).reshape(enc_count, head_count, head_dim)
    cross_scores = jnp.einsum('qhd,khd->hqk', cross_q, cross_k, precision=PRECISE)
    cross_probs = jax.nn.softmax(cross_scores, axis=-1)
    cross_att = jnp.einsum('hqk,khd->qhd', cross_probs, cross_v, precision=PRECISE).reshape(seq_rows, model_width)
    middle = after + matmul(cross_att, cross_output)
    normed_three = rms_norm(middle, ffn_gain)
    inner_act = jax.nn.gelu(matmul(normed_three, ffn_gate), approximate=True) * matmul(normed_three, ffn_up)
    return middle + matmul(inner_act, ffn_down)

def reference(inputs, encoder, self_gain, cross_gain, ffn_gain, self_query, self_key, self_value, self_output, position_bias, bucket_table, cross_query, cross_key, cross_value, cross_output, ffn_gate, ffn_up, ffn_down, cotangent):
    params = (self_gain, cross_gain, ffn_gain, self_query, self_key, self_value, self_output, position_bias, cross_query, cross_key, cross_value, cross_output, ffn_gate, ffn_up, ffn_down)
    zero_grads = jax.tree.map(jnp.zeros_like, params)

    def per_sequence(totals, items):
        block_in, enc_rows, grad_top = items

        def forward(param_set, rows_in, enc_in):
            return layer(param_set, rows_in, enc_in, bucket_table)
        result, pullback = jax.vjp(forward, params, block_in, enc_rows)
        grad_params, grad_rows, grad_enc = pullback(grad_top)
        totals = jax.tree.map(jnp.add, totals, grad_params)
        return (totals, (result, grad_rows, grad_enc))
    totals, (results, grad_rows, grad_enc) = lax.scan(per_sequence, zero_grads, (inputs, encoder, cotangent))
    return (results, grad_rows, grad_enc, totals[0], totals[1], totals[2], totals[3], totals[4], totals[5], totals[6], totals[7], totals[8], totals[9], totals[10], totals[11], totals[12], totals[13], totals[14])
```

```python
import functools
import math

import jax
import jax.numpy as jnp
from jax import lax
from jax.experimental import pallas as pl
from jax.experimental.pallas import tpu as pltpu
from jax.sharding import PartitionSpec as P

HIGH = lax.Precision.HIGH
MESH = pl.DeviceIdType.MESH
F32 = jnp.float32
eps_norm = 1e-06
gelu_coef = math.sqrt(2.0 / math.pi)
masked_score = -1e30
vmem_bytes = 56 << 20


def mm(a, b):
    return jnp.dot(a, b, precision=HIGH, preferred_element_type=F32)


def mm_tn(a, b):
    return lax.dot_general(
        a, b, (((0,), (0,)), ((), ())), precision=HIGH, preferred_element_type=F32
    )


def mm_nt(a, b):
    return lax.dot_general(
        a, b, (((1,), (1,)), ((), ())), precision=HIGH, preferred_element_type=F32
    )


def unit_of(rows):
    scale = lax.rsqrt(jnp.mean(rows * rows, axis=-1, keepdims=True) + eps_norm)
    return rows * scale, scale


def unit_backward(grad_unit, unit, scale):
    return scale * (grad_unit - unit * jnp.mean(grad_unit * unit, axis=-1, keepdims=True))


def gelu_parts(gate_pre):
    squared = gate_pre * gate_pre
    tangent = jnp.tanh(gelu_coef * (gate_pre + 0.044715 * squared * gate_pre))
    gelu_out = 0.5 * gate_pre * (1.0 + tangent)
    gelu_slope = 0.5 * (1.0 + tangent) + 0.5 * gate_pre * (1.0 - tangent * tangent) * gelu_coef * (
        1.0 + 3.0 * 0.044715 * squared
    )
    return (gelu_out, gelu_slope)


def my_place(R):
    rep = lax.axis_index("rep")
    f = lax.axis_index("fsdp")
    return rep, f, f // R, lax.rem(f, R)


def greet(peers):
    barrier = pltpu.get_barrier_semaphore()
    for peer in peers:
        pl.semaphore_signal(barrier, inc=1, device_id=peer, device_id_type=MESH)
    pl.semaphore_wait(barrier, len(peers))


def remote(src, dst, send_sem, recv_sem, peer):
    return pltpu.make_async_remote_copy(
        src_ref=src,
        dst_ref=dst,
        send_sem=send_sem,
        recv_sem=recv_sem,
        device_id=peer,
        device_id_type=MESH,
    )


def lane_peers(rep, g, r, G, R):
    return [(rep, lax.rem(g + k, G) * R + r) for k in range(1, G)]


def group_peers(rep, g, r, G, R):
    return [(rep, g * R + lax.rem(r + j, R)) for j in range(1, R)]


def comm_call(kernel, outs, ins, scratch, collective_id, vmem_ins=False, vmem_outs=False):
    def space(vmem):
        return pl.BlockSpec(memory_space=pltpu.VMEM if vmem else pl.ANY)

    return pl.pallas_call(
        kernel,
        out_shape=outs,
        in_specs=[space(vmem_ins)] * len(ins),
        out_specs=[space(vmem_outs)] * len(outs),
        scratch_shapes=scratch,
        compiler_params=pltpu.CompilerParams(
            collective_id=collective_id, has_side_effects=True, vmem_limit_bytes=vmem_bytes
        ),
    )(*ins)


def gather_kernel(G, R, own, spread, *refs):
    count = own + spread
    ins, outs = refs[:count], refs[count : 2 * count]
    local_sem, lane_send, lane_recv, group_send, group_recv = refs[2 * count :]
    rep, f, g, r = my_place(R)
    lanes = lane_peers(rep, g, r, G, R)
    groups = group_peers(rep, g, r, G, R)
    greet(lanes + groups)

    def source(a, k):
        return ins[a] if a < own else ins[a].at[lax.rem(g + k, G)]

    lane_copies, group_copies, locals_ = [], [], []
    for a in range(count):
        for k in range(G - 1, 0, -1):
            copy = remote(
                source(a, k), outs[a].at[f], lane_send.at[a, k - 1], lane_recv.at[a, k - 1], lanes[k - 1]
            )
            copy.start()
            lane_copies.append((a, k, copy))
    for a in range(count):
        copy = pltpu.make_async_copy(source(a, 0), outs[a].at[f], local_sem.at[a])
        copy.start()
        locals_.append(copy)
        for j in range(1, R):
            copy = remote(
                source(a, 0),
                outs[a].at[f],
                group_send.at[a, j - 1, 0],
                group_recv.at[a, j - 1, 0],
                groups[j - 1],
            )
            copy.start()
            group_copies.append(copy)
    for a, k, copy in sorted(lane_copies, key=lambda t: (t[0], t[1])):
        copy.wait_recv()
        came = lax.rem(g + G - k, G) * R + r
        for j in range(1, R):
            onward = remote(
                outs[a].at[came],
                outs[a].at[came],
                group_send.at[a, j - 1, k],
                group_recv.at[a, j - 1, k],
                groups[j - 1],
            )
            onward.start()
            group_copies.append(onward)
    for copy in group_copies:
        copy.wait()
    for _, _, copy in lane_copies:
        copy.wait_send()
    for copy in locals_:
        copy.wait()


def gather(G, R, own, spread, collective_id):
    n = G * R
    outs = [jax.ShapeDtypeStruct((n,) + x.shape, x.dtype) for x in own]
    outs += [jax.ShapeDtypeStruct((n,) + x.shape[1:], x.dtype) for x in spread]
    count = len(outs)
    sem = pltpu.SemaphoreType.DMA
    return comm_call(
        functools.partial(gather_kernel, G, R, len(own), len(spread)),
        outs,
        list(own) + list(spread),
        [
            sem((count,)),
            sem((count, G - 1)),
            sem((count, G - 1)),
            sem((count, R - 1, G)),
            sem((count, R - 1, G)),
        ],
        collective_id,
    )


def lane_kernel(G, R, x_ref, o_ref, local_sem, lane_send, lane_recv):
    rep, f, g, r = my_place(R)
    lanes = lane_peers(rep, g, r, G, R)
    greet(lanes)
    copies = []
    for k in range(G - 1, 0, -1):
        copy = remote(
            x_ref.at[lax.rem(g + k, G)], o_ref.at[g], lane_send.at[k - 1], lane_recv.at[k - 1], lanes[k - 1]
        )
        copy.start()
        copies.append(copy)
    own = pltpu.make_async_copy(x_ref.at[g], o_ref.at[g], local_sem)
    own.start()
    own.wait()
    for copy in copies:
        copy.wait()


def lane_exchange(G, R, x, collective_id):
    sem = pltpu.SemaphoreType.DMA
    return comm_call(
        functools.partial(lane_kernel, G, R),
        [jax.ShapeDtypeStruct(x.shape, x.dtype)],
        [x],
        [sem, sem((G - 1,)), sem((G - 1,))],
        collective_id,
    )[0]


def scatter_kernel(G, R, pooled, summed, x_ref, o_ref, *scratch):
    rep, f, g, r = my_place(R)
    lanes = lane_peers(rep, g, r, G, R)
    groups = group_peers(rep, g, r, G, R) if pooled else []
    if pooled:
        group_buf, group_send, group_recv = scratch[:3]
        scratch = scratch[3:]
    lane_out, lane_in, lane_send, lane_recv = scratch
    greet(lanes + groups)
    order = list(range(G - 1, -1, -1))
    group_copies = []
    if pooled:
        for k in order:
            for j in range(1, R):
                copy = remote(
                    x_ref.at[lax.rem(g + k, G), lax.rem(r + j, R)],
                    group_buf.at[j - 1, k],
                    group_send.at[j - 1, k],
                    group_recv.at[j - 1, k],
                    groups[j - 1],
                )
                copy.start()
                group_copies.append((j, k, copy))
    lane_copies = []
    for k in order:
        to = lax.rem(g + k, G)
        if pooled:
            for j, kk, copy in group_copies:
                if kk == k:
                    copy.wait_recv()
            total = x_ref[to, r]
            for j in range(1, R):
                total = total + group_buf[j - 1, k]
        else:
            total = x_ref[to]
        if k > 0:
            lane_out[k - 1] = total
            copy = remote(
                lane_out.at[k - 1], lane_in.at[k - 1], lane_send.at[k - 1], lane_recv.at[k - 1], lanes[k - 1]
            )
            copy.start()
            lane_copies.append((k, copy))
        elif summed:
            o_ref[...] = total
        else:
            o_ref[g] = total
    for k, copy in lane_copies:
        copy.wait_recv()
        if summed:
            o_ref[...] += lane_in[k - 1]
        else:
            o_ref[lax.rem(g + G - k, G)] = lane_in[k - 1]
    for _, copy in lane_copies:
        copy.wait_send()
    for _, _, copy in group_copies:
        copy.wait_send()


def scatter(G, R, x, pooled, summed, collective_id):
    block = x.shape[2:] if pooled else x.shape[1:]
    sem = pltpu.SemaphoreType.DMA
    scratch = []
    if pooled:
        scratch = [
            pltpu.VMEM((max(R - 1, 1), G) + block, F32),
            sem((max(R - 1, 1), G)),
            sem((max(R - 1, 1), G)),
        ]
    scratch += [
        pltpu.VMEM((G - 1,) + block, F32),
        pltpu.VMEM((G - 1,) + block, F32),
        sem((G - 1,)),
        sem((G - 1,)),
    ]
    out = jax.ShapeDtypeStruct(block if summed else (G,) + block, F32)
    return comm_call(
        functools.partial(scatter_kernel, G, R, pooled, summed),
        [out],
        [x],
        scratch,
        collective_id,
        vmem_ins=True,
        vmem_outs=True,
    )[0]


def group_kernel(G, R, x_ref, o_ref, group_buf, group_send, group_recv):
    rep, f, g, r = my_place(R)
    groups = group_peers(rep, g, r, G, R)
    greet(groups)
    copies = []
    for j in range(1, R):
        copy = remote(
            x_ref.at[:, lax.rem(r + j, R)],
            group_buf.at[j - 1],
            group_send.at[j - 1],
            group_recv.at[j - 1],
            groups[j - 1],
        )
        copy.start()
        copies.append(copy)
    for copy in copies:
        copy.wait()
    total = x_ref[:, r]
    for j in range(1, R):
        total = total + group_buf[j - 1]
    o_ref[...] = total


def group_sum(G, R, x, collective_id):
    shape = (x.shape[0],) + x.shape[2:]
    sem = pltpu.SemaphoreType.DMA
    return comm_call(
        functools.partial(group_kernel, G, R),
        [jax.ShapeDtypeStruct(shape, F32)],
        [x],
        [pltpu.VMEM((R - 1,) + shape, F32), sem((R - 1,)), sem((R - 1,))],
        collective_id,
        vmem_ins=True,
        vmem_outs=True,
    )[0]


def attention_kernel(
    G, R, heads, dh, x_ref, w_ref, vec_ref, att_ref, q_ref, k_ref, v_ref, lse_ref, unit_ref, strip_ref
):
    r = lax.rem(lax.axis_index("fsdp"), R)
    T = att_ref.shape[1]
    C = heads * dh
    S = x_ref.shape[0]
    chunk = 256

    @pl.loop(0, S // chunk)
    def _(c):
        rows = pl.ds(pl.multiple_of(c * chunk, chunk), chunk)
        unit, _ = unit_of(x_ref[rows, :])
        unit_ref[rows, :] = unit
        kv = mm(unit, w_ref[:, C:])
        for h in range(heads):
            k_ref[h, rows, :] = kv[:, h * dh : (h + 1) * dh]
            v_ref[h, rows, :] = kv[:, C + h * dh : C + (h + 1) * dh]

    @pl.loop(0, G)
    def _(i):
        rows = pl.ds(pl.multiple_of((i * R + r) * T, T), T)
        q = mm(unit_ref[rows, :], w_ref[:, :C])
        for h in range(heads):
            q_ref[h, pl.ds(pl.multiple_of(i * T, T), T), :] = q[:, h * dh : (h + 1) * dh]

    make_strips(R, heads, T, vec_ref, strip_ref)
    for i in range(G):
        L = R * (i + 1) * T
        outs = []
        for h in range(heads):
            scores = strip_scores(R, T, i, r, h, L, k_ref, q_ref, strip_ref)
            top = jnp.max(scores, axis=0, keepdims=True)
            probs = jnp.exp(scores - top)
            total = jnp.sum(probs, axis=0, keepdims=True)
            out_t = mm_tn(v_ref[h, :L, :], probs) / total
            outs.append(out_t.T)
            lse_ref[i, h : h + 1, :] = top + jnp.log(total)
        att_ref[i] = jnp.concatenate(outs, axis=1)


def make_strips(R, heads, T, vec_ref, strip_ref):
    for h in range(heads):
        vec = jnp.broadcast_to(vec_ref[h : h + 1, :], (2 * T, 3 * T))
        pair = pltpu.roll(vec, 0, 1, stride=1, stride_axis=0)[:, :T]
        if R > 1:
            strip_ref[h, : (R - 1) * T, :] = jnp.zeros(((R - 1) * T, T), F32)
            strip_ref[h, (R + 1) * T :, :] = jnp.full(((R - 1) * T, T), masked_score, F32)
        strip_ref[h, (R - 1) * T : (R + 1) * T, :] = pair


def strip_scores(R, T, i, r, h, L, k_ref, q_ref, strip_ref):
    scores = mm_nt(k_ref[h, :L, :], q_ref[h, i * T : (i + 1) * T, :])
    skip = 1 if i == 0 else 0
    width = (R + 1 - skip) * T
    start = pl.multiple_of((R - 1 - r + skip) * T, T)
    near = scores[L - width :, :] + strip_ref[h, pl.ds(start, width), :]
    if width == L:
        return near
    return jnp.concatenate([scores[: L - width, :], near], axis=0)


def attention_forward(G, R, heads, dh, x_all, w_cols, vec):
    S = x_all.shape[0]
    T = S // (G * R)
    C = heads * dh
    vm = pl.BlockSpec(memory_space=pltpu.VMEM)
    return pl.pallas_call(
        functools.partial(attention_kernel, G, R, heads, dh),
        out_shape=[
            jax.ShapeDtypeStruct((G, T, C), F32),
            jax.ShapeDtypeStruct((heads, G * T, dh), F32),
            jax.ShapeDtypeStruct((heads, S, dh), F32),
            jax.ShapeDtypeStruct((heads, S, dh), F32),
            jax.ShapeDtypeStruct((G, 8, T), F32),
        ],
        in_specs=[vm] * 3,
        out_specs=[vm] * 5,
        scratch_shapes=[pltpu.VMEM((S, x_all.shape[1]), F32), pltpu.VMEM((heads, 2 * R * T, T), F32)],
        compiler_params=pltpu.CompilerParams(vmem_limit_bytes=vmem_bytes),
    )(x_all, w_cols, vec)


def attention_back_kernel(
    G,
    R,
    heads,
    dh,
    buckets,
    q_ref,
    k_ref,
    v_ref,
    lse_ref,
    att_ref,
    grad_ref,
    vec_ref,
    ids_ref,
    dq_ref,
    dkv_ref,
    gbias_ref,
    strip_ref,
    near_ref,
    far_ref,
    dk_ref,
    dv_ref,
):
    r = lax.rem(lax.axis_index("fsdp"), R)
    T = att_ref.shape[1]
    C = heads * dh
    make_strips(R, heads, T, vec_ref, strip_ref)
    near_ref[...] = jnp.zeros_like(near_ref)
    far_ref[...] = jnp.zeros_like(far_ref)
    for i in range(G - 1, -1, -1):
        L = R * (i + 1) * T
        grad = grad_ref[i]
        prod_t = (grad * att_ref[i]).T
        dqs = []
        for h in range(heads):
            scores = strip_scores(R, T, i, r, h, L, k_ref, q_ref, strip_ref)
            probs = jnp.exp(scores - lse_ref[i, h : h + 1, :])
            grad_h = grad[:, h * dh : (h + 1) * dh]
            delta = jnp.sum(prod_t[h * dh : (h + 1) * dh, :], axis=0, keepdims=True)
            dscores = probs * (mm_nt(v_ref[h, :L, :], grad_h) - delta)
            q_h = q_ref[h, i * T : (i + 1) * T, :]
            dv = mm(probs, grad_h)
            dk = mm(dscores, q_h)
            if i == G - 1:
                dv_ref[h] = dv
                dk_ref[h] = dk
            else:
                dv_ref[h, :L, :] += dv
                dk_ref[h, :L, :] += dk
            dqs.append(mm_tn(k_ref[h, :L, :], dscores).T)
            skip = 1 if i == 0 else 0
            width = (R + 1 - skip) * T
            near_ref[h, skip * T :, :] += dscores[L - width :, :]
            if width < L:
                far_ref[h : h + 1, :] += jnp.sum(dscores[: L - width, :], axis=0, keepdims=True)
        dq_ref[i] = jnp.concatenate(dqs, axis=1)
    S = dkv_ref.shape[0]
    for c in range(0, S, 256):
        rows = slice(c, c + 256)
        parts = [dk_ref[h, rows, :] for h in range(heads)] + [dv_ref[h, rows, :] for h in range(heads)]
        dkv_ref[rows, :] = jnp.concatenate(parts, axis=1)
    ids = jnp.broadcast_to(ids_ref[0:1, :], (2 * T, 3 * T))
    ids = pltpu.roll(ids, 0, 1, stride=1, stride_axis=0)[:, :T]
    for h in range(heads):
        pair = near_ref[h, pl.ds(pl.multiple_of(r * T, T), 2 * T), :]
        far = far_ref[h : h + 1, :]
        for idx in range(R - 1):
            block = jnp.sum(near_ref[h, idx * T : (idx + 1) * T, :], axis=0, keepdims=True)
            far = far + jnp.where(idx < r, block, 0.0)
        for b in range(buckets):
            part = jnp.sum(jnp.where(ids == b, pair, 0.0), axis=0, keepdims=True)
            if b == buckets - 1:
                part = part + far
            gbias_ref[h, b : b + 1, :] = part


def attention_backward(G, R, heads, dh, buckets, q, k, v, lse, att, grad, vec, ids):
    S = k.shape[1]
    T = S // (G * R)
    C = heads * dh
    vm = pl.BlockSpec(memory_space=pltpu.VMEM)
    return pl.pallas_call(
        functools.partial(attention_back_kernel, G, R, heads, dh, buckets),
        out_shape=[
            jax.ShapeDtypeStruct((G, T, C), F32),
            jax.ShapeDtypeStruct((S, 2 * C), F32),
            jax.ShapeDtypeStruct((heads, buckets, T), F32),
        ],
        in_specs=[vm] * 8,
        out_specs=[vm] * 3,
        scratch_shapes=[
            pltpu.VMEM((heads, 2 * R * T, T), F32),
            pltpu.VMEM((heads, (R + 1) * T, T), F32),
            pltpu.VMEM((8, T), F32),
            pltpu.VMEM((heads, S, dh), F32),
            pltpu.VMEM((heads, S, dh), F32),
        ],
        compiler_params=pltpu.CompilerParams(vmem_limit_bytes=vmem_bytes),
    )(q, k, v, lse, att, grad, vec, ids)


def to_heads(rows, heads):
    return jnp.transpose(rows.reshape(rows.shape[0], heads, -1), (1, 0, 2))


def from_heads(rows):
    return jnp.transpose(rows, (1, 0, 2)).reshape(rows.shape[1], -1)


def bmm(spec, a, b):
    return jnp.einsum(spec, a, b, precision=HIGH, preferred_element_type=F32)


def shards(
    n,
    inputs,
    encoder,
    self_gain,
    cross_gain,
    ffn_gain,
    self_query,
    self_key,
    self_value,
    self_output,
    position_bias,
    bucket_table,
    cross_query,
    cross_key,
    cross_value,
    cross_output,
    ffn_gate,
    ffn_up,
    ffn_down,
    cotangent,
):
    x = inputs[0]
    enc = encoder[0]
    cot = cotangent[0]
    T, D = x.shape
    buckets, H = position_bias.shape
    dh = D // H
    G = math.gcd(H, n)
    R = n // G
    heads = H // G
    C = heads * dh
    Dn = D // n
    enc_local = enc.shape[0]
    f = lax.axis_index("fsdp")
    g, r = f // R, lax.rem(f, R)

    def fold(w, gain):
        return w * gain[:, None]

    def by_group(w):
        return w.reshape(Dn, G, C)

    wq, wk, wv = (fold(w, self_gain) for w in (self_query, self_key, self_value))
    w_send = jnp.transpose(
        jnp.concatenate([by_group(wq), by_group(wk), by_group(wv)], axis=2), (1, 0, 2)
    )
    dist = jnp.concatenate(
        [jnp.arange(T, 2 * T), jnp.full((T,), -1), jnp.arange(T)]
    )
    row_bucket = jnp.concatenate(
        [bucket_table[T : 2 * T], jnp.zeros((T,), jnp.int32), bucket_table[:T]]
    )
    onehot = (row_bucket[:, None] == jnp.arange(buckets, dtype=jnp.int32)[None, :]).astype(F32)
    vec = jnp.dot(
        onehot, position_bias - position_bias[buckets - 1 :], precision=lax.Precision.HIGHEST
    )
    vec = jnp.where(dist[:, None] < 0, masked_score, vec)
    vec = lax.dynamic_slice_in_dim(vec.T, g * heads, heads, 0)
    vec = jnp.pad(vec, ((0, 8 - heads), (0, 0)))
    ids = jnp.broadcast_to(
        jnp.where(dist < 0, -1, row_bucket).astype(F32)[None, :], (8, 3 * T)
    )

    x_all, w_cols = gather(G, R, [x], [w_send], 1)
    x_all = x_all.reshape(n * T, D)
    w_cols = w_cols.reshape(D, 3 * C)

    wide = jnp.concatenate([self_output, fold(cross_query, cross_gain), cross_output], axis=1)
    wide_all = lax.all_gather(wide, "fsdp", axis=0, tiled=True)
    cot_all = lax.all_gather(cot, "fsdp", axis=0, tiled=True)
    so_full, cq_full, co_full = wide_all[:, :D], wide_all[:, D : 2 * D], wide_all[:, 2 * D :]
    small = jnp.concatenate([enc.reshape(enc_local, n, Dn), jnp.broadcast_to(ffn_gain, (1, n, Dn))], axis=0)
    small = lax.all_to_all(small, "fsdp", 1, 0, tiled=False)
    enc_cols = small[:, :enc_local, :].reshape(n * enc_local, Dn)
    gain_three = small[:, enc_local, :].reshape(D)
    ckv_w = jnp.concatenate([cross_key, cross_value], axis=1)
    ckv = lax.psum(mm(enc_cols, ckv_w), "fsdp")

    att, q, k, v, lse = attention_forward(G, R, heads, dh, x_all, w_cols, vec)
    att_rows = lane_exchange(G, R, att, 2)
    attended = jnp.transpose(att_rows, (1, 0, 2)).reshape(T, D)

    after = x + mm(attended, so_full)
    unit_two, scale_two = unit_of(after)
    cq = to_heads(mm(unit_two, cq_full), H)
    ck, cv = to_heads(ckv[:, :D], H), to_heads(ckv[:, D:], H)
    cscores = bmm("hqd,hkd->hqk", cq, ck)
    cweights = jnp.exp(cscores - jnp.max(cscores, axis=2, keepdims=True))
    cprobs = cweights / jnp.sum(cweights, axis=2, keepdims=True)
    cout = bmm("hqk,hkd->hqd", cprobs, cv)
    cflat = from_heads(cout)
    middle = after + mm(cflat, co_full)
    unit_three, scale_three = unit_of(middle)
    normed_three = unit_three * gain_three

    (n3_all,) = gather(G, R, [normed_three], [], 3)
    n3_all = n3_all.reshape(n * T, D)
    gate_up = jnp.concatenate([ffn_gate, ffn_up], axis=1)
    F = ffn_gate.shape[1]
    pre = mm(n3_all, gate_up)
    gate_pre, up_pre = pre[:, :F], pre[:, F:]
    gelu_out, gelu_slope = gelu_parts(gate_pre)
    inner = gelu_out * up_pre
    grad_inner = mm_nt(cot_all, ffn_down)
    grad_pre = jnp.concatenate([grad_inner * up_pre * gelu_slope, grad_inner * gelu_out], axis=1)
    dn3_part = mm_nt(grad_pre, gate_up)
    dn3 = scatter(G, R, dn3_part.reshape(G, R, T, D), True, True, 4)
    out_part = mm(inner, ffn_down)
    out_rows = middle + scatter(G, R, out_part.reshape(G, R, T, D), True, True, 5)
    d_gate_up = mm_tn(n3_all, grad_pre)
    d_down = mm_tn(inner, cot_all)
    d_gate, d_up, d_down = lax.psum((d_gate_up[:, :F], d_gate_up[:, F:], d_down), "rep")

    d_gain_three = jnp.sum(dn3 * unit_three, axis=0)
    d_middle = cot + unit_backward(dn3 * gain_three, unit_three, scale_three)
    d_co = mm_tn(cflat, d_middle)
    d_cout = to_heads(mm_nt(d_middle, co_full), H)
    cdelta = jnp.sum(d_cout * cout, axis=2)
    d_cprobs = bmm("hqd,hkd->hqk", d_cout, cv)
    d_cscores = cprobs * (d_cprobs - cdelta[:, :, None])
    d_cq = from_heads(bmm("hqk,hkd->hqd", d_cscores, ck))
    d_ck = from_heads(bmm("hqk,hqd->hkd", d_cscores, cq))
    d_cv = from_heads(bmm("hqk,hqd->hkd", cprobs, d_cout))
    d_after = d_middle + unit_backward(mm_nt(d_cq, cq_full), unit_two, scale_two)
    d_cq_w = mm_tn(unit_two, d_cq)
    d_ckv = lax.psum(jnp.concatenate([d_ck, d_cv], axis=1), "fsdp")
    d_ckv_w = mm_tn(enc_cols, d_ckv)
    d_enc_cols = mm_nt(d_ckv, ckv_w)
    d_enc = lax.all_to_all(d_enc_cols.reshape(n, enc_local, Dn), "fsdp", 0, 1, tiled=False)
    d_enc = d_enc.reshape(enc_local, D)

    d_att = jnp.transpose(mm_nt(d_after, so_full).reshape(T, G, C), (1, 0, 2))
    d_att = lane_exchange(G, R, d_att, 6)
    d_so = mm_tn(attended, d_after)
    d_wide = lax.psum_scatter(
        jnp.concatenate([d_so, d_cq_w, d_co], axis=1), "fsdp", scatter_dimension=0, tiled=True
    )
    dq, dkv, gbias = attention_backward(
        G, R, heads, dh, buckets, q, k, v, lse, att, d_att, vec, ids
    )
    dkv = group_sum(G, R, dkv.reshape(G, R, T, 2 * C), 7)
    dqkv = jnp.concatenate([dq, dkv], axis=2)
    own_x = lax.dynamic_index_in_dim(x_all.reshape(G, R, T, D), r, 1, keepdims=False)
    unit_own, _ = unit_of(own_x)
    d_w = mm_tn(unit_own.reshape(G * T, D), dqkv.reshape(G * T, 3 * C))
    du_part = mm_nt(dqkv.reshape(G * T, 3 * C), w_cols).reshape(G, T, D)
    du = scatter(G, R, du_part, False, True, 8)
    unit_one, scale_one = unit_of(x)
    d_x = d_after + unit_backward(du, unit_one, scale_one)
    d_w = scatter(G, R, d_w.reshape(G, R, Dn, 3 * C), True, False, 9)
    d_w = jnp.transpose(d_w, (1, 0, 2))
    d_qkv = [d_w[:, :, a * C : (a + 1) * C].reshape(Dn, D) for a in range(3)]

    grad_bias = jnp.sum(gbias, axis=2).T
    grad_bias = lax.dynamic_update_slice(jnp.zeros((buckets, H), F32), grad_bias, (0, g * heads))
    tiny = jnp.concatenate([d_gain_three.reshape(n, Dn), grad_bias.reshape(n, -1)], axis=1)
    tiny = lax.psum(tiny, ("rep", "fsdp"))
    tiny = lax.dynamic_index_in_dim(tiny, f, 0, keepdims=False)
    d_qkv_o, d_wide, d_ckv_w = lax.psum((jnp.concatenate(d_qkv, axis=1), d_wide, d_ckv_w), "rep")

    dwq, dwk, dwv = (d_qkv_o[:, a * D : (a + 1) * D] for a in range(3))
    dso, dcq, dco = (d_wide[:, a * D : (a + 1) * D] for a in range(3))
    g_self = jnp.sum(dwq * self_query + dwk * self_key + dwv * self_value, axis=1)
    g_cross = jnp.sum(dcq * cross_query, axis=1)
    return (
        out_rows[None],
        d_x[None],
        d_enc[None],
        g_self,
        g_cross,
        tiny[:Dn],
        fold(dwq, self_gain),
        fold(dwk, self_gain),
        fold(dwv, self_gain),
        dso,
        tiny[Dn:].reshape(buckets // n, H),
        fold(dcq, cross_gain),
        d_ckv_w[:, :D],
        d_ckv_w[:, D:],
        dco,
        d_gate,
        d_up,
        d_down,
    )


def solution(mesh):
    rows = P("rep", "fsdp", None)
    gain = P("fsdp")
    weight = P("fsdp", None)
    columns = P(None, "fsdp")
    args = (rows, rows, gain, gain, gain) + (weight,) * 4 + (P(), P()) + (weight,) * 4
    args += (columns, columns, weight, rows)
    outs = (rows, rows, rows, gain, gain, gain) + (weight,) * 9 + (columns, columns, weight)
    return jax.shard_map(
        functools.partial(shards, mesh.shape["fsdp"]),
        mesh=mesh,
        in_specs=args,
        out_specs=outs,
        check_vma=False,
    )
```

```python
import functools
import math

import jax
import jax.numpy as jnp
from jax import lax
from jax.experimental import pallas as pl
from jax.experimental.pallas import tpu as pltpu
from jax.sharding import PartitionSpec as P

HIGH = lax.Precision.HIGH
MESH = pl.DeviceIdType.MESH
F32 = jnp.float32
eps_norm = 1e-06
gelu_coef = math.sqrt(2.0 / math.pi)
masked_score = -1e30
vmem_bytes = 60 << 20
pieces = 2


def mm(a, b):
    return jnp.dot(a, b, precision=HIGH, preferred_element_type=F32)


def mm_tn(a, b):
    return lax.dot_general(
        a, b, (((0,), (0,)), ((), ())), precision=HIGH, preferred_element_type=F32
    )


def mm_nt(a, b):
    return lax.dot_general(
        a, b, (((1,), (1,)), ((), ())), precision=HIGH, preferred_element_type=F32
    )


BF16 = jnp.bfloat16


def halves(a):
    high = a.astype(BF16)
    return high, (a - high.astype(F32)).astype(BF16)


def dot3(a, b, dims=(((1,), (0,)), ((), ()))):
    def dot(x, y):
        return lax.dot_general(x, y, dims, preferred_element_type=F32)

    return dot(a[0], b[0]) + (dot(a[0], b[1]) + dot(a[1], b[0]))


def unit_of(rows):
    scale = lax.rsqrt(jnp.mean(rows * rows, axis=-1, keepdims=True) + eps_norm)
    return rows * scale, scale


def unit_backward(grad_unit, unit, scale):
    return scale * (grad_unit - unit * jnp.mean(grad_unit * unit, axis=-1, keepdims=True))


def gelu_parts(gate_pre):
    squared = gate_pre * gate_pre
    tangent = jnp.tanh(gelu_coef * (gate_pre + 0.044715 * squared * gate_pre))
    gelu_out = 0.5 * gate_pre * (1.0 + tangent)
    gelu_slope = 0.5 * (1.0 + tangent) + 0.5 * gate_pre * (1.0 - tangent * tangent) * gelu_coef * (
        1.0 + 3.0 * 0.044715 * squared
    )
    return (gelu_out, gelu_slope)


def my_place(R):
    rep = lax.axis_index("rep")
    f = lax.axis_index("fsdp")
    return rep, f, f // R, lax.rem(f, R)


def greet(peers):
    barrier = pltpu.get_barrier_semaphore()
    for peer in peers:
        pl.semaphore_signal(barrier, inc=1, device_id=peer, device_id_type=MESH)
    pl.semaphore_wait(barrier, len(peers))


def remote(src, dst, send_sem, recv_sem, peer):
    return pltpu.make_async_remote_copy(
        src_ref=src,
        dst_ref=dst,
        send_sem=send_sem,
        recv_sem=recv_sem,
        device_id=peer,
        device_id_type=MESH,
    )


def lane_peers(rep, g, r, G, R):
    return [(rep, lax.rem(g + k, G) * R + r) for k in range(1, G)]


def group_peers(rep, g, r, G, R):
    return [(rep, g * R + lax.rem(r + j, R)) for j in range(1, R)]


def comm_call(kernel, outs, ins, scratch, collective_id, vmem_ins=False, vmem_outs=False):
    def space(vmem):
        return pl.BlockSpec(memory_space=pltpu.VMEM if vmem else pl.ANY)

    return pl.pallas_call(
        kernel,
        out_shape=outs,
        in_specs=[space(vmem_ins)] * len(ins),
        out_specs=[space(vmem_outs)] * len(outs),
        scratch_shapes=scratch,
        compiler_params=pltpu.CompilerParams(
            collective_id=collective_id, has_side_effects=True, vmem_limit_bytes=vmem_bytes
        ),
    )(*ins)


def gather_kernel(G, R, own, spread, *refs):
    count = own + spread
    ins, outs = refs[:count], refs[count : 2 * count]
    local_sem, lane_send, lane_recv, group_send, group_recv = refs[2 * count :]
    rep, f, g, r = my_place(R)
    lanes = lane_peers(rep, g, r, G, R)
    groups = group_peers(rep, g, r, G, R)
    greet(lanes + groups)

    def source(a, k):
        return ins[a] if a < own else ins[a].at[lax.rem(g + k, G)]

    lane_copies, group_copies, locals_ = [], [], []
    for a in range(count):
        for k in range(G - 1, 0, -1):
            copy = remote(
                source(a, k), outs[a].at[f], lane_send.at[a, k - 1], lane_recv.at[a, k - 1], lanes[k - 1]
            )
            copy.start()
            lane_copies.append((a, k, copy))
    for a in range(count):
        copy = pltpu.make_async_copy(source(a, 0), outs[a].at[f], local_sem.at[a])
        copy.start()
        locals_.append(copy)
        for j in range(1, R):
            copy = remote(
                source(a, 0),
                outs[a].at[f],
                group_send.at[a, j - 1, 0],
                group_recv.at[a, j - 1, 0],
                groups[j - 1],
            )
            copy.start()
            group_copies.append(copy)
    for a, k, copy in sorted(lane_copies, key=lambda t: (t[0], t[1])):
        copy.wait_recv()
        came = lax.rem(g + G - k, G) * R + r
        for j in range(1, R):
            onward = remote(
                outs[a].at[came],
                outs[a].at[came],
                group_send.at[a, j - 1, k],
                group_recv.at[a, j - 1, k],
                groups[j - 1],
            )
            onward.start()
            group_copies.append(onward)
    for copy in group_copies:
        copy.wait()
    for _, _, copy in lane_copies:
        copy.wait_send()
    for copy in locals_:
        copy.wait()


def gather(G, R, own, spread, collective_id):
    n = G * R
    outs = [jax.ShapeDtypeStruct((n,) + x.shape, x.dtype) for x in own]
    outs += [jax.ShapeDtypeStruct((n,) + x.shape[1:], x.dtype) for x in spread]
    count = len(outs)
    sem = pltpu.SemaphoreType.DMA
    return comm_call(
        functools.partial(gather_kernel, G, R, len(own), len(spread)),
        outs,
        list(own) + list(spread),
        [
            sem((count,)),
            sem((count, G - 1)),
            sem((count, G - 1)),
            sem((count, R - 1, G)),
            sem((count, R - 1, G)),
        ],
        collective_id,
    )


def lane_kernel(G, R, x_ref, o_ref, local_sem, lane_send, lane_recv):
    rep, f, g, r = my_place(R)
    lanes = lane_peers(rep, g, r, G, R)
    greet(lanes)
    copies = []
    for k in range(G - 1, 0, -1):
        copy = remote(
            x_ref.at[lax.rem(g + k, G)], o_ref.at[g], lane_send.at[k - 1], lane_recv.at[k - 1], lanes[k - 1]
        )
        copy.start()
        copies.append(copy)
    own = pltpu.make_async_copy(x_ref.at[g], o_ref.at[g], local_sem)
    own.start()
    own.wait()
    for copy in copies:
        copy.wait()


def lane_exchange(G, R, x, collective_id):
    sem = pltpu.SemaphoreType.DMA
    return comm_call(
        functools.partial(lane_kernel, G, R),
        [jax.ShapeDtypeStruct(x.shape, x.dtype)],
        [x],
        [sem, sem((G - 1,)), sem((G - 1,))],
        collective_id,
    )[0]


def scatter_kernel(G, R, pooled, summed, x_ref, o_ref, *scratch):
    rep, f, g, r = my_place(R)
    lanes = lane_peers(rep, g, r, G, R)
    groups = group_peers(rep, g, r, G, R) if pooled else []
    if pooled:
        group_buf, group_send, group_recv = scratch[:3]
        scratch = scratch[3:]
    lane_out, lane_in, lane_send, lane_recv = scratch
    greet(lanes + groups)
    order = list(range(G - 1, -1, -1))
    group_copies = []
    if pooled:
        for k in order:
            for j in range(1, R):
                copy = remote(
                    x_ref.at[lax.rem(g + k, G), lax.rem(r + j, R)],
                    group_buf.at[j - 1, k],
                    group_send.at[j - 1, k],
                    group_recv.at[j - 1, k],
                    groups[j - 1],
                )
                copy.start()
                group_copies.append((j, k, copy))
    lane_copies = []
    for k in order:
        to = lax.rem(g + k, G)
        if pooled:
            for j, kk, copy in group_copies:
                if kk == k:
                    copy.wait_recv()
            total = x_ref[to, r]
            for j in range(1, R):
                total = total + group_buf[j - 1, k]
        else:
            total = x_ref[to]
        if k > 0:
            lane_out[k - 1] = total
            copy = remote(
                lane_out.at[k - 1], lane_in.at[k - 1], lane_send.at[k - 1], lane_recv.at[k - 1], lanes[k - 1]
            )
            copy.start()
            lane_copies.append((k, copy))
        elif summed:
            o_ref[...] = total
        else:
            o_ref[g] = total
    for k, copy in lane_copies:
        copy.wait_recv()
        if summed:
            o_ref[...] += lane_in[k - 1]
        else:
            o_ref[lax.rem(g + G - k, G)] = lane_in[k - 1]
    for _, copy in lane_copies:
        copy.wait_send()
    for _, _, copy in group_copies:
        copy.wait_send()


def scatter(G, R, x, pooled, summed, collective_id):
    block = x.shape[2:] if pooled else x.shape[1:]
    sem = pltpu.SemaphoreType.DMA
    scratch = []
    if pooled:
        scratch = [
            pltpu.VMEM((max(R - 1, 1), G) + block, F32),
            sem((max(R - 1, 1), G)),
            sem((max(R - 1, 1), G)),
        ]
    scratch += [
        pltpu.VMEM((G - 1,) + block, F32),
        pltpu.VMEM((G - 1,) + block, F32),
        sem((G - 1,)),
        sem((G - 1,)),
    ]
    out = jax.ShapeDtypeStruct(block if summed else (G,) + block, F32)
    return comm_call(
        functools.partial(scatter_kernel, G, R, pooled, summed),
        [out],
        [x],
        scratch,
        collective_id,
        vmem_ins=True,
        vmem_outs=True,
    )[0]


def group_kernel(G, R, x_ref, o_ref, group_buf, group_send, group_recv):
    rep, f, g, r = my_place(R)
    groups = group_peers(rep, g, r, G, R)
    greet(groups)
    copies = []
    for j in range(1, R):
        copy = remote(
            x_ref.at[:, lax.rem(r + j, R)],
            group_buf.at[j - 1],
            group_send.at[j - 1],
            group_recv.at[j - 1],
            groups[j - 1],
        )
        copy.start()
        copies.append(copy)
    for copy in copies:
        copy.wait()
    total = x_ref[:, r]
    for j in range(1, R):
        total = total + group_buf[j - 1]
    o_ref[...] = total


def group_sum(G, R, x, collective_id):
    shape = (x.shape[0],) + x.shape[2:]
    sem = pltpu.SemaphoreType.DMA
    return comm_call(
        functools.partial(group_kernel, G, R),
        [jax.ShapeDtypeStruct(shape, F32)],
        [x],
        [pltpu.VMEM((R - 1,) + shape, F32), sem((R - 1,)), sem((R - 1,))],
        collective_id,
        vmem_ins=True,
        vmem_outs=True,
    )[0]


def first_kernel(
    G,
    R,
    Q,
    heads,
    dh,
    x_ref,
    w_ref,
    wide_ref,
    small_ref,
    ckv_w_ref,
    vec_ref,
    att_ref,
    rows_ref,
    q_ref,
    kv_ref,
    lse_ref,
    wcols_ref,
    own_ref,
    small_all_ref,
    ckv_ref,
    wide_all_ref,
    x_buf,
    unit_ref,
    strip_ref,
    x_sems,
    w_sems,
    wide_sems,
    att_sems,
    small_sems,
    ckv_parts,
    ckv_pool,
    ckv_inbox,
    ckv_sems,
    ckv_chain_sems,
):
    rep, f, g, r = my_place(R)
    n = G * R
    T, D = x_ref.shape
    C = heads * dh
    greet(everyone(rep, f, n, Q))

    small = Deal(n, small_ref, small_all_ref, small_sems)
    weights = Spread(G, R, Q, lambda k: w_ref.at[lax.rem(g + k, G)], wcols_ref, w_sems)
    wide = Spread(G, R, Q, lambda k: wide_ref, wide_all_ref, wide_sems)
    chain = Chain(G, R, x_buf, x_sems)
    ckv_sum = Reduce(G, R, ckv_parts, ckv_pool, ckv_inbox, ckv_sems)
    ckv_chain = Chain(G, R, ckv_ref, ckv_chain_sems)
    small.start()
    weights.start()
    wide.start()
    x_buf[f] = x_ref[...].reshape(pieces, T // pieces, D)
    chain.start()
    make_strips(R, heads, T, vec_ref, strip_ref)
    weights.across()
    small.arrive()
    enc_rows = ckv_parts.shape[3]
    enc_cols = small_all_ref[:, :enc_rows, :].reshape(n * enc_rows, small_ref.shape[2])
    ckv_parts[...] = mm(enc_cols, ckv_w_ref[...]).reshape(ckv_parts.shape)
    for o in range(G):
        ckv_sum.offer(o)
    wide.across()
    weights.share()
    for o in range(G):
        ckv_sum.pooled(o)
    weights.arrive()
    w = wcols_ref[...].reshape(D, 3 * C)
    for t in range(G):
        src = chain.arrive(t)
        if t > 0:
            ckv_sum.hand_on(t - 1)
        unit, _ = unit_of(x_buf[pl.ds(src * R, R)].reshape(R * T, D))
        rows = pl.ds(pl.multiple_of(src * (R * T), R * T), R * T)
        unit_ref[...] = unit
        mine = unit_ref[pl.ds(pl.multiple_of(r * T, T), T), :]
        mine_rows = pl.ds(pl.multiple_of(src * T, T), T)
        own_ref[mine_rows, :] = mine
        kv = mm(unit, w[:, : 2 * C])
        q = mm(mine, w[:, 2 * C :])
        for h in range(heads):
            kv_ref[h, rows, :] = kv[:, 2 * h * dh : 2 * (h + 1) * dh]
            q_h = q[:, h * dh : (h + 1) * dh]
            q_ref[h, mine_rows, :] = jnp.concatenate([q_h, jnp.zeros_like(q_h)], axis=1)
    ckv_sum.collect(ckv_ref.at[f])
    ckv_chain.start()
    for i in range(G):
        L = R * (i + 1) * T
        outs = []
        for h in range(heads):
            scores = strip_scores(R, T, i, r, h, L, kv_ref, q_ref, strip_ref)
            top = jnp.max(scores, axis=0, keepdims=True)
            probs = jnp.exp(scores - top)
            total = jnp.sum(probs, axis=0, keepdims=True)
            out_t = mm_tn(kv_ref[h, :L, :], probs)[dh:, :] / total
            outs.append(out_t.T)
            lse_ref[i, h : h + 1, :] = top + jnp.log(total)
        att_ref[i] = jnp.concatenate(outs, axis=1)
        lane_send(G, R, i, att_ref, rows_ref, att_sems)
        ckv_chain.arrive(i)
    wide.share()
    lane_wait(G, R, att_ref, rows_ref, att_sems)
    wide.arrive()
    small.finish()
    weights.finish()
    chain.finish()
    ckv_sum.finish()
    ckv_chain.finish()
    wide.finish()


def lane_send(G, R, i, src_ref, dst_ref, sems):
    rep, f, g, r = my_place(R)

    @pl.when(g == i)
    def _():
        pltpu.make_async_copy(src_ref.at[i], dst_ref.at[i], sems[2]).start()

    @pl.when(g != i)
    def _():
        remote(src_ref.at[i], dst_ref.at[g], sems[0].at[i], sems[1].at[g], (rep, i * R + r)).start()


def lane_wait(G, R, src_ref, dst_ref, sems):
    rep, f, g, r = my_place(R)
    pltpu.make_async_copy(src_ref.at[g], dst_ref.at[g], sems[2]).wait()
    for i in range(G):

        @pl.when(g != i)
        def _():
            copy = remote(src_ref.at[i], dst_ref.at[i], sems[0].at[i], sems[1].at[i], (rep, i * R + r))
            copy.wait_send()
            copy.wait_recv()


def lane_sems(G):
    sem = pltpu.SemaphoreType.DMA
    return (sem((G,)), sem((G,)), sem)


class Spread:
    def __init__(self, G, R, Q, source, out, sems):
        self.sizes = (G, R, Q)
        self.source, self.out, self.sems = source, out, sems
        rep, f, g, r = my_place(R)
        self.place = (rep, f, g, r)
        self.lanes = lane_peers(rep, g, r, G, R)
        self.groups = group_peers(rep, g, r, G, R)
        self.reps = [(lax.rem(rep + j, Q), f) for j in range(1, Q)]

    def slot(self, k):
        G, R, Q = self.sizes
        _, _, g, r = self.place
        return lax.rem(g + G - k, G) * R + r

    def lane_copy(self, k):
        rep, f = self.place[:2]
        return remote(
            self.source(k), self.out.at[f, rep], self.sems[0].at[k - 1], self.sems[1].at[k - 1], self.lanes[k - 1]
        )

    def own_copy(self):
        rep, f = self.place[:2]
        return pltpu.make_async_copy(self.source(0), self.out.at[f, rep], self.sems[6])

    def rep_copy(self, k, j):
        part = self.out.at[self.slot(k), self.place[0]]
        return remote(part, part, self.sems[2].at[k, j - 1], self.sems[3].at[k, j - 1], self.reps[j - 1])

    def group_copy(self, k, j):
        part = self.out.at[self.slot(k)]
        return remote(part, part, self.sems[4].at[k, j - 1], self.sems[5].at[k, j - 1], self.groups[j - 1])

    def start(self):
        G = self.sizes[0]
        for k in range(G - 1, 0, -1):
            self.lane_copy(k).start()
        self.own_copy().start()

    def across(self):
        G, R, Q = self.sizes
        for k in range(G):
            if k == 0:
                self.own_copy().wait()
            else:
                self.lane_copy(k).wait_recv()
            for j in range(1, Q):
                self.rep_copy(k, j).start()

    def share(self):
        G, R, Q = self.sizes
        for k in range(G):
            for j in range(1, Q):
                self.rep_copy(k, j).wait_recv()
            for j in range(1, R):
                self.group_copy(k, j).start()

    def arrive(self):
        G, R, Q = self.sizes
        for k in range(G):
            for j in range(1, R):
                self.group_copy(k, j).wait_recv()

    def finish(self):
        G, R, Q = self.sizes
        for k in range(G):
            if k > 0:
                self.lane_copy(k).wait_send()
            for j in range(1, Q):
                self.rep_copy(k, j).wait_send()
            for j in range(1, R):
                self.group_copy(k, j).wait_send()


class Deal:
    def __init__(self, n, parts, out, sems):
        self.n, self.parts, self.out, self.sems = n, parts, out, sems
        self.rep, self.f = lax.axis_index("rep"), lax.axis_index("fsdp")

    def copy(self, k):
        to = lax.rem(self.f + k, self.n)
        return remote(
            self.parts.at[to],
            self.out.at[self.f],
            self.sems[0].at[k - 1],
            self.sems[1].at[k - 1],
            (self.rep, to),
        )

    def start(self):
        for k in range(1, self.n):
            self.copy(k).start()
        self.out[self.f] = self.parts[self.f]

    def arrive(self):
        for k in range(1, self.n):
            self.copy(k).wait_recv()

    def finish(self):
        for k in range(1, self.n):
            self.copy(k).wait_send()


def deal_sems(n):
    sem = pltpu.SemaphoreType.DMA
    return (sem((n - 1,)), sem((n - 1,)))


def everyone(rep, f, n, Q):
    return [(rep, lax.rem(f + k, n)) for k in range(1, n)] + [
        (lax.rem(rep + j, Q), f) for j in range(1, Q)
    ]


def spread_sems(G, R, Q):
    sem = pltpu.SemaphoreType.DMA
    return (
        sem((G - 1,)),
        sem((G - 1,)),
        sem((G, Q - 1)),
        sem((G, Q - 1)),
        sem((G, R - 1)),
        sem((G, R - 1)),
        sem,
    )


def lookup(table, i, t):
    rows, columns = len(table), len(table[0])
    flat = i * columns + t
    value = table[0][0] + 0 * flat
    for a in range(rows):
        for b in range(columns):
            if table[a][b] != table[0][0]:
                value = jnp.where(flat == a * columns + b, table[a][b], value)
    return value


class Chain:
    def __init__(self, G, R, buf, sems):
        self.G, self.R, self.buf, self.sems = G, R, buf, sems
        self.pieces = buf.shape[1]
        self.rep, self.f, self.g, self.r = my_place(R)
        self.groups = group_peers(self.rep, self.g, self.r, G, R)
        self.order, self.first, self.second = [], [], []
        for i in range(G):
            order = sorted(range(G), key=lambda s: (abs(s - i), s))
            self.order.append(order)
            far = [abs(s - i) for s in order]
            fresh = [t > 0 and far[t] != far[t - 1] for t in range(G)]
            paired = [fresh[t] and t + 1 < G and far[t + 1] == far[t] for t in range(G)]
            self.first.append([order[t] if fresh[t] else -1 for t in range(G)])
            self.second.append([order[t + 1] if paired[t] else -1 for t in range(G)])

    def part(self, src, p):
        return self.buf.at[src * self.R + self.r, p]

    def step(self, src, side, p):
        part = self.part(src, p)
        to = (self.rep, (self.g + side) * self.R + self.r)
        way = 0 if side > 0 else 1
        return remote(part, part, self.sems[0].at[way, src, p], self.sems[1].at[src, p], to)

    def group_copy(self, src, j, p):
        part = self.part(src, p)
        return remote(
            part, part, self.sems[2].at[j - 1, src, p], self.sems[3].at[j - 1, src, p], self.groups[j - 1]
        )

    def sends(self, src):
        right = jnp.logical_and(src <= self.g, self.g < self.G - 1)
        left = jnp.logical_and(src >= self.g, self.g > 0)
        return ((1, right), (-1, left))

    def onward(self, src, p):
        for side, cond in self.sends(src):

            @pl.when(cond)
            def _():
                self.step(src, side, p).start()

        for j in range(1, self.R):
            self.group_copy(src, j, p).start()

    def start(self):
        for p in range(self.pieces):
            self.onward(self.g, p)

    def arrive(self, t):
        for table in (self.first, self.second):
            came = lookup(table, self.g, t)

            @pl.when(came >= 0)
            def _():
                for p in range(self.pieces):
                    self.step(came, 1, p).wait_recv()
                    self.onward(came, p)

        src = lookup(self.order, self.g, t)
        for j in range(1, self.R):
            for p in range(self.pieces):
                self.group_copy(src, j, p).wait_recv()
        return src

    def finish(self):
        for src in range(self.G):
            for p in range(self.pieces):
                for side, cond in self.sends(src):

                    @pl.when(cond)
                    def _():
                        self.step(src, side, p).wait_send()

                for j in range(1, self.R):
                    self.group_copy(src, j, p).wait_send()


def chain_sems(G, R, pieces):
    sem = pltpu.SemaphoreType.DMA
    return (sem((2, G, pieces)), sem((G, pieces)), sem((R - 1, G, pieces)), sem((R - 1, G, pieces)))


def make_strips(R, heads, T, vec_ref, strip_ref):
    for h in range(heads):
        vec = jnp.broadcast_to(vec_ref[h : h + 1, :], (2 * T, 3 * T))
        pair = pltpu.roll(vec, 0, 1, stride=1, stride_axis=0)[:, :T]
        if R > 1:
            strip_ref[h, : (R - 1) * T, :] = jnp.zeros(((R - 1) * T, T), F32)
            strip_ref[h, (R + 1) * T :, :] = jnp.full(((R - 1) * T, T), masked_score, F32)
        strip_ref[h, (R - 1) * T : (R + 1) * T, :] = pair


def strip_scores(R, T, i, r, h, L, kv_ref, q_ref, strip_ref):
    scores = mm_nt(kv_ref[h, :L, :], q_ref[h, i * T : (i + 1) * T, :])
    skip = 1 if i == 0 else 0
    width = (R + 1 - skip) * T
    start = pl.multiple_of((R - 1 - r + skip) * T, T)
    near = scores[L - width :, :] + strip_ref[h, pl.ds(start, width), :]
    if width == L:
        return near
    return jnp.concatenate([scores[: L - width, :], near], axis=0)


def first_stage(G, R, Q, heads, dh, x, w_mine, wide_mine, small, ckv_w, vec, collective_id):
    T, D = x.shape
    n = G * R
    S = n * T
    C = heads * dh
    enc_rows = small.shape[1] - 8
    vm = pl.BlockSpec(memory_space=pltpu.VMEM)
    hbm = pl.BlockSpec(memory_space=pl.ANY)
    shape = lambda *dims: jax.ShapeDtypeStruct(dims, F32)
    return pl.pallas_call(
        functools.partial(first_kernel, G, R, Q, heads, dh),
        out_shape=[
            shape(G, T, C),
            shape(G, T, C),
            shape(heads, G * T, 2 * dh),
            shape(heads, S, 2 * dh),
            shape(G, 8, T),
            shape(n, Q, *w_mine.shape[1:]),
            shape(G * T, D),
            shape(*small.shape),
            shape(n, 1, enc_rows, 2 * D),
            shape(n, Q, *wide_mine.shape),
        ],
        in_specs=[vm, vm, hbm, vm, vm, vm],
        out_specs=[vm] * 9 + [hbm],
        scratch_shapes=[
            pltpu.VMEM((n, pieces, T // pieces, D), F32),
            pltpu.VMEM((R * T, D), F32),
            pltpu.VMEM((heads, 2 * R * T, T), F32),
            chain_sems(G, R, pieces),
            spread_sems(G, R, Q),
            spread_sems(G, R, Q),
            lane_sems(G),
            deal_sems(n),
        ]
        + reduce_scratch(G, R, 1, (enc_rows, 2 * D))
        + [chain_sems(G, R, 1)],
        compiler_params=pltpu.CompilerParams(
            collective_id=collective_id, has_side_effects=True, vmem_limit_bytes=vmem_bytes
        ),
    )(x, w_mine, wide_mine, small, ckv_w, vec)


class Reduce:
    def __init__(self, G, R, parts, pool, inbox, sems):
        self.G, self.parts, self.pool, self.inbox, self.sems = G, parts, pool, inbox, sems
        self.pieces = parts.shape[2]
        self.rep, self.f, self.g, self.r = my_place(R)
        self.stride = R
        self.R = R if pool is not None else 1
        self.mine = self.r if pool is not None else 0
        self.groups = group_peers(self.rep, self.g, self.r, G, R)
        orders = []
        for g in range(G):
            due = {o: o + g if o > g else (G - 1 - o) + (G - 1 - g) for o in range(G) if o != g}
            held = [o for o in due if (g > 0 if o > g else g < G - 1)]
            orders.append((sorted(held, key=lambda o: due[o]) + [-1] * G)[: G - 1])
        self.orders = orders

    def group_copy(self, o, j, p):
        other = lax.rem(self.r + j, self.R)
        return remote(
            self.parts.at[o, other, p],
            self.pool.at[j - 1, o, p],
            self.sems[0].at[j - 1, o, p],
            self.sems[1].at[j - 1, o, p],
            self.groups[j - 1],
        )

    def lane_copy(self, o, p):
        right = o > self.g
        to = jnp.where(right, self.g + 1, self.g - 1)
        last_left = jnp.logical_and(jnp.logical_not(right), to == o)
        slot = jnp.where(last_left, self.G, o)
        part = self.parts.at[o, self.mine, p]
        peer = (self.rep, to * self.stride + self.r)
        return remote(part, self.inbox.at[slot, p], self.sems[2].at[o, p], self.sems[3].at[slot, p], peer)

    def inbox_wait(self, slot, p):
        remote(
            self.parts.at[0, self.mine, p],
            self.inbox.at[slot, p],
            self.sems[2].at[0, p],
            self.sems[3].at[slot, p],
            (self.rep, self.f),
        ).wait_recv()

    def offer(self, o):
        for p in range(self.pieces):
            for j in range(1, self.R):
                self.group_copy(o, j, p).start()

    def pooled(self, o):
        first = jnp.logical_or(
            jnp.logical_and(o > self.g, self.g == 0),
            jnp.logical_and(o < self.g, self.g == self.G - 1),
        )
        for p in range(self.pieces):
            for j in range(1, self.R):
                self.group_copy(o, j, p).wait_recv()
            if self.R > 1:
                total = self.parts[o, self.mine, p]
                for j in range(1, self.R):
                    total = total + self.pool[j - 1, o, p]
                self.parts[o, self.mine, p] = total

            @pl.when(first)
            def _():
                self.lane_copy(o, p).start()

    def hand_on(self, index):
        o = lookup(self.orders, self.g, index)

        @pl.when(o >= 0)
        def _():
            for p in range(self.pieces):
                self.inbox_wait(o, p)
                self.parts[o, self.mine, p] += self.inbox[o, p]
                self.lane_copy(o, p).start()

    def collect(self, out):
        for p in range(self.pieces):
            out[p] = self.parts[self.g, self.mine, p]

        for cond, slot in ((self.g > 0, self.g), (self.g < self.G - 1, self.G)):

            @pl.when(cond)
            def _():
                for p in range(self.pieces):
                    self.inbox_wait(slot, p)
                    out[p] += self.inbox[slot, p]

    def finish(self):
        for o in range(self.G):
            for p in range(self.pieces):
                for j in range(1, self.R):
                    self.group_copy(o, j, p).wait_send()

            @pl.when(self.g != o)
            def _():
                for p in range(self.pieces):
                    self.lane_copy(o, p).wait_send()


def reduce_scratch(G, R, pieces, block):
    sem = pltpu.SemaphoreType.DMA
    block = (pieces, block[0] // pieces) + block[1:]
    return [
        pltpu.VMEM((G, R) + block, F32),
        pltpu.VMEM((max(R - 1, 1), G) + block, F32),
        pltpu.VMEM((G + 1,) + block, F32),
        (sem((max(R - 1, 1), G, pieces)), sem((max(R - 1, 1), G, pieces)), sem((G, pieces)), sem((G + 1, pieces))),
    ]


def ffn_kernel(
    G,
    R,
    n3_ref,
    cot_ref,
    gate_ref,
    up_ref,
    down_ref,
    dn3_ref,
    out_ref,
    d_gate_ref,
    d_up_ref,
    d_down_ref,
    n3_buf,
    cot_buf,
    n3_high,
    n3_low,
    inner_high,
    inner_low,
    grads_high,
    grads_low,
    wide_high,
    wide_low,
    tall_high,
    tall_low,
    dn3_parts,
    dn3_pool,
    dn3_inbox,
    dn3_sems,
    n3_sems,
    cot_sems,
):
    rep, f, g, r = my_place(R)
    T, D = n3_ref.shape
    F = gate_ref.shape[1]
    rows_each = R * T
    block = (R, pieces, T // pieces, D)
    lanes = [(rep, lax.rem(g + k, G) * R + r) for k in range(1, G)]
    greet(lanes + group_peers(rep, g, r, G, R))
    chain = Chain(G, R, n3_buf, n3_sems)
    cot_chain = Chain(G, R, cot_buf, cot_sems)
    d_three = Reduce(G, R, dn3_parts, dn3_pool, dn3_inbox, dn3_sems)
    n3_buf[f] = n3_ref[...].reshape(pieces, T // pieces, D)
    chain.start()
    cot_buf[f] = cot_ref[...].reshape(pieces, T // pieces, D)
    cot_chain.start()
    for index, ref in enumerate((gate_ref, up_ref, down_ref)):
        high, low = halves(ref[...])
        span = slice(index * F, (index + 1) * F)
        wide = index < 2
        wide_high[:, span] = high if wide else high.T
        wide_low[:, span] = low if wide else low.T
        tall_high[span, :] = high.T if wide else high
        tall_low[span, :] = low.T if wide else low

    @pl.loop(0, G)
    def _(t):
        src = chain.arrive(t)
        rows = pl.ds(pl.multiple_of(src * rows_each, rows_each), rows_each)
        n3 = halves(n3_buf[pl.ds(src * R, R)].reshape(rows_each, D))
        n3_high[rows, :], n3_low[rows, :] = n3
        pre = dot3(n3, (wide_high[:, : 2 * F], wide_low[:, : 2 * F]))
        gate_pre, up_pre = pre[:, :F], pre[:, F:]
        gelu_out, gelu_slope = gelu_parts(gate_pre)
        inner = halves(gelu_out * up_pre)
        inner_high[rows, :], inner_low[rows, :] = inner
        cot_chain.arrive(t)
        cot = halves(cot_buf[pl.ds(src * R, R)].reshape(rows_each, D))
        grad_inner = dot3(cot, (wide_high[:, 2 * F :], wide_low[:, 2 * F :]))
        grads = halves(
            jnp.concatenate([grad_inner * up_pre * gelu_slope, grad_inner * gelu_out], axis=1)
        )
        grads_high[rows, :], grads_low[rows, :] = grads
        dn3 = dot3(grads, (tall_high[: 2 * F, :], tall_low[: 2 * F, :]))
        dn3_parts[src] = dn3.reshape(block)
        d_three.offer(src)
        out = dot3(inner, (tall_high[2 * F :, :], tall_low[2 * F :, :]))
        out_ref[src] = out.reshape(block)
        d_three.pooled(src)

    S = G * rows_each
    tn = (((0,), (0,)), ((), ()))
    n3 = (n3_high[...], n3_low[...])
    for index in range(G - 1):
        d_three.hand_on(index)
        if index == 0:
            d_gate_ref[...] = dot3(n3, (grads_high[:, :F], grads_low[:, :F]), tn)
        if index == 1:
            d_up_ref[...] = dot3(n3, (grads_high[:, F:], grads_low[:, F:]), tn)
    cot = halves(cot_buf[...].reshape(S, D))
    d_down_ref[...] = dot3((inner_high[...], inner_low[...]), cot, tn)
    d_three.collect(dn3_ref)
    chain.finish()
    cot_chain.finish()
    d_three.finish()


def ffn_stage(G, R, n3, cot, gate, up, down, collective_id):
    T, D = n3.shape
    F = gate.shape[1]
    n = G * R
    S = n * T
    vm = pl.BlockSpec(memory_space=pltpu.VMEM)
    block = (pieces, T // pieces, D)
    shape = lambda *dims: jax.ShapeDtypeStruct(dims, F32)
    dn3, out, d_gate, d_up, d_down = pl.pallas_call(
        functools.partial(ffn_kernel, G, R),
        out_shape=[shape(*block), shape(G, R, *block), shape(D, F), shape(D, F), shape(F, D)],
        in_specs=[vm] * 5,
        out_specs=[vm] * 5,
        scratch_shapes=[
            pltpu.VMEM((n,) + block, F32),
            pltpu.VMEM((n,) + block, F32),
            pltpu.VMEM((S, D), BF16),
            pltpu.VMEM((S, D), BF16),
            pltpu.VMEM((S, F), BF16),
            pltpu.VMEM((S, F), BF16),
            pltpu.VMEM((S, 2 * F), BF16),
            pltpu.VMEM((S, 2 * F), BF16),
            pltpu.VMEM((D, 3 * F), BF16),
            pltpu.VMEM((D, 3 * F), BF16),
            pltpu.VMEM((3 * F, D), BF16),
            pltpu.VMEM((3 * F, D), BF16),
        ]
        + reduce_scratch(G, R, pieces, (T, D))
        + [chain_sems(G, R, pieces)] * 2,
        compiler_params=pltpu.CompilerParams(
            collective_id=collective_id, has_side_effects=True, vmem_limit_bytes=vmem_bytes
        ),
    )(n3, cot, gate, up, down)
    return dn3.reshape(T, D), out, d_gate, d_up, d_down


class Fold:
    def __init__(self, G, R, Q, acc, pool, rep_in, lane_out, lane_in, out, summed, sems):
        self.G, self.R, self.Q = G, R, Q
        self.acc, self.pool, self.rep_in = acc, pool, rep_in
        self.lane_out, self.lane_in, self.out, self.summed, self.sems = lane_out, lane_in, out, summed, sems
        self.rep, self.f, self.g, self.r = my_place(R)
        self.groups = group_peers(self.rep, self.g, self.r, G, R)
        self.lanes = lane_peers(self.rep, self.g, self.r, G, R)
        self.to_rep = [lax.rem(self.rep + j, Q) for j in range(1, Q)]

    def own_copy(self, parts):
        return pltpu.make_async_copy(parts.at[:, self.r], self.acc, self.sems[8])

    def group_copy(self, parts, o, j):
        return remote(
            parts.at[o, lax.rem(self.r + j, self.R)],
            self.pool.at[j - 1, o],
            self.sems[0].at[j - 1, o],
            self.sems[1].at[j - 1, o],
            self.groups[j - 1],
        )

    def rep_copy(self, o, j):
        return remote(
            self.acc.at[o, self.to_rep[j - 1]],
            self.rep_in.at[j - 1, o],
            self.sems[2].at[j - 1, o],
            self.sems[3].at[j - 1, o],
            (self.to_rep[j - 1], self.f),
        )

    def lane_copy(self, k):
        return remote(
            self.lane_out.at[k],
            self.lane_in.at[k - 1],
            self.sems[4].at[k - 1],
            self.sems[5].at[k - 1],
            self.lanes[k - 1],
        )

    def back_copy(self, j):
        part = self.out.at[self.rep]
        return remote(
            part, part, self.sems[6].at[j - 1], self.sems[7].at[j - 1], (self.to_rep[j - 1], self.f)
        )

    def to_group(self, parts):
        for o in range(self.G):
            for j in range(1, self.R):
                self.group_copy(parts, o, j).start()
        self.own_copy(parts).start()

    def to_replicas(self, parts):
        if parts is not None:
            self.own_copy(parts).wait()
        for o in range(self.G):
            if parts is not None:
                for j in range(1, self.R):
                    self.group_copy(parts, o, j).wait_recv()
                    self.acc[o] += self.pool[j - 1, o]
            for j in range(1, self.Q):
                self.rep_copy(o, j).start()

    def to_owner(self):
        for o in range(self.G):
            for j in range(1, self.Q):
                self.rep_copy(o, j).wait_recv()
        for k in range(self.G - 1, -1, -1):
            o = lax.rem(self.g + k, self.G) if self.G > 1 else 0
            total = self.acc[o, self.rep]
            for j in range(1, self.Q):
                total = total + self.rep_in[j - 1, o]
            self.lane_out[k] = total
            if k > 0:
                self.lane_copy(k).start()

    def to_everyone(self):
        if self.summed:
            total = self.lane_out[0]
            for k in range(1, self.G):
                self.lane_copy(k).wait_recv()
                total = total + self.lane_in[k - 1]
            self.out[self.rep] = total
        else:
            self.out[self.rep, self.g] = self.lane_out[0]
            for k in range(1, self.G):
                self.lane_copy(k).wait_recv()
                self.out[self.rep, lax.rem(self.g + self.G - k, self.G)] = self.lane_in[k - 1]
        for j in range(1, self.Q):
            self.back_copy(j).start()

    def finish(self, parts):
        for j in range(1, self.Q):
            self.back_copy(j).wait_recv()
        for o in range(self.G):
            if parts is not None:
                for j in range(1, self.R):
                    self.group_copy(parts, o, j).wait_send()
            for j in range(1, self.Q):
                self.rep_copy(o, j).wait_send()
        for k in range(1, self.G):
            self.lane_copy(k).wait_send()
        for j in range(1, self.Q):
            self.back_copy(j).wait_send()


def fold_scratch(G, R, Q, m, W, pooled=True):
    sem = pltpu.SemaphoreType.DMA
    some = max(R - 1, 1) if pooled else 1
    lanes = max(G - 1, 1)
    return [
        pltpu.VMEM((G, Q, m, W), F32),
        pltpu.VMEM((some, G, Q, m, W) if pooled else (1, 1, 1, 8, 128), F32),
        pltpu.VMEM((Q - 1, G, m, W), F32),
        pltpu.VMEM((G, m, W), F32),
        pltpu.VMEM((lanes, m, W), F32),
        (
            sem((some, G)),
            sem((some, G)),
            sem((Q - 1, G)),
            sem((Q - 1, G)),
            sem((lanes,)),
            sem((lanes,)),
            sem((Q - 1,)),
            sem((Q - 1,)),
            sem,
        ),
    ]


def back_kernel(
    G,
    R,
    Q,
    heads,
    dh,
    buckets,
    fused,
    d_att_ref,
    q_ref,
    kv_ref,
    lse_ref,
    att_ref,
    vec_ref,
    ids_ref,
    own_ref,
    w_ref,
    d_gain_ref,
    enc_ref,
    ckv_w_ref,
    d_ckv_ref,
    d_wide_ref,
    out_parts_ref,
    du_ref,
    out_ref,
    d_w_out,
    d_wide_out,
    d_ckv_w_out,
    d_enc_out,
    tiny_out,
    *scratch,
):
    (strip_ref, near_ref, far_ref, dkv_ref, dq_ref, grad_ref, dkv_parts, dkv_pool) = scratch[:8]
    (d_w_parts, tiny_parts, tiny_in, enc_parts, ckv_all) = scratch[8:13]
    att_sems, dkv_send, dkv_recv, tiny_sems, tiny_rep_send, tiny_rep_recv = scratch[13:19]
    enc_sems, ckv_chain_sems, load_sem = scratch[19:22]
    rest = scratch[22:]
    ckv_scratch, du_scratch = rest[:4], rest[4:7]
    wide_scratch, dw_scratch, cw_scratch = rest[7:13], rest[13:19], rest[19:25]
    out_scratch = rest[25:]

    rep, f, g, r = my_place(R)
    n = G * R
    T = att_ref.shape[1]
    C = heads * dh
    D = w_ref.shape[0]
    groups = group_peers(rep, g, r, G, R)
    reps = [(lax.rem(rep + j, Q), f) for j in range(1, Q)]
    greet(everyone(rep, f, n, Q))

    for i in range(G):
        lane_send(G, R, i, d_att_ref, grad_ref, att_sems)
    out_sum = Reduce(G, R, *out_scratch) if fused else None
    ckv_sum = Reduce(G, R, *ckv_scratch)
    du_sum = Reduce(G, R, du_scratch[0], None, du_scratch[1], du_scratch[2])
    ckv_chain = Chain(G, R, ckv_all, ckv_chain_sems)
    wide = Fold(G, R, Q, *wide_scratch[:5], d_wide_out, True, wide_scratch[5])
    d_w = Fold(G, R, Q, *dw_scratch[:5], d_w_out, False, dw_scratch[5])
    d_cw = Fold(1, 1, Q, *cw_scratch[:5], d_ckv_w_out, True, cw_scratch[5])
    d_cw.f = f
    if fused:
        load = pltpu.make_async_copy(out_parts_ref, out_scratch[0], load_sem)
        load.start()
    ckv_scratch[0][...] = d_ckv_ref[...]
    for o in range(G):
        ckv_sum.offer(o)
    wide.to_group(d_wide_ref)
    make_strips(R, heads, T, vec_ref, strip_ref)
    near_ref[...] = jnp.zeros_like(near_ref)
    far_ref[...] = jnp.zeros_like(far_ref)
    for o in range(G):
        ckv_sum.pooled(o)
    wide.to_replicas(d_wide_ref)
    lane_wait(G, R, d_att_ref, grad_ref, att_sems)
    if fused:
        load.wait()
        for o in range(G):
            out_sum.offer(o)
    for index in range(G - 1):
        ckv_sum.hand_on(index)
    if fused:
        for o in range(G):
            out_sum.pooled(o)

    for i in range(G - 1, -1, -1):
        L = R * (i + 1) * T
        grad = grad_ref[i]
        prod_t = (grad * att_ref[i]).T
        dqs = []
        for h in range(heads):
            scores = strip_scores(R, T, i, r, h, L, kv_ref, q_ref, strip_ref)
            probs = jnp.exp(scores - lse_ref[i, h : h + 1, :])
            grad_h = grad[:, h * dh : (h + 1) * dh]
            delta = jnp.sum(prod_t[h * dh : (h + 1) * dh, :], axis=0, keepdims=True)
            grad_h = jnp.concatenate([jnp.zeros_like(grad_h), grad_h], axis=1)
            dscores = probs * (mm_nt(kv_ref[h, :L, :], grad_h) - delta)
            q_h = q_ref[h, i * T : (i + 1) * T, :]
            dkv = mm(
                jnp.concatenate([dscores, probs], axis=1), jnp.concatenate([q_h, grad_h], axis=0)
            )
            if i == G - 1:
                dkv_ref[h] = dkv
            else:
                dkv_ref[h, :L, :] += dkv
            dqs.append(mm_tn(kv_ref[h, :L, :], dscores)[:dh, :].T)
            skip = 1 if i == 0 else 0
            width = (R + 1 - skip) * T
            near_ref[h, skip * T :, :] += dscores[L - width :, :]
            if width < L:
                far_ref[h : h + 1, :] += jnp.sum(dscores[: L - width, :], axis=0, keepdims=True)
        dq_ref[i] = jnp.concatenate(dqs, axis=1)
        if i == 2:
            ckv_sum.collect(ckv_all.at[f])
            ckv_chain.start()
        if fused and i > 0:
            out_sum.hand_on(G - 1 - i)

    for i in range(G):
        for b in range(R):
            rows = slice((i * R + b) * T, (i * R + b + 1) * T)
            dkv_parts[i, b] = jnp.concatenate([dkv_ref[h, rows, :] for h in range(heads)], axis=1)

    def dkv_copy(i, j):
        return remote(
            dkv_parts.at[i, lax.rem(r + j, R)],
            dkv_pool.at[j - 1, i],
            dkv_send.at[j - 1, i],
            dkv_recv.at[j - 1, i],
            groups[j - 1],
        )

    for i in range(G):
        for j in range(1, R):
            dkv_copy(i, j).start()

    ids = jnp.broadcast_to(ids_ref[0:1, :], (2 * T, 3 * T))
    ids = pltpu.roll(ids, 0, 1, stride=1, stride_axis=0)[:, :T]
    each = buckets // n
    tiny_parts[...] = jnp.zeros_like(tiny_parts)
    for h in range(heads):
        pair = near_ref[h, pl.ds(pl.multiple_of(r * T, T), 2 * T), :]
        far = far_ref[h : h + 1, :]
        for idx in range(R - 1):
            block = jnp.sum(near_ref[h, idx * T : (idx + 1) * T, :], axis=0, keepdims=True)
            far = far + jnp.where(idx < r, block, 0.0)
        for b in range(buckets):
            part = jnp.sum(jnp.where(ids == b, pair, 0.0), axis=0, keepdims=True)
            if b == buckets - 1:
                part = part + far
            row = h * each + b % each
            tiny_parts[b // each, row : row + 1, :] = part
    last = heads * each
    for o in range(n):
        tiny_parts[o, last : last + 1, :] = d_gain_ref[o : o + 1, :]
    tiny = Deal(n, tiny_parts, tiny_in, tiny_sems)
    tiny.start()
    ckv_chain.arrive(0)
    ckv_chain.arrive(1)

    order = list(range(G))
    for i in order:
        for j in range(1, R):
            dkv_copy(i, j).wait_recv()
        dkv = dkv_parts[i, r]
        for j in range(1, R):
            dkv = dkv + dkv_pool[j - 1, i]
        dq_all = jnp.concatenate([dkv, dq_ref[i]], axis=1)
        du_scratch[0][i, 0] = mm_nt(dq_all, w_ref[...]).reshape(du_scratch[0].shape[2:])
        du_sum.pooled(i)
        part = mm_tn(own_ref[i * T : (i + 1) * T, :], dq_all).reshape(d_w_parts.shape)
        if i == 0:
            d_w_parts[...] = part
        else:
            d_w_parts[...] += part
    d_w.to_group(d_w_parts)
    for index in range(G - 1):
        du_sum.hand_on(index)
        if index == 0:
            wide.to_owner()
            ckv_chain.arrive(2)
    d_w.to_replicas(d_w_parts)
    ckv_chain.arrive(3)
    d_ckv = ckv_all[...].reshape(enc_ref.shape[0], 2 * D)
    enc_parts[...] = mm_nt(d_ckv, ckv_w_ref[...]).reshape(enc_parts.shape)
    d_enc = Deal(n, enc_parts, d_enc_out, enc_sems)
    d_enc.start()
    d_cw.acc[0] = mm_tn(enc_ref[...], d_ckv).reshape(d_cw.acc.shape[1:])
    d_cw.to_replicas(None)
    tiny.arrive()
    for s in range(G):
        total = tiny_in[s * R]
        for j in range(1, R):
            total = total + tiny_in[s * R + j]
        tiny_out[rep, s] = total

    def tiny_copy(j):
        part = tiny_out.at[rep]
        return remote(part, part, tiny_rep_send.at[j - 1], tiny_rep_recv.at[j - 1], reps[j - 1])

    for j in range(1, Q):
        tiny_copy(j).start()
    wide.to_everyone()
    d_w.to_owner()
    d_cw.to_owner()
    d_cw.to_everyone()
    d_w.to_everyone()
    if fused:
        out_sum.collect(out_ref)
    du_sum.collect(du_ref)

    d_enc.arrive()
    for j in range(1, Q):
        tiny_copy(j).wait()
    tiny.finish()
    d_enc.finish()
    for i in range(G):
        for j in range(1, R):
            dkv_copy(i, j).wait_send()
    if fused:
        out_sum.finish()
    ckv_sum.finish()
    du_sum.finish()
    ckv_chain.finish()
    wide.finish(d_wide_ref)
    d_w.finish(d_w_parts)
    d_cw.finish(None)


def back_stage(
    G,
    R,
    Q,
    heads,
    dh,
    buckets,
    d_att,
    q,
    kv,
    lse,
    att,
    vec,
    ids,
    unit_own,
    w_cols,
    d_gain,
    enc_cols,
    ckv_w,
    d_ckv,
    d_wide,
    out_parts,
    collective_id,
):
    n = G * R
    S = kv.shape[1]
    T = S // n
    D = w_cols.shape[0]
    C = heads * dh
    Dn = D // n
    m = Dn // Q
    enc_rows = enc_cols.shape[0] // n
    block = (pieces, T // pieces, D)
    tiny_rows = -(-(heads * (buckets // n) + 1) // 8) * 8
    vm = pl.BlockSpec(memory_space=pltpu.VMEM)
    hbm = pl.BlockSpec(memory_space=pl.ANY)
    shape = lambda *dims: jax.ShapeDtypeStruct(dims, F32)
    sem = pltpu.SemaphoreType.DMA
    some = max(R - 1, 1)
    du_parts = reduce_scratch(G, 1, pieces, (T, D))
    fused = R <= 2
    outs = pl.pallas_call(
        functools.partial(back_kernel, G, R, Q, heads, dh, buckets, fused),
        out_shape=[
            shape(*block),
            shape(*block),
            shape(Q, G, m, 3 * C),
            shape(Q, m, 3 * D),
            shape(Q, m, 2 * D),
            shape(n, enc_rows, Dn),
            shape(Q, G, tiny_rows, T),
        ],
        in_specs=[vm] * 13 + [hbm] * 2,
        out_specs=[vm] * 7,
        scratch_shapes=[
            pltpu.VMEM((heads, 2 * R * T, T), F32),
            pltpu.VMEM((heads, (R + 1) * T, T), F32),
            pltpu.VMEM((8, T), F32),
            pltpu.VMEM((heads, S, 2 * dh), F32),
            pltpu.VMEM((G, T, C), F32),
            pltpu.VMEM((G, T, C), F32),
            pltpu.VMEM((G, R, T, 2 * C), F32),
            pltpu.VMEM((some, G, T, 2 * C), F32),
            pltpu.VMEM((G, R, Q, m, 3 * C), F32),
            pltpu.VMEM((n, tiny_rows, T), F32),
            pltpu.VMEM((n, tiny_rows, T), F32),
            pltpu.VMEM((n, enc_rows, Dn), F32),
            pltpu.VMEM((n, 1, enc_rows, 2 * D), F32),
            lane_sems(G),
            sem((some, G)),
            sem((some, G)),
            deal_sems(n),
            sem((Q - 1,)),
            sem((Q - 1,)),
            deal_sems(n),
            chain_sems(G, R, 1),
            sem,
        ]
        + reduce_scratch(G, R, 1, (enc_rows, 2 * D))
        + [du_parts[0], du_parts[2], du_parts[3]]
        + fold_scratch(G, R, Q, m, 3 * D)
        + fold_scratch(G, R, Q, m, 3 * C)
        + fold_scratch(1, 1, Q, m, 2 * D, False)
        + (reduce_scratch(G, R, pieces, (T, D)) if fused else []),
        compiler_params=pltpu.CompilerParams(
            collective_id=collective_id, has_side_effects=True, vmem_limit_bytes=vmem_bytes
        ),
    )(
        d_att,
        q,
        kv,
        lse,
        att,
        vec,
        ids,
        unit_own,
        w_cols,
        d_gain,
        enc_cols,
        ckv_w,
        d_ckv.reshape(G, R, 1, enc_rows, 2 * D),
        d_wide.reshape(G, R, Q, m, 3 * D),
        out_parts,
    )
    if not fused:
        outs = list(outs)
        outs[1] = scatter(G, R, out_parts.reshape(G, R, T, D), True, True, collective_id + 1)
    return outs


def to_heads(rows, heads):
    return jnp.transpose(rows.reshape(rows.shape[0], heads, -1), (1, 0, 2))


def from_heads(rows):
    return jnp.transpose(rows, (1, 0, 2)).reshape(rows.shape[1], -1)


def bmm(spec, a, b):
    return jnp.einsum(spec, a, b, precision=HIGH, preferred_element_type=F32)


def shards(
    n,
    inputs,
    encoder,
    self_gain,
    cross_gain,
    ffn_gain,
    self_query,
    self_key,
    self_value,
    self_output,
    position_bias,
    bucket_table,
    cross_query,
    cross_key,
    cross_value,
    cross_output,
    ffn_gate,
    ffn_up,
    ffn_down,
    cotangent,
):
    x = inputs[0]
    enc = encoder[0]
    cot = cotangent[0]
    T, D = x.shape
    buckets, H = position_bias.shape
    dh = D // H
    G = math.gcd(H, n)
    R = n // G
    heads = H // G
    C = heads * dh
    Dn = D // n
    enc_local = enc.shape[0]
    f = lax.axis_index("fsdp")
    g, r = f // R, lax.rem(f, R)

    Q = lax.axis_size("rep")
    q = lax.axis_index("rep")
    part = Dn // Q

    def fold(w, gain):
        return w * gain[:, None]

    def mine(w):
        return lax.dynamic_slice_in_dim(w, q * part, part, 0)

    def by_group(w):
        return fold(mine(w), mine(self_gain)).reshape(part, G, heads, dh)

    w_mine = jnp.concatenate([by_group(self_key), by_group(self_value)], axis=3)
    w_mine = jnp.concatenate(
        [w_mine.reshape(part, G, 2 * C), by_group(self_query).reshape(part, G, C)], axis=2
    )
    w_mine = jnp.transpose(w_mine, (1, 0, 2))
    wide_mine = jnp.concatenate(
        [mine(self_output), fold(mine(cross_query), mine(cross_gain)), mine(cross_output)], axis=1
    )
    dist = jnp.concatenate(
        [jnp.arange(T, 2 * T), jnp.full((T,), -1), jnp.arange(T)]
    )
    row_bucket = jnp.concatenate(
        [bucket_table[T : 2 * T], jnp.zeros((T,), jnp.int32), bucket_table[:T]]
    )
    onehot = (row_bucket[:, None] == jnp.arange(buckets, dtype=jnp.int32)[None, :]).astype(F32)
    vec = jnp.dot(
        onehot, position_bias - position_bias[buckets - 1 :], precision=lax.Precision.HIGHEST
    )
    vec = jnp.where(dist[:, None] < 0, masked_score, vec)
    vec = lax.dynamic_slice_in_dim(vec.T, g * heads, heads, 0)
    vec = jnp.pad(vec, ((0, 8 - heads), (0, 0)))
    ids = jnp.broadcast_to(
        jnp.where(dist < 0, -1, row_bucket).astype(F32)[None, :], (8, 3 * T)
    )

    small = jnp.transpose(enc.reshape(enc_local, n, Dn), (1, 0, 2))
    small = jnp.concatenate([small, jnp.broadcast_to(ffn_gain, (n, 8, Dn))], axis=1)
    ckv_w = jnp.concatenate([cross_key, cross_value], axis=1)
    att, att_rows, q, kv, lse, w_cols, unit_own, small_all, ckv, wide_all = first_stage(
        G, R, Q, heads, dh, x, w_mine, wide_mine, small, ckv_w, vec, 1
    )
    enc_cols = small_all[:, :enc_local, :].reshape(n * enc_local, Dn)
    gain_three = small_all[:, enc_local, :].reshape(D)
    ckv = ckv.reshape(n * enc_local, 2 * D)
    w_cols = w_cols.reshape(D, 3 * C)
    wide_all = wide_all.reshape(D, 3 * D)
    so_full, cq_full, co_full = wide_all[:, :D], wide_all[:, D : 2 * D], wide_all[:, 2 * D :]
    attended = jnp.transpose(att_rows, (1, 0, 2)).reshape(T, D)

    after = x + mm(attended, so_full)
    unit_two, scale_two = unit_of(after)
    cq = to_heads(mm(unit_two, cq_full), H)
    ck, cv = to_heads(ckv[:, :D], H), to_heads(ckv[:, D:], H)
    cscores = bmm("hqd,hkd->hqk", cq, ck)
    cweights = jnp.exp(cscores - jnp.max(cscores, axis=2, keepdims=True))
    cprobs = cweights / jnp.sum(cweights, axis=2, keepdims=True)
    cout = bmm("hqk,hkd->hqd", cprobs, cv)
    cflat = from_heads(cout)
    middle = after + mm(cflat, co_full)
    unit_three, scale_three = unit_of(middle)
    normed_three = unit_three * gain_three

    dn3, out_parts, d_gate, d_up, d_down = ffn_stage(
        G, R, normed_three, cot, ffn_gate, ffn_up, ffn_down, 3
    )
    d_gate, d_up, d_down = lax.psum((d_gate, d_up, d_down), "rep")

    d_gain_three = jnp.sum(dn3 * unit_three, axis=0)
    d_middle = cot + unit_backward(dn3 * gain_three, unit_three, scale_three)
    d_co = mm_tn(cflat, d_middle)
    d_cout = to_heads(mm_nt(d_middle, co_full), H)
    cdelta = jnp.sum(d_cout * cout, axis=2)
    d_cprobs = bmm("hqd,hkd->hqk", d_cout, cv)
    d_cscores = cprobs * (d_cprobs - cdelta[:, :, None])
    d_cq = from_heads(bmm("hqk,hkd->hqd", d_cscores, ck))
    d_ck = from_heads(bmm("hqk,hqd->hkd", d_cscores, cq))
    d_cv = from_heads(bmm("hqk,hqd->hkd", cprobs, d_cout))
    d_after = d_middle + unit_backward(mm_nt(d_cq, cq_full), unit_two, scale_two)
    d_cq_w = mm_tn(unit_two, d_cq)
    d_ckv = jnp.concatenate([d_ck, d_cv], axis=1)
    d_gain = jnp.pad(d_gain_three.reshape(n, Dn), ((0, 0), (0, T - Dn)))

    d_att = jnp.transpose(mm_nt(d_after, so_full).reshape(T, G, C), (1, 0, 2))
    d_wide = jnp.concatenate([mm_tn(attended, d_after), d_cq_w, d_co], axis=1)
    du, out_sum, d_w, d_wide, d_ckv_w, d_enc, tiny = back_stage(
        G,
        R,
        Q,
        heads,
        dh,
        buckets,
        d_att,
        q,
        kv,
        lse,
        att,
        vec,
        ids,
        unit_own,
        w_cols,
        d_gain,
        enc_cols,
        ckv_w,
        d_ckv,
        d_wide,
        out_parts,
        5,
    )
    out_rows = middle + out_sum.reshape(T, D)
    unit_one, scale_one = unit_of(x)
    d_x = d_after + unit_backward(du.reshape(T, D), unit_one, scale_one)
    d_enc = jnp.transpose(d_enc, (1, 0, 2)).reshape(enc_local, D)
    d_w = jnp.transpose(d_w, (0, 2, 1, 3)).reshape(Dn, G, 3 * C)
    dwq = d_w[:, :, 2 * C :].reshape(Dn, D)
    d_kv = d_w[:, :, : 2 * C].reshape(Dn, H, 2 * dh)
    dwk, dwv = d_kv[:, :, :dh].reshape(Dn, D), d_kv[:, :, dh:].reshape(Dn, D)
    d_wide = d_wide.reshape(Dn, 3 * D)
    d_ckv_w = d_ckv_w.reshape(Dn, 2 * D)
    dso, dcq, dco = (d_wide[:, a * D : (a + 1) * D] for a in range(3))
    each = buckets // n
    tiny = jnp.sum(tiny, axis=0)
    grad_bias = jnp.sum(tiny[:, : heads * each, :], axis=2).reshape(G, heads, each)
    grad_bias = jnp.transpose(grad_bias, (2, 0, 1)).reshape(each, H)
    g_ffn = jnp.sum(tiny[:, heads * each, :Dn], axis=0)
    g_self = jnp.sum(dwq * self_query + dwk * self_key + dwv * self_value, axis=1)
    g_cross = jnp.sum(dcq * cross_query, axis=1)
    return (
        out_rows[None],
        d_x[None],
        d_enc[None],
        g_self,
        g_cross,
        g_ffn,
        fold(dwq, self_gain),
        fold(dwk, self_gain),
        fold(dwv, self_gain),
        dso,
        grad_bias,
        fold(dcq, cross_gain),
        d_ckv_w[:, :D],
        d_ckv_w[:, D:],
        dco,
        d_gate,
        d_up,
        d_down,
    )


def solution(mesh):
    rows = P("rep", "fsdp", None)
    gain = P("fsdp")
    weight = P("fsdp", None)
    columns = P(None, "fsdp")
    args = (rows, rows, gain, gain, gain) + (weight,) * 4 + (P(), P()) + (weight,) * 4
    args += (columns, columns, weight, rows)
    outs = (rows, rows, rows, gain, gain, gain) + (weight,) * 9 + (columns, columns, weight)
    return jax.shard_map(
        functools.partial(shards, mesh.shape["fsdp"]),
        mesh=mesh,
        in_specs=args,
        out_specs=outs,
        check_vma=False,
    )
```

```python
import functools
import math

import jax
import jax.numpy as jnp
from jax import lax
from jax.experimental import pallas as pl
from jax.experimental.pallas import tpu as pltpu
from jax.sharding import PartitionSpec as P

HIGH = lax.Precision.HIGH
MESH = pl.DeviceIdType.MESH
F32 = jnp.float32
eps_norm = 1e-06
gelu_coef = math.sqrt(2.0 / math.pi)
masked_score = -1e30
vmem_bytes = 62 << 20
pieces = 2


def mm(a, b):
    return jnp.dot(a, b, precision=HIGH, preferred_element_type=F32)


def mm_tn(a, b):
    return lax.dot_general(
        a, b, (((0,), (0,)), ((), ())), precision=HIGH, preferred_element_type=F32
    )


def mm_nt(a, b):
    return lax.dot_general(
        a, b, (((1,), (1,)), ((), ())), precision=HIGH, preferred_element_type=F32
    )


BF16 = jnp.bfloat16


def halves(a):
    high = a.astype(BF16)
    return high, (a - high.astype(F32)).astype(BF16)


def dot3(a, b, dims=(((1,), (0,)), ((), ()))):
    def dot(x, y):
        return lax.dot_general(x, y, dims, preferred_element_type=F32)

    return dot(a[0], b[0]) + (dot(a[0], b[1]) + dot(a[1], b[0]))


def unit_of(rows):
    scale = lax.rsqrt(jnp.mean(rows * rows, axis=-1, keepdims=True) + eps_norm)
    return rows * scale, scale


def unit_backward(grad_unit, unit, scale):
    return scale * (grad_unit - unit * jnp.mean(grad_unit * unit, axis=-1, keepdims=True))


def gelu_parts(gate_pre):
    squared = gate_pre * gate_pre
    tangent = jnp.tanh(gelu_coef * (gate_pre + 0.044715 * squared * gate_pre))
    gelu_out = 0.5 * gate_pre * (1.0 + tangent)
    gelu_slope = 0.5 * (1.0 + tangent) + 0.5 * gate_pre * (1.0 - tangent * tangent) * gelu_coef * (
        1.0 + 3.0 * 0.044715 * squared
    )
    return (gelu_out, gelu_slope)


def my_place(R):
    rep = lax.axis_index("rep")
    f = lax.axis_index("fsdp")
    return rep, f, f // R, lax.rem(f, R)


def greet(peers):
    barrier = pltpu.get_barrier_semaphore()
    for peer in peers:
        pl.semaphore_signal(barrier, inc=1, device_id=peer, device_id_type=MESH)
    pl.semaphore_wait(barrier, len(peers))


def remote(src, dst, send_sem, recv_sem, peer):
    return pltpu.make_async_remote_copy(
        src_ref=src,
        dst_ref=dst,
        send_sem=send_sem,
        recv_sem=recv_sem,
        device_id=peer,
        device_id_type=MESH,
    )


def lane_peers(rep, g, r, G, R):
    return [(rep, lax.rem(g + k, G) * R + r) for k in range(1, G)]


def group_peers(rep, g, r, G, R):
    return [(rep, g * R + lax.rem(r + j, R)) for j in range(1, R)]


def comm_call(kernel, outs, ins, scratch, collective_id, vmem_ins=False, vmem_outs=False):
    def space(vmem):
        return pl.BlockSpec(memory_space=pltpu.VMEM if vmem else pl.ANY)

    return pl.pallas_call(
        kernel,
        out_shape=outs,
        in_specs=[space(vmem_ins)] * len(ins),
        out_specs=[space(vmem_outs)] * len(outs),
        scratch_shapes=scratch,
        compiler_params=pltpu.CompilerParams(
            collective_id=collective_id, has_side_effects=True, vmem_limit_bytes=vmem_bytes
        ),
    )(*ins)


def scatter_kernel(G, R, pooled, summed, x_ref, o_ref, *scratch):
    rep, f, g, r = my_place(R)
    lanes = lane_peers(rep, g, r, G, R)
    groups = group_peers(rep, g, r, G, R) if pooled else []
    if pooled:
        group_buf, group_send, group_recv = scratch[:3]
        scratch = scratch[3:]
    lane_out, lane_in, lane_send, lane_recv = scratch
    greet(lanes + groups)
    order = list(range(G - 1, -1, -1))
    group_copies = []
    if pooled:
        for k in order:
            for j in range(1, R):
                copy = remote(
                    x_ref.at[lax.rem(g + k, G), lax.rem(r + j, R)],
                    group_buf.at[j - 1, k],
                    group_send.at[j - 1, k],
                    group_recv.at[j - 1, k],
                    groups[j - 1],
                )
                copy.start()
                group_copies.append((j, k, copy))
    lane_copies = []
    for k in order:
        to = lax.rem(g + k, G)
        if pooled:
            for j, kk, copy in group_copies:
                if kk == k:
                    copy.wait_recv()
            total = x_ref[to, r]
            for j in range(1, R):
                total = total + group_buf[j - 1, k]
        else:
            total = x_ref[to]
        if k > 0:
            lane_out[k - 1] = total
            copy = remote(
                lane_out.at[k - 1], lane_in.at[k - 1], lane_send.at[k - 1], lane_recv.at[k - 1], lanes[k - 1]
            )
            copy.start()
            lane_copies.append((k, copy))
        elif summed:
            o_ref[...] = total
        else:
            o_ref[g] = total
    for k, copy in lane_copies:
        copy.wait_recv()
        if summed:
            o_ref[...] += lane_in[k - 1]
        else:
            o_ref[lax.rem(g + G - k, G)] = lane_in[k - 1]
    for _, copy in lane_copies:
        copy.wait_send()
    for _, _, copy in group_copies:
        copy.wait_send()


def scatter(G, R, x, pooled, summed, collective_id):
    block = x.shape[2:] if pooled else x.shape[1:]
    sem = pltpu.SemaphoreType.DMA
    scratch = []
    if pooled:
        scratch = [
            pltpu.VMEM((max(R - 1, 1), G) + block, F32),
            sem((max(R - 1, 1), G)),
            sem((max(R - 1, 1), G)),
        ]
    scratch += [
        pltpu.VMEM((G - 1,) + block, F32),
        pltpu.VMEM((G - 1,) + block, F32),
        sem((G - 1,)),
        sem((G - 1,)),
    ]
    out = jax.ShapeDtypeStruct(block if summed else (G,) + block, F32)
    return comm_call(
        functools.partial(scatter_kernel, G, R, pooled, summed),
        [out],
        [x],
        scratch,
        collective_id,
        vmem_ins=True,
        vmem_outs=True,
    )[0]


def named(names, refs):
    return dict(zip(names, refs, strict=True))


def first_kernel(G, R, Q, H, dh, names, *refs):
    m = named(names, refs)
    rep, f, g, r = my_place(R)
    n = G * R
    heads = H // G
    T, D = m["x"].shape
    C = heads * dh
    greet(everyone(rep, f, n, Q))

    small = Deal(n, m["small"], m["small_all"], m["small_sems"])
    weights = Spread(G, R, Q, lambda k: m["w_mine"].at[lax.rem(g + k, G)], m["w"], m["w_sems"])
    wide = Spread(G, R, Q, lambda k: m["wide_mine"], m["wide"], m["wide_sems"])
    chain = Chain(G, R, m["x_buf"], m["x_sems"])
    cot_chain = Chain(G, R, m["cot_all"], m["cot_sems"])
    ckv_sum = Reduce(G, R, *m["ckv_scratch"])
    ckv_chain = Chain(G, R, m["ckv"], m["ckv_chain_sems"])
    small.start()
    weights.start()
    wide.start()
    m["x_buf"][f] = m["x"][...].reshape(pieces, T // pieces, D)
    chain.start()
    cot_own = pltpu.make_async_copy(m["cot"], m["cot_all"].at[f], m["cot_own_sem"])
    cot_own.start()
    make_strips(R, heads, T, m["vec"], m["strip"])
    weights.across()
    small.arrive()
    ckv_parts = ckv_sum.parts
    enc_rows = ckv_parts.shape[3]
    enc_cols = m["small_all"][:, :enc_rows, :].reshape(n * enc_rows, m["small"].shape[2])
    ckv_parts[...] = mm(enc_cols, m["ckv_w"][...]).reshape(ckv_parts.shape)
    gain = jnp.concatenate([m["small_all"][s, enc_rows : enc_rows + 1, :] for s in range(n)], axis=1)
    m["gain"][...] = gain
    for o in range(G):
        ckv_sum.offer(o)
    wide.across()
    weights.share()
    for o in range(G):
        ckv_sum.pooled(o)
    weights.arrive()
    w = m["w"][...].reshape(D, 3 * C)
    for t in range(G):
        src = chain.arrive(t)
        if t > 0:
            ckv_sum.hand_on(t - 1)
        unit, _ = unit_of(m["x_buf"][pl.ds(src * R, R)].reshape(R * T, D))
        rows = pl.ds(pl.multiple_of(src * (R * T), R * T), R * T)
        m["unit"][...] = unit
        mine = m["unit"][pl.ds(pl.multiple_of(r * T, T), T), :]
        mine_rows = pl.ds(pl.multiple_of(src * T, T), T)
        m["own"][mine_rows, :] = mine
        kv = mm(unit, w[:, : 2 * C])
        q = mm(mine, w[:, 2 * C :])
        for h in range(heads):
            m["kv"][h, rows, :] = kv[:, 2 * h * dh : 2 * (h + 1) * dh]
            m["q"][h, mine_rows, :] = beside(q[:, h * dh : (h + 1) * dh], 0)
    ckv_sum.collect(m["ckv"].at[f])
    ckv_chain.start()
    cot_own.wait()
    cot_chain.start()
    for i in range(G):
        L = R * (i + 1) * T
        outs = []
        for h in range(heads):
            scores = strip_scores(R, T, i, r, h, L, m["kv"], m["q"], m["strip"])
            top = jnp.max(scores, axis=0, keepdims=True)
            probs = jnp.exp(scores - top)
            total = jnp.sum(probs, axis=0, keepdims=True)
            out_t = mm_tn(m["kv"][h, :L, :], probs)[dh:, :] / total
            outs.append(out_t.T)
            m["lse"][i, h : h + 1, :] = top + jnp.log(total)
        m["att"][i] = jnp.concatenate(outs, axis=1)
        lane_send(G, R, i, m["att"], m["rows"], m["att_sems"])
        ckv_chain.arrive(i)
    wide.share()
    cot_chain.arrive(0)
    cot_chain.arrive(1)
    lane_wait(G, R, m["att"], m["rows"], m["att_sems"])
    wide.arrive()

    attended = jnp.concatenate([m["rows"][i] for i in range(G)], axis=1)
    after = m["x"][...] + mm(attended, m["wide"][:, :, 0].reshape(D, D))
    m["after"][...] = after
    unit_two, _ = unit_of(after)
    m["cq"][...] = mm(unit_two, m["wide"][:, :, 1].reshape(D, D))
    cot_chain.arrive(2)
    enc_count = n * enc_rows
    for h in range(0, H, 2):
        outs = []
        for a in (h, h + 1):
            ckv = m["ckv"][:, 0, :, 2 * a * dh : 2 * (a + 1) * dh].reshape(enc_count, 2 * dh)
            scores = mm_nt(ckv, beside(m["cq"][:, a * dh : (a + 1) * dh], 0))
            probs = jnp.exp(scores - jnp.max(scores, axis=0, keepdims=True))
            probs = probs / jnp.sum(probs, axis=0, keepdims=True)
            m["probs"][a] = probs
            outs.append(mm_tn(ckv, probs)[dh:, :].T)
        m["cflat"][:, h * dh : (h + 2) * dh] = jnp.concatenate(outs, axis=1)
    middle = after + mm(m["cflat"][...], m["wide"][:, :, 2].reshape(D, D))
    m["middle"][...] = middle
    unit_three, _ = unit_of(middle)
    m["n3"][...] = unit_three * gain
    cot_chain.arrive(3)

    small.finish()
    weights.finish()
    chain.finish()
    cot_chain.finish()
    ckv_sum.finish()
    ckv_chain.finish()
    wide.finish()


def beside(a, at):
    zero = jnp.zeros_like(a)
    return jnp.concatenate([zero, a] if at else [a, zero], axis=1)


def lane_send(G, R, i, src_ref, dst_ref, sems):
    rep, f, g, r = my_place(R)

    @pl.when(g == i)
    def _():
        pltpu.make_async_copy(src_ref.at[i], dst_ref.at[i], sems[2]).start()

    @pl.when(g != i)
    def _():
        remote(src_ref.at[i], dst_ref.at[g], sems[0].at[i], sems[1].at[g], (rep, i * R + r)).start()


def lane_wait(G, R, src_ref, dst_ref, sems):
    rep, f, g, r = my_place(R)
    pltpu.make_async_copy(src_ref.at[g], dst_ref.at[g], sems[2]).wait()
    for i in range(G):

        @pl.when(g != i)
        def _():
            copy = remote(src_ref.at[i], dst_ref.at[i], sems[0].at[i], sems[1].at[i], (rep, i * R + r))
            copy.wait_send()
            copy.wait_recv()


def lane_sems(G):
    sem = pltpu.SemaphoreType.DMA
    return (sem((G,)), sem((G,)), sem)


class Spread:
    def __init__(self, G, R, Q, source, out, sems):
        self.sizes = (G, R, Q)
        self.source, self.out, self.sems = source, out, sems
        rep, f, g, r = my_place(R)
        self.place = (rep, f, g, r)
        self.lanes = lane_peers(rep, g, r, G, R)
        self.groups = group_peers(rep, g, r, G, R)
        self.reps = [(lax.rem(rep + j, Q), f) for j in range(1, Q)]

    def slot(self, k):
        G, R, Q = self.sizes
        _, _, g, r = self.place
        return lax.rem(g + G - k, G) * R + r

    def lane_copy(self, k):
        rep, f = self.place[:2]
        return remote(
            self.source(k), self.out.at[f, rep], self.sems[0].at[k - 1], self.sems[1].at[k - 1], self.lanes[k - 1]
        )

    def own_copy(self):
        rep, f = self.place[:2]
        return pltpu.make_async_copy(self.source(0), self.out.at[f, rep], self.sems[6])

    def rep_copy(self, k, j):
        part = self.out.at[self.slot(k), self.place[0]]
        return remote(part, part, self.sems[2].at[k, j - 1], self.sems[3].at[k, j - 1], self.reps[j - 1])

    def group_copy(self, k, j):
        part = self.out.at[self.slot(k)]
        return remote(part, part, self.sems[4].at[k, j - 1], self.sems[5].at[k, j - 1], self.groups[j - 1])

    def start(self):
        G = self.sizes[0]
        for k in range(G - 1, 0, -1):
            self.lane_copy(k).start()
        self.own_copy().start()

    def across(self):
        G, R, Q = self.sizes
        for k in range(G):
            if k == 0:
                self.own_copy().wait()
            else:
                self.lane_copy(k).wait_recv()
            for j in range(1, Q):
                self.rep_copy(k, j).start()

    def share(self):
        G, R, Q = self.sizes
        for k in range(G):
            for j in range(1, Q):
                self.rep_copy(k, j).wait_recv()
            for j in range(1, R):
                self.group_copy(k, j).start()

    def arrive(self):
        G, R, Q = self.sizes
        for k in range(G):
            for j in range(1, R):
                self.group_copy(k, j).wait_recv()

    def finish(self):
        G, R, Q = self.sizes
        for k in range(G):
            if k > 0:
                self.lane_copy(k).wait_send()
            for j in range(1, Q):
                self.rep_copy(k, j).wait_send()
            for j in range(1, R):
                self.group_copy(k, j).wait_send()


class Deal:
    def __init__(self, n, parts, out, sems):
        self.n, self.parts, self.out, self.sems = n, parts, out, sems
        self.rep, self.f = lax.axis_index("rep"), lax.axis_index("fsdp")

    def copy(self, k):
        to = lax.rem(self.f + k, self.n)
        return remote(
            self.parts.at[to],
            self.out.at[self.f],
            self.sems[0].at[k - 1],
            self.sems[1].at[k - 1],
            (self.rep, to),
        )

    def start(self):
        for k in range(1, self.n):
            self.copy(k).start()
        self.out[self.f] = self.parts[self.f]

    def arrive(self):
        for k in range(1, self.n):
            self.copy(k).wait_recv()

    def finish(self):
        for k in range(1, self.n):
            self.copy(k).wait_send()


def deal_sems(n):
    sem = pltpu.SemaphoreType.DMA
    return (sem((n - 1,)), sem((n - 1,)))


def everyone(rep, f, n, Q):
    return [(rep, lax.rem(f + k, n)) for k in range(1, n)] + [
        (lax.rem(rep + j, Q), f) for j in range(1, Q)
    ]


def spread_sems(G, R, Q):
    sem = pltpu.SemaphoreType.DMA
    return (
        sem((G - 1,)),
        sem((G - 1,)),
        sem((G, Q - 1)),
        sem((G, Q - 1)),
        sem((G, R - 1)),
        sem((G, R - 1)),
        sem,
    )


def lookup(table, i, t):
    rows, columns = len(table), len(table[0])
    flat = i * columns + t
    value = table[0][0] + 0 * flat
    for a in range(rows):
        for b in range(columns):
            if table[a][b] != table[0][0]:
                value = jnp.where(flat == a * columns + b, table[a][b], value)
    return value


class Chain:
    def __init__(self, G, R, buf, sems):
        self.G, self.R, self.buf, self.sems = G, R, buf, sems
        self.pieces = buf.shape[1]
        self.rep, self.f, self.g, self.r = my_place(R)
        self.groups = group_peers(self.rep, self.g, self.r, G, R)
        self.order, self.first, self.second = [], [], []
        for i in range(G):
            order = sorted(range(G), key=lambda s: (abs(s - i), s))
            self.order.append(order)
            far = [abs(s - i) for s in order]
            fresh = [t > 0 and far[t] != far[t - 1] for t in range(G)]
            paired = [fresh[t] and t + 1 < G and far[t + 1] == far[t] for t in range(G)]
            self.first.append([order[t] if fresh[t] else -1 for t in range(G)])
            self.second.append([order[t + 1] if paired[t] else -1 for t in range(G)])

    def part(self, src, p):
        return self.buf.at[src * self.R + self.r, p]

    def step(self, src, side, p):
        part = self.part(src, p)
        to = (self.rep, (self.g + side) * self.R + self.r)
        way = 0 if side > 0 else 1
        return remote(part, part, self.sems[0].at[way, src, p], self.sems[1].at[src, p], to)

    def group_copy(self, src, j, p):
        part = self.part(src, p)
        return remote(
            part, part, self.sems[2].at[j - 1, src, p], self.sems[3].at[j - 1, src, p], self.groups[j - 1]
        )

    def sends(self, src):
        right = jnp.logical_and(src <= self.g, self.g < self.G - 1)
        left = jnp.logical_and(src >= self.g, self.g > 0)
        return ((1, right), (-1, left))

    def onward(self, src, p):
        for side, cond in self.sends(src):

            @pl.when(cond)
            def _():
                self.step(src, side, p).start()

        for j in range(1, self.R):
            self.group_copy(src, j, p).start()

    def start(self):
        for p in range(self.pieces):
            self.onward(self.g, p)

    def arrive(self, t):
        for table in (self.first, self.second):
            came = lookup(table, self.g, t)

            @pl.when(came >= 0)
            def _():
                for p in range(self.pieces):
                    self.step(came, 1, p).wait_recv()
                    self.onward(came, p)

        src = lookup(self.order, self.g, t)
        for j in range(1, self.R):
            for p in range(self.pieces):
                self.group_copy(src, j, p).wait_recv()
        return src

    def finish(self):
        for src in range(self.G):
            for p in range(self.pieces):
                for side, cond in self.sends(src):

                    @pl.when(cond)
                    def _():
                        self.step(src, side, p).wait_send()

                for j in range(1, self.R):
                    self.group_copy(src, j, p).wait_send()


def chain_sems(G, R, pieces):
    sem = pltpu.SemaphoreType.DMA
    return (sem((2, G, pieces)), sem((G, pieces)), sem((R - 1, G, pieces)), sem((R - 1, G, pieces)))


def make_strips(R, heads, T, vec_ref, strip_ref):
    for h in range(heads):
        vec = jnp.broadcast_to(vec_ref[h : h + 1, :], (2 * T, 3 * T))
        pair = pltpu.roll(vec, 0, 1, stride=1, stride_axis=0)[:, :T]
        if R > 1:
            strip_ref[h, : (R - 1) * T, :] = jnp.zeros(((R - 1) * T, T), F32)
            strip_ref[h, (R + 1) * T :, :] = jnp.full(((R - 1) * T, T), masked_score, F32)
        strip_ref[h, (R - 1) * T : (R + 1) * T, :] = pair


def strip_scores(R, T, i, r, h, L, kv_ref, q_ref, strip_ref):
    scores = mm_nt(kv_ref[h, :L, :], q_ref[h, i * T : (i + 1) * T, :])
    skip = 1 if i == 0 else 0
    width = (R + 1 - skip) * T
    start = pl.multiple_of((R - 1 - r + skip) * T, T)
    near = scores[L - width :, :] + strip_ref[h, pl.ds(start, width), :]
    if width == L:
        return near
    return jnp.concatenate([scores[: L - width, :], near], axis=0)


def call_stage(kernel, ins, outs, scratch, collective_id):
    vm = pl.BlockSpec(memory_space=pltpu.VMEM)
    hbm = pl.BlockSpec(memory_space=pl.ANY)
    names = tuple(ins) + tuple(outs) + tuple(scratch)
    results = pl.pallas_call(
        functools.partial(kernel, names),
        out_shape=[jax.ShapeDtypeStruct(shape, F32) for shape, _ in outs.values()],
        in_specs=[hbm if far else vm for _, far in ins.values()],
        out_specs=[hbm if far else vm for _, far in outs.values()],
        scratch_shapes=list(scratch.values()),
        compiler_params=pltpu.CompilerParams(
            collective_id=collective_id, has_side_effects=True, vmem_limit_bytes=vmem_bytes
        ),
    )(*(value for value, _ in ins.values()))
    return dict(zip(outs, results, strict=True))


def first_stage(G, R, Q, H, dh, ins, collective_id):
    T, D = ins["x"].shape
    n = G * R
    S = n * T
    heads = H // G
    C = heads * dh
    enc_rows = ins["small"].shape[1] - 8
    part = D // n // Q
    block = (pieces, T // pieces, D)
    far_ins, far_outs = ("w_mine", "wide_mine", "cot"), ("cot_all",)
    outs = {
        "att": (G, T, C),
        "rows": (G, T, C),
        "q": (heads, G * T, 2 * dh),
        "kv": (heads, S, 2 * dh),
        "lse": (G, 8, T),
        "w": (n, Q, part, 3 * C),
        "own": (G * T, D),
        "small_all": ins["small"].shape,
        "ckv": (n, 1, enc_rows, 2 * D),
        "gain": (1, D),
        "after": (T, D),
        "middle": (T, D),
        "n3": (T, D),
        "cq": (T, D),
        "cflat": (T, D),
        "probs": (H, n * enc_rows, T),
        "wide": (n, Q, 3, part, D),
        "cot_all": (n,) + block,
    }
    scratch = {
        "x_buf": pltpu.VMEM((n,) + block, F32),
        "unit": pltpu.VMEM((R * T, D), F32),
        "strip": pltpu.VMEM((heads, 2 * R * T, T), F32),
        "x_sems": chain_sems(G, R, pieces),
        "cot_sems": chain_sems(G, R, pieces),
        "cot_own_sem": pltpu.SemaphoreType.DMA,
        "w_sems": spread_sems(G, R, Q),
        "wide_sems": spread_sems(G, R, Q),
        "att_sems": lane_sems(G),
        "small_sems": deal_sems(n),
        "ckv_scratch": tuple(reduce_scratch(G, R, 1, (enc_rows, 2 * D))),
        "ckv_chain_sems": chain_sems(G, R, 1),
    }
    return call_stage(
        functools.partial(first_kernel, G, R, Q, H, dh),
        {name: (value, name in far_ins) for name, value in ins.items()},
        {name: (shape, name in far_outs) for name, shape in outs.items()},
        scratch,
        collective_id,
    )


class Reduce:
    def __init__(self, G, R, parts, pool, inbox, sems, mode="near"):
        self.G, self.parts, self.pool, self.inbox, self.sems = G, parts, pool, inbox, sems
        self.pieces = parts.shape[2]
        self.rep, self.f, self.g, self.r = my_place(R)
        self.stride = R
        self.R = R if pool is not None else 1
        self.mine = self.r if pool is not None else 0
        self.groups = group_peers(self.rep, self.g, self.r, G, R)
        orders = []
        for g in range(G):
            due = {o: o + g if o > g else (G - 1 - o) + (G - 1 - g) for o in range(G) if o != g}
            if mode == "far":
                due = {o: G - 1 - o + g if o > g else o + G - 1 - g for o in due}
            held = [o for o in due if (g > 0 if o > g else g < G - 1)]
            orders.append((sorted(held, key=lambda o: due[o]) + [-1] * G)[: G - 1])
        self.orders = orders
        self.far_first = [sorted(range(G), key=lambda o: -abs(o - i)) for i in range(G)]

    def group_copy(self, o, j, p):
        other = lax.rem(self.r + j, self.R)
        return remote(
            self.parts.at[o, other, p],
            self.pool.at[j - 1, o, p],
            self.sems[0].at[j - 1, o, p],
            self.sems[1].at[j - 1, o, p],
            self.groups[j - 1],
        )

    def lane_copy(self, o, p):
        right = o > self.g
        to = jnp.where(right, self.g + 1, self.g - 1)
        last_left = jnp.logical_and(jnp.logical_not(right), to == o)
        slot = jnp.where(last_left, self.G, o)
        part = self.parts.at[o, self.mine, p]
        peer = (self.rep, to * self.stride + self.r)
        return remote(part, self.inbox.at[slot, p], self.sems[2].at[o, p], self.sems[3].at[slot, p], peer)

    def inbox_wait(self, slot, p):
        remote(
            self.parts.at[0, self.mine, p],
            self.inbox.at[slot, p],
            self.sems[2].at[0, p],
            self.sems[3].at[slot, p],
            (self.rep, self.f),
        ).wait_recv()

    def offer(self, o):
        for p in range(self.pieces):
            for j in range(1, self.R):
                self.group_copy(o, j, p).start()

    def pooled(self, o):
        first = jnp.logical_or(
            jnp.logical_and(o > self.g, self.g == 0),
            jnp.logical_and(o < self.g, self.g == self.G - 1),
        )
        for p in range(self.pieces):
            for j in range(1, self.R):
                self.group_copy(o, j, p).wait_recv()
            if self.R > 1:
                total = self.parts[o, self.mine, p]
                for j in range(1, self.R):
                    total = total + self.pool[j - 1, o, p]
                self.parts[o, self.mine, p] = total

            @pl.when(first)
            def _():
                self.lane_copy(o, p).start()

    def hand_on(self, index):
        o = lookup(self.orders, self.g, index)

        @pl.when(o >= 0)
        def _():
            for p in range(self.pieces):
                self.inbox_wait(o, p)
                self.parts[o, self.mine, p] += self.inbox[o, p]
                self.lane_copy(o, p).start()

    def collect(self, out):
        for p in range(self.pieces):
            out[p] = self.parts[self.g, self.mine, p]

        for cond, slot in ((self.g > 0, self.g), (self.g < self.G - 1, self.G)):

            @pl.when(cond)
            def _():
                for p in range(self.pieces):
                    self.inbox_wait(slot, p)
                    out[p] += self.inbox[slot, p]

    def finish(self):
        for o in range(self.G):
            for p in range(self.pieces):
                for j in range(1, self.R):
                    self.group_copy(o, j, p).wait_send()

            @pl.when(self.g != o)
            def _():
                for p in range(self.pieces):
                    self.lane_copy(o, p).wait_send()


def reduce_scratch(G, R, pieces, block):
    sem = pltpu.SemaphoreType.DMA
    block = (pieces, block[0] // pieces) + block[1:]
    return [
        pltpu.VMEM((G, R) + block, F32),
        pltpu.VMEM((R - 1, G) + block if R > 1 else (8, 128), F32),
        pltpu.VMEM((G + 1,) + block, F32),
        (sem((max(R - 1, 1), G, pieces)), sem((max(R - 1, 1), G, pieces)), sem((G, pieces)), sem((G + 1, pieces))),
    ]


def ffn_kernel(
    G,
    R,
    n3_ref,
    cot_ref,
    gate_ref,
    up_ref,
    down_ref,
    dn3_ref,
    out_ref,
    d_gate_ref,
    d_up_ref,
    d_down_ref,
    gate_parts,
    up_parts,
    down_parts,
    gate_in,
    up_in,
    down_in,
    rep_sems,
    n3_buf,
    n3_high,
    n3_low,
    inner_high,
    inner_low,
    grads_high,
    grads_low,
    wide_high,
    wide_low,
    tall_high,
    tall_low,
    dn3_parts,
    dn3_pool,
    dn3_inbox,
    dn3_sems,
    n3_sems,
):
    rep, f, g, r = my_place(R)
    T, D = n3_ref.shape
    F = gate_ref.shape[1]
    rows_each = R * T
    block = (R, pieces, T // pieces, D)
    Q = gate_parts.shape[0]
    greet(lane_peers(rep, g, r, G, R) + group_peers(rep, g, r, G, R) + everyone(rep, f, 1, Q))
    sums = [
        (gate_parts, gate_in, d_gate_ref),
        (up_parts, up_in, d_up_ref),
        (down_parts, down_in, d_down_ref),
    ]

    def rep_copy(a, j):
        to = lax.rem(rep + j, Q)
        sems = rep_sems[0].at[a, j - 1], rep_sems[1].at[a, j - 1]
        return remote(sums[a][0].at[to], sums[a][1].at[j - 1], *sems, (to, f))

    def to_replicas(a, value):
        sums[a][0][...] = value.reshape(sums[a][0].shape)
        for j in range(1, Q):
            rep_copy(a, j).start()

    chain = Chain(G, R, n3_buf, n3_sems)
    d_three = Reduce(G, R, dn3_parts, dn3_pool, dn3_inbox, dn3_sems)
    n3_buf[f] = n3_ref[...].reshape(pieces, T // pieces, D)
    chain.start()
    for index, ref in enumerate((gate_ref, up_ref, down_ref)):
        high, low = halves(ref[...])
        span = slice(index * F, (index + 1) * F)
        wide = index < 2
        wide_high[:, span] = high if wide else high.T
        wide_low[:, span] = low if wide else low.T
        tall_high[span, :] = high.T if wide else high
        tall_low[span, :] = low.T if wide else low

    @pl.loop(0, G)
    def _(t):
        src = chain.arrive(t)
        rows = pl.ds(pl.multiple_of(src * rows_each, rows_each), rows_each)
        n3 = halves(n3_buf[pl.ds(src * R, R)].reshape(rows_each, D))
        n3_high[rows, :], n3_low[rows, :] = n3
        pre = dot3(n3, (wide_high[:, : 2 * F], wide_low[:, : 2 * F]))
        gate_pre, up_pre = pre[:, :F], pre[:, F:]
        gelu_out, gelu_slope = gelu_parts(gate_pre)
        inner = halves(gelu_out * up_pre)
        inner_high[rows, :], inner_low[rows, :] = inner
        cot = halves(cot_ref[pl.ds(src * R, R)].reshape(rows_each, D))
        grad_inner = dot3(cot, (wide_high[:, 2 * F :], wide_low[:, 2 * F :]))
        grads = halves(
            jnp.concatenate([grad_inner * up_pre * gelu_slope, grad_inner * gelu_out], axis=1)
        )
        grads_high[rows, :], grads_low[rows, :] = grads
        dn3 = dot3(grads, (tall_high[: 2 * F, :], tall_low[: 2 * F, :]))
        dn3_parts[src] = dn3.reshape(block)
        d_three.offer(src)
        out = dot3(inner, (tall_high[2 * F :, :], tall_low[2 * F :, :]))
        out_ref[src] = out.reshape(block)
        d_three.pooled(src)

    S = G * rows_each
    tn = (((0,), (0,)), ((), ()))
    n3 = (n3_high[...], n3_low[...])
    to_replicas(0, dot3(n3, (grads_high[:, :F], grads_low[:, :F]), tn))
    d_three.hand_on(0)
    to_replicas(1, dot3(n3, (grads_high[:, F:], grads_low[:, F:]), tn))
    d_three.hand_on(1)
    cot = halves(cot_ref[...].reshape(S, D))
    to_replicas(2, dot3((inner_high[...], inner_low[...]), cot, tn))
    for index in range(2, G - 1):
        d_three.hand_on(index)
    d_three.collect(dn3_ref)
    for a in range(3):
        total = sums[a][0][rep]
        for j in range(1, Q):
            rep_copy(a, j).wait_recv()
            total = total + sums[a][1][j - 1]
        sums[a][2][...] = total
        for j in range(1, Q):
            rep_copy(a, j).wait_send()
    chain.finish()
    d_three.finish()


def ffn_stage(G, R, Q, n3, cot, gate, up, down, collective_id):
    T, D = n3.shape
    F = gate.shape[1]
    n = G * R
    S = n * T
    vm = pl.BlockSpec(memory_space=pltpu.VMEM)
    block = (pieces, T // pieces, D)
    shape = lambda *dims: jax.ShapeDtypeStruct(dims, F32)
    dn3, out, d_gate, d_up, d_down = pl.pallas_call(
        functools.partial(ffn_kernel, G, R),
        out_shape=[
            shape(*block),
            shape(G, R, *block),
            shape(D // Q, F),
            shape(D // Q, F),
            shape(F // Q, D),
        ],
        in_specs=[vm] * 5,
        out_specs=[vm] * 5,
        scratch_shapes=[
            pltpu.VMEM((Q, D // Q, F), F32),
            pltpu.VMEM((Q, D // Q, F), F32),
            pltpu.VMEM((Q, F // Q, D), F32),
            pltpu.VMEM((Q - 1, D // Q, F), F32),
            pltpu.VMEM((Q - 1, D // Q, F), F32),
            pltpu.VMEM((Q - 1, F // Q, D), F32),
            (pltpu.SemaphoreType.DMA((3, Q - 1)), pltpu.SemaphoreType.DMA((3, Q - 1))),
            pltpu.VMEM((n,) + block, F32),
            pltpu.VMEM((S, D), BF16),
            pltpu.VMEM((S, D), BF16),
            pltpu.VMEM((S, F), BF16),
            pltpu.VMEM((S, F), BF16),
            pltpu.VMEM((S, 2 * F), BF16),
            pltpu.VMEM((S, 2 * F), BF16),
            pltpu.VMEM((D, 3 * F), BF16),
            pltpu.VMEM((D, 3 * F), BF16),
            pltpu.VMEM((3 * F, D), BF16),
            pltpu.VMEM((3 * F, D), BF16),
        ]
        + reduce_scratch(G, R, pieces, (T, D))
        + [chain_sems(G, R, pieces)],
        compiler_params=pltpu.CompilerParams(
            collective_id=collective_id, has_side_effects=True, vmem_limit_bytes=vmem_bytes
        ),
    )(n3, cot, gate, up, down)
    return dn3.reshape(T, D), out, d_gate, d_up, d_down


class Fold:
    def __init__(self, G, R, Q, scratch, out, summed):
        self.G, self.R, self.Q = G, R, Q
        self.parts, self.pool, self.rep_in, self.lane_out, self.lane_in, self.sems = scratch
        self.A = self.parts.shape[0]
        self.out, self.summed = out, summed
        self.rep, self.f, self.g, self.r = my_place(R)
        self.groups = group_peers(self.rep, self.g, self.r, G, R)
        self.lanes = lane_peers(self.rep, self.g, self.r, G, R)
        self.to_rep = [lax.rem(self.rep + j, Q) for j in range(1, Q)]
        if G * R == 1:
            self.g = self.r = 0

    def group_copy(self, a, o, j):
        return remote(
            self.parts.at[a, o, lax.rem(self.r + j, self.R)],
            self.pool.at[j - 1, a, o],
            self.sems[0].at[j - 1, a, o],
            self.sems[1].at[j - 1, a, o],
            self.groups[j - 1],
        )

    def rep_copy(self, o, j):
        return remote(
            self.parts.at[:, o, self.r, self.to_rep[j - 1]],
            self.rep_in.at[j - 1, o],
            self.sems[2].at[j - 1, o],
            self.sems[3].at[j - 1, o],
            (self.to_rep[j - 1], self.f),
        )

    def lane_copy(self, k):
        return remote(
            self.lane_out.at[k],
            self.lane_in.at[k - 1],
            self.sems[4].at[k - 1],
            self.sems[5].at[k - 1],
            self.lanes[k - 1],
        )

    def back_copy(self, j):
        part = self.out.at[self.rep]
        return remote(
            part, part, self.sems[6].at[j - 1], self.sems[7].at[j - 1], (self.to_rep[j - 1], self.f)
        )

    def to_group(self, a):
        for o in range(self.G):
            for j in range(1, self.R):
                self.group_copy(a, o, j).start()

    def to_replicas(self):
        for o in range(self.G):
            for a in range(self.A):
                for j in range(1, self.R):
                    self.group_copy(a, o, j).wait_recv()
                    self.parts[a, o, self.r] += self.pool[j - 1, a, o]
            for j in range(1, self.Q):
                self.rep_copy(o, j).start()

    def to_owner(self):
        for k in range(self.G - 1, -1, -1):
            o = lax.rem(self.g + k, self.G)
            for j in range(1, self.Q):
                self.rep_wait(o, j)
            total = self.parts[:, o, self.r, self.rep]
            for j in range(1, self.Q):
                total = total + self.rep_in[j - 1, o]
            self.lane_out[k] = total
            if k > 0:
                self.lane_copy(k).start()

    def rep_wait(self, o, j):
        self.rep_copy(o, j).wait_recv()

    def to_everyone(self):
        if self.summed:
            total = self.lane_out[0]
            for k in range(1, self.G):
                self.lane_copy(k).wait_recv()
                total = total + self.lane_in[k - 1]
            self.out[self.rep] = total
        else:
            self.out[self.rep, self.g] = self.lane_out[0]
            for k in range(1, self.G):
                self.lane_copy(k).wait_recv()
                self.out[self.rep, lax.rem(self.g + self.G - k, self.G)] = self.lane_in[k - 1]
        for j in range(1, self.Q):
            self.back_copy(j).start()

    def finish(self):
        for j in range(1, self.Q):
            self.back_copy(j).wait()
        for o in range(self.G):
            for a in range(self.A):
                for j in range(1, self.R):
                    self.group_copy(a, o, j).wait_send()
            for j in range(1, self.Q):
                self.rep_copy(o, j).wait_send()
        for k in range(1, self.G):
            self.lane_copy(k).wait_send()


def fold_scratch(A, G, R, Q, m, W):
    sem = pltpu.SemaphoreType.DMA
    some, lanes = max(R - 1, 1), max(G - 1, 1)
    return (
        pltpu.VMEM((A, G, R, Q, m, W), F32),
        pltpu.VMEM((some, A, G, Q, m, W) if R > 1 else (1, 1, 1, 1, 8, 128), F32),
        pltpu.VMEM((Q - 1, G, A, m, W), F32),
        pltpu.VMEM((G, A, m, W), F32),
        pltpu.VMEM((lanes, A, m, W), F32),
        (
            sem((some, A, G)),
            sem((some, A, G)),
            sem((Q - 1, G)),
            sem((Q - 1, G)),
            sem((lanes,)),
            sem((lanes,)),
            sem((Q - 1,)),
            sem((Q - 1,)),
        ),
    )


def back_kernel(G, R, Q, H, dh, buckets, fused, names, *refs):
    m = named(names, refs)
    rep, f, g, r = my_place(R)
    n = G * R
    heads = H // G
    T, D = m["x"].shape
    C = heads * dh
    Dn = D // n
    groups = group_peers(rep, g, r, G, R)
    reps = [(lax.rem(rep + j, Q), f) for j in range(1, Q)]
    greet(everyone(rep, f, n, Q))

    ffn_names = ("d_gate", "d_up", "d_down")

    def ffn_own(a):
        name = ffn_names[a]
        return pltpu.make_async_copy(m[name + "_in"], m[name].at[rep], m["ffn_sems"][2].at[a])

    def ffn_copy(a, j):
        name = ffn_names[a]
        sems = m["ffn_sems"][0].at[a, j - 1], m["ffn_sems"][1].at[a, j - 1]
        return remote(m[name + "_in"], m[name].at[rep], *sems, reps[j - 1])

    for a in range(3):
        for j in range(1, Q):
            ffn_copy(a, j).start()
        ffn_own(a).start()
    out_sum = Reduce(G, R, *m["out_scratch"], mode="far") if fused else None
    ckv_sum = Reduce(G, R, *m["ckv_scratch"])
    du_parts, _, du_inbox, du_sems = m["du_scratch"]
    du_sum = Reduce(G, R, du_parts, None, du_inbox, du_sems)
    ckv_chain = Chain(G, R, m["ckv_all"], m["ckv_chain_sems"])
    wides = [Fold(G, R, Q, m[f"wide_scratch{a}"], m[f"d_wide{a}"], True) for a in range(3)] if fused else []
    d_w = Fold(G, R, Q, m["dw_scratch"], m["d_w"], False)
    d_cw = Fold(1, 1, Q, m["cw_scratch"], m["d_ckv_w"], True)

    def load(a):
        return pltpu.make_async_copy(m["wide"].at[:, :, a], m["weight"], m["load_sem"])

    def weight():
        return m["weight"][...].reshape(D, D)

    def give(a, value):
        if fused:
            wides[a].parts[0] = value.reshape(wides[a].parts.shape[1:])
            wides[a].to_group(0)
        else:
            m[f"d_wide{a}"][...] = value

    load(2).start()
    if fused:
        load_out = pltpu.make_async_copy(m["out_parts"], out_sum.parts, m["out_sem"])
        load_out.start()

    unit_three, scale_three = unit_of(m["middle"][...])
    dn3 = m["dn3"][...]
    d_gain = jnp.sum(dn3 * unit_three, axis=0, keepdims=True)
    m["d_middle"][...] = m["cot"][...] + unit_backward(dn3 * m["gain"][...], unit_three, scale_three)
    if fused:
        load_out.wait()
        for o in range(G):
            out_sum.offer(o)
    load(2).wait()
    m["d_after"][...] = mm_nt(m["d_middle"][...], weight())
    load(1).start()
    enc_rows = ckv_sum.parts.shape[3]
    enc_count = n * enc_rows
    for h in range(0, H, 2):
        outs = []
        for a in (h, h + 1):
            span = slice(2 * a * dh, 2 * (a + 1) * dh)
            ckv = m["ckv"][:, 0, :, span].reshape(enc_count, 2 * dh)
            probs = m["probs"][a]
            grad = beside(m["d_after"][:, a * dh : (a + 1) * dh], 1)
            d_probs = mm_nt(ckv, grad)
            delta = jnp.sum(probs * d_probs, axis=0, keepdims=True)
            d_scores = probs * (d_probs - delta)
            cq = beside(m["cq"][:, a * dh : (a + 1) * dh], 0)
            d_ckv = mm(jnp.concatenate([d_scores, probs], axis=1), jnp.concatenate([cq, grad], axis=0))
            ckv_sum.parts[:, :, :, :, span] = d_ckv.reshape(G, R, 1, enc_rows, 2 * dh)
            outs.append(mm_tn(ckv, d_scores)[:dh, :].T)
        m["d_cq"][:, h * dh : (h + 2) * dh] = jnp.concatenate(outs, axis=1)
    for o in range(G):
        ckv_sum.offer(o)
    if fused:
        out_sum.pooled(lookup(out_sum.far_first, g, 0))
    give(2, mm_tn(m["cflat"][...], m["d_middle"][...]))
    load(1).wait()
    unit_two, scale_two = unit_of(m["after"][...])
    d_unit = mm_nt(m["d_cq"][...], weight())
    load(0).start()
    m["d_after"][...] = m["d_middle"][...] + unit_backward(d_unit, unit_two, scale_two)
    for o in range(G):
        ckv_sum.pooled(o)
    if fused:
        wides[2].to_replicas()
    give(1, mm_tn(unit_two, m["d_cq"][...]))
    load(0).wait()
    d_att = mm_nt(m["d_after"][...], weight())
    for i in range(G):
        m["d_att"][i] = d_att[:, i * C : (i + 1) * C]
        lane_send(G, R, i, m["d_att"], m["grad"], m["att_sems"])
    if fused:
        for t in range(1, G):
            out_sum.pooled(lookup(out_sum.far_first, g, t))
        wides[1].to_replicas()
    attended = jnp.concatenate([m["rows"][i] for i in range(G)], axis=1)
    give(0, mm_tn(attended, m["d_after"][...]))
    if fused:
        out_sum.hand_on(0)
    make_strips(R, heads, T, m["vec"], m["strip"])
    m["near"][...] = jnp.zeros_like(m["near"])
    m["far"][...] = jnp.zeros_like(m["far"])
    ckv_sum.hand_on(0)
    if fused:
        wides[0].to_replicas()
    ckv_sum.hand_on(1)
    lane_wait(G, R, m["d_att"], m["grad"], m["att_sems"])

    def dkv_copy(i, j):
        return remote(
            m["dkv_parts"].at[i, lax.rem(r + j, R)],
            m["dkv_pool"].at[j - 1, i],
            m["dkv_send"].at[j - 1, i],
            m["dkv_recv"].at[j - 1, i],
            groups[j - 1],
        )

    dqkv = m["dqkv"]

    def own_gradient(i):
        for j in range(1, R):
            dkv_copy(i, j).wait_recv()
        dkv = m["dkv_parts"][i, r]
        for j in range(1, R):
            dkv = dkv + m["dkv_pool"][j - 1, i]
        dqkv[i, :, : 2 * C] = dkv

    for i in range(G - 1, -1, -1):
        L = R * (i + 1) * T
        grad = m["grad"][i]
        prod_t = (grad * m["att"][i]).T
        dqs = []
        for h in range(heads):
            scores = strip_scores(R, T, i, r, h, L, m["kv"], m["q"], m["strip"])
            probs = jnp.exp(scores - m["lse"][i, h : h + 1, :])
            grad_h = beside(grad[:, h * dh : (h + 1) * dh], 1)
            delta = jnp.sum(prod_t[h * dh : (h + 1) * dh, :], axis=0, keepdims=True)
            d_scores = probs * (mm_nt(m["kv"][h, :L, :], grad_h) - delta)
            q_h = m["q"][h, i * T : (i + 1) * T, :]
            dkv = mm(
                jnp.concatenate([d_scores, probs], axis=1), jnp.concatenate([q_h, grad_h], axis=0)
            )
            if i == G - 1:
                m["dkv"][h] = dkv
            else:
                m["dkv"][h, :L, :] += dkv
            dqs.append(mm_tn(m["kv"][h, :L, :], d_scores)[:dh, :].T)
            skip = 1 if i == 0 else 0
            width = (R + 1 - skip) * T
            m["near"][h, skip * T :, :] += d_scores[L - width :, :]
            if width < L:
                m["far"][h : h + 1, :] += jnp.sum(d_scores[: L - width, :], axis=0, keepdims=True)
        m["dqkv"][i, :, 2 * C :] = jnp.concatenate(dqs, axis=1)
        for b in range(R):
            rows = slice((i * R + b) * T, (i * R + b + 1) * T)
            m["dkv_parts"][i, b] = jnp.concatenate([m["dkv"][h, rows, :] for h in range(heads)], axis=1)
        for j in range(1, R):
            dkv_copy(i, j).start()
        if i < G - 1:
            own_gradient(i + 1)
        if fused and i > 1:
            out_sum.hand_on(G - i)
        if i == 3:
            ckv_sum.hand_on(2)
        if i == 2:
            ckv_sum.collect(m["ckv_all"].at[f])
            ckv_chain.start()
        if i == 1:
            ckv_chain.arrive(0)
            ckv_chain.arrive(1)
    own_gradient(0)
    if fused:
        wides[2].to_owner()
    w = m["w"][...].reshape(D, 3 * C)
    for i in range(G):
        du_parts[i, 0] = mm_nt(dqkv[i], w).reshape(du_parts.shape[2:])
        du_sum.pooled(i)
    d_w.parts[0] = mm_tn(m["own"][...], dqkv[...].reshape(G * T, 3 * C)).reshape(d_w.parts.shape[1:])
    d_w.to_group(0)
    if fused:
        wides[1].to_owner()
        wides[2].to_everyone()

    ids = jnp.broadcast_to(m["ids"][0:1, :], (2 * T, 3 * T))
    ids = pltpu.roll(ids, 0, 1, stride=1, stride_axis=0)[:, :T]
    each = buckets // n
    tiny_parts = m["tiny_parts"]
    tiny_parts[...] = jnp.zeros_like(tiny_parts)
    for h in range(heads):
        pair = m["near"][h, pl.ds(pl.multiple_of(r * T, T), 2 * T), :]
        far = m["far"][h : h + 1, :]
        for idx in range(R - 1):
            block = jnp.sum(m["near"][h, idx * T : (idx + 1) * T, :], axis=0, keepdims=True)
            far = far + jnp.where(idx < r, block, 0.0)
        for b in range(buckets):
            part = jnp.sum(jnp.where(ids == b, pair, 0.0), axis=0, keepdims=True)
            if b == buckets - 1:
                part = part + far
            row = h * each + b % each
            tiny_parts[b // each, row : row + 1, :] = part
    last = heads * each
    for o in range(n):
        tiny_parts[o, last : last + 1, :Dn] = d_gain[:, o * Dn : (o + 1) * Dn]
    tiny = Deal(n, tiny_parts, m["tiny_in"], m["tiny_sems"])
    tiny.start()

    du_sum.hand_on(0)
    d_w.to_replicas()
    ckv_chain.arrive(2)
    ckv_chain.arrive(3)
    if fused:
        wides[0].to_owner()
    d_w.to_owner()
    if fused:
        wides[1].to_everyone()
    du_sum.hand_on(1)
    d_ckv = m["ckv_all"][...].reshape(enc_count, 2 * D)
    m["enc_parts"][...] = mm_nt(d_ckv, m["ckv_w"][...]).reshape(m["enc_parts"].shape)
    d_enc = Deal(n, m["enc_parts"], m["d_enc"], m["enc_sems"])
    d_enc.start()
    enc_cols = m["small_all"][:, :enc_rows, :].reshape(enc_count, Dn)
    d_cw.parts[0, 0, 0] = mm_tn(enc_cols, d_ckv).reshape(d_cw.parts.shape[3:])
    d_cw.to_replicas()
    d_w.to_everyone()
    if fused:
        wides[0].to_everyone()
    for index in range(2, G - 1):
        du_sum.hand_on(index)
    tiny.arrive()
    for s in range(G):
        total = m["tiny_in"][s * R]
        for j in range(1, R):
            total = total + m["tiny_in"][s * R + j]
        m["tiny"][rep, s] = total

    def tiny_copy(j):
        part = m["tiny"].at[rep]
        return remote(part, part, m["tiny_rep_send"].at[j - 1], m["tiny_rep_recv"].at[j - 1], reps[j - 1])

    for j in range(1, Q):
        tiny_copy(j).start()
    d_cw.to_owner()
    d_cw.to_everyone()
    if fused:
        out_sum.collect(m["out"])
        m["out"][...] += m["middle"][...].reshape(m["out"].shape)
    du_sum.collect(m["du"])
    unit_one, scale_one = unit_of(m["x"][...])
    d_unit = m["du"][...].reshape(T, D)
    m["d_x"][...] = m["d_after"][...] + unit_backward(d_unit, unit_one, scale_one)

    d_enc.arrive()
    for a in range(3):
        ffn_own(a).wait()
        for j in range(1, Q):
            ffn_copy(a, j).wait()
    for j in range(1, Q):
        tiny_copy(j).wait()
    tiny.finish()
    d_enc.finish()
    for i in range(G):
        for j in range(1, R):
            dkv_copy(i, j).wait_send()
    if fused:
        out_sum.finish()
        for fold in wides:
            fold.finish()
    ckv_sum.finish()
    du_sum.finish()
    ckv_chain.finish()
    d_w.finish()
    d_cw.finish()


def back_stage(G, R, Q, H, dh, buckets, ins, collective_id):
    T, D = ins["x"].shape
    n = G * R
    S = n * T
    heads = H // G
    C = heads * dh
    Dn = D // n
    part = Dn // Q
    enc_rows = ins["ckv"].shape[2]
    block = (pieces, T // pieces, D)
    tiny_rows = -(-(heads * (buckets // n) + 1) // 8) * 8
    sem = pltpu.SemaphoreType.DMA
    some = max(R - 1, 1)
    fused = R <= 2
    far_ins = ("wide", "out_parts", "d_gate_in", "d_up_in", "d_down_in")
    far_outs = ("d_gate", "d_up", "d_down")
    outs = {
        "d_gate": (Q,) + ins["d_gate_in"].shape,
        "d_up": (Q,) + ins["d_up_in"].shape,
        "d_down": (Q,) + ins["d_down_in"].shape,
        "d_x": (T, D),
        "out": block,
        "d_w": (Q, G, 1, part, 3 * C),
        "d_wide0": (Q, 1, part, D) if fused else (D, D),
        "d_wide1": (Q, 1, part, D) if fused else (D, D),
        "d_wide2": (Q, 1, part, D) if fused else (D, D),
        "d_ckv_w": (Q, 1, part, 2 * D),
        "d_enc": (n, enc_rows, Dn),
        "tiny": (Q, G, tiny_rows, T),
    }
    scratch = {
        "d_middle": pltpu.VMEM((T, D), F32),
        "d_cq": pltpu.VMEM((T, D), F32),
        "d_after": pltpu.VMEM((T, D), F32),
        "d_att": pltpu.VMEM((G, T, C), F32),
        "weight": pltpu.VMEM((n, Q, part, D), F32),
        "load_sem": sem,
        "ffn_sems": (sem((3, Q - 1)), sem((3, Q - 1)), sem((3,))),
        "out_sem": sem,
        "strip": pltpu.VMEM((heads, 2 * R * T, T), F32),
        "near": pltpu.VMEM((heads, (R + 1) * T, T), F32),
        "far": pltpu.VMEM((8, T), F32),
        "dkv": pltpu.VMEM((heads, S, 2 * dh), F32),
        "dqkv": pltpu.VMEM((G, T, 3 * C), F32),
        "grad": pltpu.VMEM((G, T, C), F32),
        "dkv_parts": pltpu.VMEM((G, R, T, 2 * C), F32),
        "dkv_pool": pltpu.VMEM((some, G, T, 2 * C), F32),
        "dkv_send": sem((some, G)),
        "dkv_recv": sem((some, G)),
        "tiny_parts": pltpu.VMEM((n, tiny_rows, T), F32),
        "tiny_in": pltpu.VMEM((n, tiny_rows, T), F32),
        "tiny_sems": deal_sems(n),
        "tiny_rep_send": sem((Q - 1,)),
        "tiny_rep_recv": sem((Q - 1,)),
        "enc_parts": pltpu.VMEM((n, enc_rows, Dn), F32),
        "enc_sems": deal_sems(n),
        "ckv_all": pltpu.VMEM((n, 1, enc_rows, 2 * D), F32),
        "ckv_chain_sems": chain_sems(G, R, 1),
        "att_sems": lane_sems(G),
        "du": pltpu.VMEM(block, F32),
        "ckv_scratch": tuple(reduce_scratch(G, R, 1, (enc_rows, 2 * D))),
        "du_scratch": tuple(reduce_scratch(G, 1, pieces, (T, D))),
        "dw_scratch": fold_scratch(1, G, R, Q, part, 3 * C),
        "cw_scratch": fold_scratch(1, 1, 1, Q, part, 2 * D),
    }
    if fused:
        for a in range(3):
            scratch[f"wide_scratch{a}"] = fold_scratch(1, G, R, Q, part, D)
        scratch["out_scratch"] = tuple(reduce_scratch(G, R, pieces, (T, D)))
    results = call_stage(
        functools.partial(back_kernel, G, R, Q, H, dh, buckets, fused),
        {name: (value, name in far_ins) for name, value in ins.items()},
        {name: (shape, name in far_outs) for name, shape in outs.items()},
        scratch,
        collective_id,
    )
    if not fused:
        out = scatter(G, R, ins["out_parts"].reshape(G, R, T, D), True, True, collective_id + 1)
        results["out"] = out + ins["middle"]
        total = jnp.concatenate([results[f"d_wide{a}"] for a in range(3)], axis=1)
        total = lax.psum_scatter(total, "fsdp", scatter_dimension=0, tiled=True)
        total = lax.psum(total, "rep")
        for a in range(3):
            results[f"d_wide{a}"] = total[:, a * D : (a + 1) * D]
    return results


def shards(
    n,
    inputs,
    encoder,
    self_gain,
    cross_gain,
    ffn_gain,
    self_query,
    self_key,
    self_value,
    self_output,
    position_bias,
    bucket_table,
    cross_query,
    cross_key,
    cross_value,
    cross_output,
    ffn_gate,
    ffn_up,
    ffn_down,
    cotangent,
):
    x = inputs[0]
    enc = encoder[0]
    cot = cotangent[0]
    T, D = x.shape
    buckets, H = position_bias.shape
    dh = D // H
    G = math.gcd(H, n)
    R = n // G
    heads = H // G
    C = heads * dh
    Dn = D // n
    enc_local = enc.shape[0]
    f = lax.axis_index("fsdp")
    g, r = f // R, lax.rem(f, R)

    Q = lax.axis_size("rep")
    q = lax.axis_index("rep")
    part = Dn // Q

    def fold(w, gain):
        return w * gain[:, None]

    def mine(w):
        return lax.dynamic_slice_in_dim(w, q * part, part, 0)

    def by_group(w):
        return fold(mine(w), mine(self_gain)).reshape(part, G, heads, dh)

    w_mine = jnp.concatenate([by_group(self_key), by_group(self_value)], axis=3)
    w_mine = jnp.concatenate(
        [w_mine.reshape(part, G, 2 * C), by_group(self_query).reshape(part, G, C)], axis=2
    )
    w_mine = jnp.transpose(w_mine, (1, 0, 2))
    wide_mine = jnp.stack(
        [mine(self_output), fold(mine(cross_query), mine(cross_gain)), mine(cross_output)]
    )
    dist = jnp.concatenate(
        [jnp.arange(T, 2 * T), jnp.full((T,), -1), jnp.arange(T)]
    )
    row_bucket = jnp.concatenate(
        [bucket_table[T : 2 * T], jnp.zeros((T,), jnp.int32), bucket_table[:T]]
    )
    onehot = (row_bucket[:, None] == jnp.arange(buckets, dtype=jnp.int32)[None, :]).astype(F32)
    vec = jnp.dot(
        onehot, position_bias - position_bias[buckets - 1 :], precision=lax.Precision.HIGHEST
    )
    vec = jnp.where(dist[:, None] < 0, masked_score, vec)
    vec = lax.dynamic_slice_in_dim(vec.T, g * heads, heads, 0)
    vec = jnp.pad(vec, ((0, 8 - heads), (0, 0)))
    ids = jnp.broadcast_to(
        jnp.where(dist < 0, -1, row_bucket).astype(F32)[None, :], (8, 3 * T)
    )

    small = jnp.transpose(enc.reshape(enc_local, n, Dn), (1, 0, 2))
    small = jnp.concatenate([small, jnp.broadcast_to(ffn_gain, (n, 8, Dn))], axis=1)
    ckv_w = jnp.concatenate([w.reshape(Dn, H, dh) for w in (cross_key, cross_value)], axis=2)
    ckv_w = ckv_w.reshape(Dn, 2 * D)

    ins = {
        "x": x,
        "vec": vec,
        "small": small,
        "ckv_w": ckv_w,
        "w_mine": w_mine,
        "wide_mine": wide_mine,
        "cot": cot.reshape(pieces, T // pieces, D),
    }
    first = first_stage(G, R, Q, H, dh, ins, 1)
    dn3, out_parts, d_gate, d_up, d_down = ffn_stage(
        G, R, Q, first["n3"], first["cot_all"], ffn_gate, ffn_up, ffn_down, 3
    )
    kept = ("rows", "att", "q", "kv", "lse", "w", "own", "small_all", "ckv", "gain", "after", "middle")
    ins = {name: first[name] for name in kept + ("cq", "cflat", "probs", "wide")}
    ins.update(x=x, vec=vec, ids=ids, ckv_w=ckv_w, cot=cot, dn3=dn3, out_parts=out_parts)
    ins.update(d_gate_in=d_gate, d_up_in=d_up, d_down_in=d_down)
    back = back_stage(G, R, Q, H, dh, buckets, ins, 5)

    d_gate, d_up = (back[name].reshape(ffn_gate.shape) for name in ("d_gate", "d_up"))
    d_down = back["d_down"].reshape(ffn_down.shape)
    out_rows = back["out"].reshape(T, D)
    d_x = back["d_x"]
    d_enc = jnp.transpose(back["d_enc"], (1, 0, 2)).reshape(enc_local, D)
    d_w = jnp.transpose(back["d_w"][:, :, 0], (0, 2, 1, 3)).reshape(Dn, G, 3 * C)
    dwq = d_w[:, :, 2 * C :].reshape(Dn, D)
    d_kv = d_w[:, :, : 2 * C].reshape(Dn, H, 2 * dh)
    dwk, dwv = d_kv[:, :, :dh].reshape(Dn, D), d_kv[:, :, dh:].reshape(Dn, D)
    dso, dcq, dco = (back[f"d_wide{a}"].reshape(Dn, D) for a in range(3))
    d_ckv_w = back["d_ckv_w"].reshape(Dn, H, 2 * dh)
    dck, dcv = d_ckv_w[:, :, :dh].reshape(Dn, D), d_ckv_w[:, :, dh:].reshape(Dn, D)
    each = buckets // n
    tiny = jnp.sum(back["tiny"], axis=0)
    grad_bias = jnp.sum(tiny[:, : heads * each, :], axis=2).reshape(G, heads, each)
    grad_bias = jnp.transpose(grad_bias, (2, 0, 1)).reshape(each, H)
    g_ffn = jnp.sum(tiny[:, heads * each, :Dn], axis=0)
    g_self = jnp.sum(dwq * self_query + dwk * self_key + dwv * self_value, axis=1)
    g_cross = jnp.sum(dcq * cross_query, axis=1)
    return (
        out_rows[None],
        d_x[None],
        d_enc[None],
        g_self,
        g_cross,
        g_ffn,
        fold(dwq, self_gain),
        fold(dwk, self_gain),
        fold(dwv, self_gain),
        dso,
        grad_bias,
        fold(dcq, cross_gain),
        dck,
        dcv,
        dco,
        d_gate,
        d_up,
        d_down,
    )


def solution(mesh):
    rows = P("rep", "fsdp", None)
    gain = P("fsdp")
    weight = P("fsdp", None)
    columns = P(None, "fsdp")
    args = (rows, rows, gain, gain, gain) + (weight,) * 4 + (P(), P()) + (weight,) * 4
    args += (columns, columns, weight, rows)
    outs = (rows, rows, rows, gain, gain, gain) + (weight,) * 9 + (columns, columns, weight)
    return jax.shard_map(
        functools.partial(shards, mesh.shape["fsdp"]),
        mesh=mesh,
        in_specs=args,
        out_specs=outs,
        check_vma=False,
    )
```

```python
import functools
import math
from types import SimpleNamespace

import jax
import jax.numpy as jnp
from jax import lax
from jax.experimental import pallas as pl
from jax.experimental.pallas import tpu as pltpu
from jax.sharding import PartitionSpec as P

HIGH = lax.Precision.HIGH
MESH = pl.DeviceIdType.MESH
F32 = jnp.float32
eps_norm = 1e-06
gelu_coef = math.sqrt(2.0 / math.pi)
masked_score = -1e30
vmem_bytes = 62 << 20
pieces = 2


def mm(a, b):
    return jnp.dot(a, b, precision=HIGH, preferred_element_type=F32)


def mm_tn(a, b):
    return lax.dot_general(
        a, b, (((0,), (0,)), ((), ())), precision=HIGH, preferred_element_type=F32
    )


def mm_nt(a, b):
    return lax.dot_general(
        a, b, (((1,), (1,)), ((), ())), precision=HIGH, preferred_element_type=F32
    )


BF16 = jnp.bfloat16


def halves(a):
    high = a.astype(BF16)
    return high, (a - high.astype(F32)).astype(BF16)


def dot3(a, b, dims=(((1,), (0,)), ((), ()))):
    def dot(x, y):
        return lax.dot_general(x, y, dims, preferred_element_type=F32)

    return dot(a[0], b[0]) + (dot(a[0], b[1]) + dot(a[1], b[0]))


def unit_of(rows):
    scale = lax.rsqrt(jnp.mean(rows * rows, axis=-1, keepdims=True) + eps_norm)
    return rows * scale, scale


def unit_backward(grad_unit, unit, scale):
    return scale * (grad_unit - unit * jnp.mean(grad_unit * unit, axis=-1, keepdims=True))


def gelu_parts(gate_pre):
    squared = gate_pre * gate_pre
    tangent = jnp.tanh(gelu_coef * (gate_pre + 0.044715 * squared * gate_pre))
    gelu_out = 0.5 * gate_pre * (1.0 + tangent)
    gelu_slope = 0.5 * (1.0 + tangent) + 0.5 * gate_pre * (1.0 - tangent * tangent) * gelu_coef * (
        1.0 + 3.0 * 0.044715 * squared
    )
    return (gelu_out, gelu_slope)


def my_place(R):
    rep = lax.axis_index("rep")
    f = lax.axis_index("fsdp")
    return rep, f, f // R, lax.rem(f, R)


def greet(peers):
    barrier = pltpu.get_barrier_semaphore()
    for peer in peers:
        pl.semaphore_signal(barrier, inc=1, device_id=peer, device_id_type=MESH)
    pl.semaphore_wait(barrier, len(peers))


def remote(src, dst, send_sem, recv_sem, peer):
    return pltpu.make_async_remote_copy(
        src_ref=src,
        dst_ref=dst,
        send_sem=send_sem,
        recv_sem=recv_sem,
        device_id=peer,
        device_id_type=MESH,
    )


def lane_peers(rep, g, r, G, R):
    return [(rep, lax.rem(g + k, G) * R + r) for k in range(1, G)]


def group_peers(rep, g, r, G, R):
    return [(rep, g * R + lax.rem(r + j, R)) for j in range(1, R)]


def comm_call(kernel, outs, ins, scratch, collective_id, vmem_ins=False, vmem_outs=False):
    def space(vmem):
        return pl.BlockSpec(memory_space=pltpu.VMEM if vmem else pl.ANY)

    return pl.pallas_call(
        kernel,
        out_shape=outs,
        in_specs=[space(vmem_ins)] * len(ins),
        out_specs=[space(vmem_outs)] * len(outs),
        scratch_shapes=scratch,
        compiler_params=pltpu.CompilerParams(
            collective_id=collective_id, has_side_effects=True, vmem_limit_bytes=vmem_bytes
        ),
    )(*ins)


def scatter_kernel(G, R, pooled, summed, x_ref, o_ref, *scratch):
    rep, f, g, r = my_place(R)
    lanes = lane_peers(rep, g, r, G, R)
    groups = group_peers(rep, g, r, G, R) if pooled else []
    if pooled:
        group_buf, group_send, group_recv = scratch[:3]
        scratch = scratch[3:]
    lane_out, lane_in, lane_send, lane_recv = scratch
    greet(lanes + groups)
    order = list(range(G - 1, -1, -1))
    group_copies = []
    if pooled:
        for k in order:
            for j in range(1, R):
                copy = remote(
                    x_ref.at[lax.rem(g + k, G), lax.rem(r + j, R)],
                    group_buf.at[j - 1, k],
                    group_send.at[j - 1, k],
                    group_recv.at[j - 1, k],
                    groups[j - 1],
                )
                copy.start()
                group_copies.append((j, k, copy))
    lane_copies = []
    for k in order:
        to = lax.rem(g + k, G)
        if pooled:
            for j, kk, copy in group_copies:
                if kk == k:
                    copy.wait_recv()
            total = x_ref[to, r]
            for j in range(1, R):
                total = total + group_buf[j - 1, k]
        else:
            total = x_ref[to]
        if k > 0:
            lane_out[k - 1] = total
            copy = remote(
                lane_out.at[k - 1], lane_in.at[k - 1], lane_send.at[k - 1], lane_recv.at[k - 1], lanes[k - 1]
            )
            copy.start()
            lane_copies.append((k, copy))
        elif summed:
            o_ref[...] = total
        else:
            o_ref[g] = total
    for k, copy in lane_copies:
        copy.wait_recv()
        if summed:
            o_ref[...] += lane_in[k - 1]
        else:
            o_ref[lax.rem(g + G - k, G)] = lane_in[k - 1]
    for _, copy in lane_copies:
        copy.wait_send()
    for _, _, copy in group_copies:
        copy.wait_send()


def scatter(G, R, x, pooled, summed, collective_id):
    block = x.shape[2:] if pooled else x.shape[1:]
    sem = pltpu.SemaphoreType.DMA
    scratch = []
    if pooled:
        scratch = [
            pltpu.VMEM((max(R - 1, 1), G) + block, F32),
            sem((max(R - 1, 1), G)),
            sem((max(R - 1, 1), G)),
        ]
    scratch += [
        pltpu.VMEM((G - 1,) + block, F32),
        pltpu.VMEM((G - 1,) + block, F32),
        sem((G - 1,)),
        sem((G - 1,)),
    ]
    out = jax.ShapeDtypeStruct(block if summed else (G,) + block, F32)
    return comm_call(
        functools.partial(scatter_kernel, G, R, pooled, summed),
        [out],
        [x],
        scratch,
        collective_id,
        vmem_ins=True,
        vmem_outs=True,
    )[0]


def named(names, refs):
    return SimpleNamespace(**dict(zip(names, refs, strict=True)))


def first_kernel(G, R, Q, H, dh, names, *refs):
    m = named(names, refs)
    rep, f, g, r = my_place(R)
    n = G * R
    heads = H // G
    T, D = m.x.shape
    C = heads * dh
    loads = []
    for index, ref in enumerate((m.self_key, m.self_value, m.self_query, m.so, m.cq_w, m.co)):
        copy = pltpu.make_async_copy(ref.at[rep], m.w_in.at[index], m.load_sems.at[index])
        copy.start()
        loads.append(copy)
    greet(everyone(rep, f, n, Q))

    enc_rows = m.enc.shape[0]
    Dn = D // n
    small = Deal(n, m.small_parts, m.small_all, m.small_sems)
    weights = Spread(G, R, Q, lambda k: m.w_mine.at[lax.rem(g + k, G)], m.w, m.w_sems)
    wide = Spread(G, R, Q, lambda k: m.w_in.at[pl.ds(3, 3)], m.wide, m.wide_sems)
    chain = Chain(G, R, m.x_buf, m.x_sems)
    cot_chain = Chain(G, R, m.cot_all, m.cot_sems)
    ckv_sum = Reduce(G, R, *m.ckv_scratch)
    ckv_chain = Chain(G, R, m.ckv, m.ckv_chain_sems)
    for copy in loads:
        copy.wait()
    self_gain = m.gains[0, rep]
    for o in range(G):
        for h in range(heads):
            span = slice((o * heads + h) * dh, (o * heads + h + 1) * dh)
            both = jnp.concatenate([m.w_in[0, :, span], m.w_in[1, :, span]], axis=1)
            m.w_mine[o, :, 2 * h * dh : 2 * (h + 1) * dh] = both * self_gain
        m.w_mine[o, :, 2 * C :] = m.w_in[2, :, o * C : (o + 1) * C] * self_gain
    m.w_in[4] = m.w_in[4] * m.gains[1, rep]
    weights.start()
    wide.start()
    m.x_buf[f] = m.x[...].reshape(pieces, T // pieces, D)
    chain.start()
    for o in range(n):
        m.small_parts[o, :enc_rows, :] = m.enc[:, o * Dn : (o + 1) * Dn]
        m.small_parts[o, enc_rows:, :] = jnp.broadcast_to(m.ffn_gain[...], (8, Dn))
    small.start()
    cot_own = pltpu.make_async_copy(m.cot, m.cot_all.at[f], m.cot_own_sem)
    cot_own.start()
    for h in range(H):
        span = slice(h * dh, (h + 1) * dh)
        both = jnp.concatenate([m.cross_key[:, span], m.cross_value[:, span]], axis=1)
        m.ckv_w[:, 2 * h * dh : 2 * (h + 1) * dh] = both
    bias_rows(G, heads, T, g, m)
    make_strips(R, heads, T, m.vec, m.strip)
    weights.across()
    small.arrive()
    ckv_parts = ckv_sum.parts
    enc_cols = m.small_all[:, :enc_rows, :].reshape(n * enc_rows, Dn)
    ckv_parts[...] = mm(enc_cols, m.ckv_w[...]).reshape(ckv_parts.shape)
    gain = jnp.concatenate([m.small_all[s, enc_rows : enc_rows + 1, :] for s in range(n)], axis=1)
    m.gain[...] = gain
    for o in range(G):
        ckv_sum.offer(o)
    wide.across()
    weights.share()
    for o in range(G):
        ckv_sum.pooled(o)
    weights.arrive()
    w = m.w[...].reshape(D, 3 * C)
    for t in range(G):
        src = chain.arrive(t)
        if t > 0:
            ckv_sum.hand_on(t - 1)
        unit, _ = unit_of(m.x_buf[pl.ds(src * R, R)].reshape(R * T, D))
        rows = pl.ds(pl.multiple_of(src * (R * T), R * T), R * T)
        m.unit[...] = unit
        mine = m.unit[pl.ds(pl.multiple_of(r * T, T), T), :]
        mine_rows = pl.ds(pl.multiple_of(src * T, T), T)
        m.own[mine_rows, :] = mine
        kv = mm(unit, w[:, : 2 * C])
        q = mm(mine, w[:, 2 * C :])
        for h in range(heads):
            m.kv[h, rows, :] = kv[:, 2 * h * dh : 2 * (h + 1) * dh]
            m.q[h, mine_rows, :] = beside(q[:, h * dh : (h + 1) * dh], 0)
    ckv_sum.collect(m.ckv.at[f])
    ckv_chain.start()
    cot_own.wait()
    cot_chain.start()
    for i in range(G):
        L = R * (i + 1) * T
        outs = []
        for h in range(heads):
            scores = strip_scores(R, T, i, r, h, L, m.kv, m.q, m.strip)
            top = jnp.max(scores, axis=0, keepdims=True)
            probs = jnp.exp(scores - top)
            total = jnp.sum(probs, axis=0, keepdims=True)
            out_t = mm_tn(m.kv[h, :L, :], probs)[dh:, :] / total
            outs.append(out_t.T)
            m.lse[i, h : h + 1, :] = top + jnp.log(total)
        m.att[i] = jnp.concatenate(outs, axis=1)
        lane_send(G, R, i, m.att, m.rows, m.att_sems)
        ckv_chain.arrive(i)
    wide.share()
    cot_chain.arrive(0)
    cot_chain.arrive(1)
    lane_wait(G, R, m.att, m.rows, m.att_sems)
    wide.arrive()

    attended = jnp.concatenate([m.rows[i] for i in range(G)], axis=1)
    after = m.x[...] + mm(attended, m.wide[:, :, 0].reshape(D, D))
    m.after[...] = after
    unit_two, _ = unit_of(after)
    m.cq[...] = mm(unit_two, m.wide[:, :, 1].reshape(D, D))
    cot_chain.arrive(2)
    enc_count = n * enc_rows
    for h in range(0, H, 2):
        outs = []
        for a in (h, h + 1):
            ckv = m.ckv[:, 0, :, 2 * a * dh : 2 * (a + 1) * dh].reshape(enc_count, 2 * dh)
            scores = mm_nt(ckv, beside(m.cq[:, a * dh : (a + 1) * dh], 0))
            probs = jnp.exp(scores - jnp.max(scores, axis=0, keepdims=True))
            probs = probs / jnp.sum(probs, axis=0, keepdims=True)
            m.probs[a] = probs
            outs.append(mm_tn(ckv, probs)[dh:, :].T)
        m.cflat[:, h * dh : (h + 2) * dh] = jnp.concatenate(outs, axis=1)
    middle = after + mm(m.cflat[...], m.wide[:, :, 2].reshape(D, D))
    m.middle[...] = middle
    unit_three, _ = unit_of(middle)
    m.n3[...] = unit_three * gain
    cot_chain.arrive(3)

    small.finish()
    weights.finish()
    chain.finish()
    cot_chain.finish()
    ckv_sum.finish()
    ckv_chain.finish()
    wide.finish()


def bias_rows(G, heads, T, g, m):
    buckets = m.position_bias.shape[0]
    late, early = m.table[:, T : 2 * T], m.table[:, :T]
    row = jnp.concatenate([late, jnp.zeros_like(late), early], axis=1)
    lane = lax.broadcasted_iota(jnp.int32, (1, 3 * T), 1)
    after = jnp.logical_and(lane >= T, lane < 2 * T)
    m.ids[...] = jnp.broadcast_to(jnp.where(after, -1, row).astype(F32), m.ids.shape)
    bucket = lax.broadcasted_iota(jnp.int32, (buckets, 3 * T), 0)
    onehot = jnp.where(bucket == row, 1.0, 0.0)
    bias = m.position_bias[...]
    every = lax.dot_general(
        bias - bias[buckets - 1 :],
        onehot,
        (((0,), (0,)), ((), ())),
        precision=lax.Precision.HIGHEST,
        preferred_element_type=F32,
    )
    every = jnp.where(after, masked_score, every)
    m.vec[...] = jnp.zeros_like(m.vec)
    for h in range(heads):
        one = every[h : h + 1]
        for i in range(1, G):
            one = jnp.where(g == i, every[i * heads + h : i * heads + h + 1], one)
        m.vec[h : h + 1, :] = one


def beside(a, at):
    zero = jnp.zeros_like(a)
    return jnp.concatenate([zero, a] if at else [a, zero], axis=1)


def lane_send(G, R, i, src_ref, dst_ref, sems):
    rep, f, g, r = my_place(R)

    @pl.when(g == i)
    def _():
        pltpu.make_async_copy(src_ref.at[i], dst_ref.at[i], sems[2]).start()

    @pl.when(g != i)
    def _():
        remote(src_ref.at[i], dst_ref.at[g], sems[0].at[i], sems[1].at[g], (rep, i * R + r)).start()


def lane_wait(G, R, src_ref, dst_ref, sems):
    rep, f, g, r = my_place(R)
    pltpu.make_async_copy(src_ref.at[g], dst_ref.at[g], sems[2]).wait()
    for i in range(G):

        @pl.when(g != i)
        def _():
            copy = remote(src_ref.at[i], dst_ref.at[i], sems[0].at[i], sems[1].at[i], (rep, i * R + r))
            copy.wait_send()
            copy.wait_recv()


def lane_sems(G):
    sem = pltpu.SemaphoreType.DMA
    return (sem((G,)), sem((G,)), sem)


class Spread:
    def __init__(self, G, R, Q, source, out, sems):
        self.sizes = (G, R, Q)
        self.source, self.out, self.sems = source, out, sems
        rep, f, g, r = my_place(R)
        self.place = (rep, f, g, r)
        self.lanes = lane_peers(rep, g, r, G, R)
        self.groups = group_peers(rep, g, r, G, R)
        self.reps = [(lax.rem(rep + j, Q), f) for j in range(1, Q)]

    def slot(self, k):
        G, R, Q = self.sizes
        _, _, g, r = self.place
        return lax.rem(g + G - k, G) * R + r

    def lane_copy(self, k):
        rep, f = self.place[:2]
        return remote(
            self.source(k), self.out.at[f, rep], self.sems[0].at[k - 1], self.sems[1].at[k - 1], self.lanes[k - 1]
        )

    def own_copy(self):
        rep, f = self.place[:2]
        return pltpu.make_async_copy(self.source(0), self.out.at[f, rep], self.sems[6])

    def rep_copy(self, k, j):
        part = self.out.at[self.slot(k), self.place[0]]
        return remote(part, part, self.sems[2].at[k, j - 1], self.sems[3].at[k, j - 1], self.reps[j - 1])

    def group_copy(self, k, j):
        part = self.out.at[self.slot(k)]
        return remote(part, part, self.sems[4].at[k, j - 1], self.sems[5].at[k, j - 1], self.groups[j - 1])

    def start(self):
        G = self.sizes[0]
        for k in range(G - 1, 0, -1):
            self.lane_copy(k).start()
        self.own_copy().start()

    def across(self):
        G, R, Q = self.sizes
        for k in range(G):
            if k == 0:
                self.own_copy().wait()
            else:
                self.lane_copy(k).wait_recv()
            for j in range(1, Q):
                self.rep_copy(k, j).start()

    def share(self):
        G, R, Q = self.sizes
        for k in range(G):
            for j in range(1, Q):
                self.rep_copy(k, j).wait_recv()
            for j in range(1, R):
                self.group_copy(k, j).start()

    def arrive(self):
        G, R, Q = self.sizes
        for k in range(G):
            for j in range(1, R):
                self.group_copy(k, j).wait_recv()

    def finish(self):
        G, R, Q = self.sizes
        for k in range(G):
            if k > 0:
                self.lane_copy(k).wait_send()
            for j in range(1, Q):
                self.rep_copy(k, j).wait_send()
            for j in range(1, R):
                self.group_copy(k, j).wait_send()


class Deal:
    def __init__(self, n, parts, out, sems):
        self.n, self.parts, self.out, self.sems = n, parts, out, sems
        self.rep, self.f = lax.axis_index("rep"), lax.axis_index("fsdp")

    def copy(self, k):
        to = lax.rem(self.f + k, self.n)
        return remote(
            self.parts.at[to],
            self.out.at[self.f],
            self.sems[0].at[k - 1],
            self.sems[1].at[k - 1],
            (self.rep, to),
        )

    def start(self):
        for k in range(1, self.n):
            self.copy(k).start()
        self.out[self.f] = self.parts[self.f]

    def arrive(self):
        for k in range(1, self.n):
            self.copy(k).wait_recv()

    def finish(self):
        for k in range(1, self.n):
            self.copy(k).wait_send()


def deal_sems(n):
    sem = pltpu.SemaphoreType.DMA
    return (sem((n - 1,)), sem((n - 1,)))


def everyone(rep, f, n, Q):
    return [(rep, lax.rem(f + k, n)) for k in range(1, n)] + [
        (lax.rem(rep + j, Q), f) for j in range(1, Q)
    ]


def spread_sems(G, R, Q):
    sem = pltpu.SemaphoreType.DMA
    return (
        sem((G - 1,)),
        sem((G - 1,)),
        sem((G, Q - 1)),
        sem((G, Q - 1)),
        sem((G, R - 1)),
        sem((G, R - 1)),
        sem,
    )


def lookup(table, i, t):
    rows, columns = len(table), len(table[0])
    flat = i * columns + t
    value = table[0][0] + 0 * flat
    for a in range(rows):
        for b in range(columns):
            if table[a][b] != table[0][0]:
                value = jnp.where(flat == a * columns + b, table[a][b], value)
    return value


class Chain:
    def __init__(self, G, R, buf, sems):
        self.G, self.R, self.buf, self.sems = G, R, buf, sems
        self.pieces = buf.shape[1]
        self.rep, self.f, self.g, self.r = my_place(R)
        self.groups = group_peers(self.rep, self.g, self.r, G, R)
        self.order, self.first, self.second = [], [], []
        for i in range(G):
            order = sorted(range(G), key=lambda s: (abs(s - i), s))
            self.order.append(order)
            far = [abs(s - i) for s in order]
            fresh = [t > 0 and far[t] != far[t - 1] for t in range(G)]
            paired = [fresh[t] and t + 1 < G and far[t + 1] == far[t] for t in range(G)]
            self.first.append([order[t] if fresh[t] else -1 for t in range(G)])
            self.second.append([order[t + 1] if paired[t] else -1 for t in range(G)])

    def part(self, src, p):
        return self.buf.at[src * self.R + self.r, p]

    def step(self, src, side, p):
        part = self.part(src, p)
        to = (self.rep, (self.g + side) * self.R + self.r)
        way = 0 if side > 0 else 1
        return remote(part, part, self.sems[0].at[way, src, p], self.sems[1].at[src, p], to)

    def group_copy(self, src, j, p):
        part = self.part(src, p)
        return remote(
            part, part, self.sems[2].at[j - 1, src, p], self.sems[3].at[j - 1, src, p], self.groups[j - 1]
        )

    def sends(self, src):
        right = jnp.logical_and(src <= self.g, self.g < self.G - 1)
        left = jnp.logical_and(src >= self.g, self.g > 0)
        return ((1, right), (-1, left))

    def onward(self, src, p):
        for side, cond in self.sends(src):

            @pl.when(cond)
            def _():
                self.step(src, side, p).start()

        for j in range(1, self.R):
            self.group_copy(src, j, p).start()

    def start(self):
        for p in range(self.pieces):
            self.onward(self.g, p)

    def arrive(self, t):
        for table in (self.first, self.second):
            came = lookup(table, self.g, t)

            @pl.when(came >= 0)
            def _():
                for p in range(self.pieces):
                    self.step(came, 1, p).wait_recv()
                    self.onward(came, p)

        src = lookup(self.order, self.g, t)
        for j in range(1, self.R):
            for p in range(self.pieces):
                self.group_copy(src, j, p).wait_recv()
        return src

    def finish(self):
        for src in range(self.G):
            for p in range(self.pieces):
                for side, cond in self.sends(src):

                    @pl.when(cond)
                    def _():
                        self.step(src, side, p).wait_send()

                for j in range(1, self.R):
                    self.group_copy(src, j, p).wait_send()


def chain_sems(G, R, pieces):
    sem = pltpu.SemaphoreType.DMA
    return (sem((2, G, pieces)), sem((G, pieces)), sem((R - 1, G, pieces)), sem((R - 1, G, pieces)))


def make_strips(R, heads, T, vec_ref, strip_ref):
    for h in range(heads):
        vec = jnp.broadcast_to(vec_ref[h : h + 1, :], (2 * T, 3 * T))
        pair = pltpu.roll(vec, 0, 1, stride=1, stride_axis=0)[:, :T]
        if R > 1:
            strip_ref[h, : (R - 1) * T, :] = jnp.zeros(((R - 1) * T, T), F32)
            strip_ref[h, (R + 1) * T :, :] = jnp.full(((R - 1) * T, T), masked_score, F32)
        strip_ref[h, (R - 1) * T : (R + 1) * T, :] = pair


def strip_scores(R, T, i, r, h, L, kv_ref, q_ref, strip_ref):
    scores = mm_nt(kv_ref[h, :L, :], q_ref[h, i * T : (i + 1) * T, :])
    skip = 1 if i == 0 else 0
    width = (R + 1 - skip) * T
    start = pl.multiple_of((R - 1 - r + skip) * T, T)
    near = scores[L - width :, :] + strip_ref[h, pl.ds(start, width), :]
    if width == L:
        return near
    return jnp.concatenate([scores[: L - width, :], near], axis=0)


def call_stage(kernel, near_ins, far_ins, near_outs, far_outs, scratch, collective_id):
    vm = pl.BlockSpec(memory_space=pltpu.VMEM)
    hbm = pl.BlockSpec(memory_space=pl.ANY)
    outs = near_outs | far_outs
    names = tuple(near_ins) + tuple(far_ins) + tuple(outs) + tuple(scratch)
    results = pl.pallas_call(
        functools.partial(kernel, names),
        out_shape=[jax.ShapeDtypeStruct(shape, F32) for shape in outs.values()],
        in_specs=[vm] * len(near_ins) + [hbm] * len(far_ins),
        out_specs=[vm] * len(near_outs) + [hbm] * len(far_outs),
        scratch_shapes=list(scratch.values()),
        compiler_params=pltpu.CompilerParams(
            collective_id=collective_id,
            has_side_effects=collective_id is not None,
            vmem_limit_bytes=vmem_bytes,
        ),
    )(*near_ins.values(), *far_ins.values())
    return named(tuple(outs), results)


def first_stage(G, R, Q, H, dh, near_ins, far_ins, collective_id):
    T, D = near_ins["x"].shape
    n = G * R
    S = n * T
    heads = H // G
    C = heads * dh
    enc_rows = near_ins["enc"].shape[0]
    part = D // n // Q
    block = (pieces, T // pieces, D)
    outs = dict(
        att=(G, T, C),
        rows=(G, T, C),
        q=(heads, G * T, 2 * dh),
        kv=(heads, S, 2 * dh),
        lse=(G, 8, T),
        w=(n, Q, part, 3 * C),
        own=(G * T, D),
        small_all=(n, enc_rows + 8, D // n),
        vec=(8, 3 * T),
        ids=(8, 3 * T),
        ckv_w=(D // n, 2 * D),
        ckv=(n, 1, enc_rows, 2 * D),
        gain=(1, D),
        after=(T, D),
        middle=(T, D),
        n3=(T, D),
        cq=(T, D),
        cflat=(T, D),
        probs=(H, n * enc_rows, T),
        wide=(n, Q, 3, part, D),
    )
    far_outs = dict(cot_all=(n,) + block)
    scratch = dict(
        x_buf=pltpu.VMEM((n,) + block, F32),
        unit=pltpu.VMEM((R * T, D), F32),
        strip=pltpu.VMEM((heads, 2 * R * T, T), F32),
        x_sems=chain_sems(G, R, pieces),
        cot_sems=chain_sems(G, R, pieces),
        cot_own_sem=pltpu.SemaphoreType.DMA,
        w_in=pltpu.VMEM((6, part, D), F32),
        w_mine=pltpu.VMEM((G, part, 3 * C), F32),
        small_parts=pltpu.VMEM((n, enc_rows + 8, D // n), F32),
        load_sems=pltpu.SemaphoreType.DMA((6,)),
        w_sems=spread_sems(G, R, Q),
        wide_sems=spread_sems(G, R, Q),
        att_sems=lane_sems(G),
        small_sems=deal_sems(n),
        ckv_scratch=tuple(reduce_scratch(G, R, 1, (enc_rows, 2 * D))),
        ckv_chain_sems=chain_sems(G, R, 1),
    )
    return call_stage(
        functools.partial(first_kernel, G, R, Q, H, dh),
        near_ins,
        far_ins,
        outs,
        far_outs,
        scratch,
        collective_id,
    )


class Reduce:
    def __init__(self, G, R, parts, pool, inbox, sems, mode="near"):
        self.G, self.parts, self.pool, self.inbox, self.sems = G, parts, pool, inbox, sems
        self.pieces = parts.shape[2]
        self.rep, self.f, self.g, self.r = my_place(R)
        self.stride = R
        self.R = R if pool is not None else 1
        self.mine = self.r if pool is not None else 0
        self.groups = group_peers(self.rep, self.g, self.r, G, R)
        orders = []
        for g in range(G):
            due = {o: o + g if o > g else (G - 1 - o) + (G - 1 - g) for o in range(G) if o != g}
            if mode == "far":
                due = {o: G - 1 - o + g if o > g else o + G - 1 - g for o in due}
            held = [o for o in due if (g > 0 if o > g else g < G - 1)]
            orders.append((sorted(held, key=lambda o: due[o]) + [-1] * G)[: G - 1])
        self.orders = orders
        self.far_first = [sorted(range(G), key=lambda o: -abs(o - i)) for i in range(G)]

    def group_copy(self, o, j, p):
        other = lax.rem(self.r + j, self.R)
        return remote(
            self.parts.at[o, other, p],
            self.pool.at[j - 1, o, p],
            self.sems[0].at[j - 1, o, p],
            self.sems[1].at[j - 1, o, p],
            self.groups[j - 1],
        )

    def lane_copy(self, o, p):
        right = o > self.g
        to = jnp.where(right, self.g + 1, self.g - 1)
        last_left = jnp.logical_and(jnp.logical_not(right), to == o)
        slot = jnp.where(last_left, self.G, o)
        part = self.parts.at[o, self.mine, p]
        peer = (self.rep, to * self.stride + self.r)
        return remote(part, self.inbox.at[slot, p], self.sems[2].at[o, p], self.sems[3].at[slot, p], peer)

    def inbox_wait(self, slot, p):
        remote(
            self.parts.at[0, self.mine, p],
            self.inbox.at[slot, p],
            self.sems[2].at[0, p],
            self.sems[3].at[slot, p],
            (self.rep, self.f),
        ).wait_recv()

    def offer(self, o):
        for p in range(self.pieces):
            for j in range(1, self.R):
                self.group_copy(o, j, p).start()

    def pooled(self, o):
        first = jnp.logical_or(
            jnp.logical_and(o > self.g, self.g == 0),
            jnp.logical_and(o < self.g, self.g == self.G - 1),
        )
        for p in range(self.pieces):
            for j in range(1, self.R):
                self.group_copy(o, j, p).wait_recv()
            if self.R > 1:
                total = self.parts[o, self.mine, p]
                for j in range(1, self.R):
                    total = total + self.pool[j - 1, o, p]
                self.parts[o, self.mine, p] = total

            @pl.when(first)
            def _():
                self.lane_copy(o, p).start()

    def hand_on(self, index):
        o = lookup(self.orders, self.g, index)

        @pl.when(o >= 0)
        def _():
            for p in range(self.pieces):
                self.inbox_wait(o, p)
                self.parts[o, self.mine, p] += self.inbox[o, p]
                self.lane_copy(o, p).start()

    def collect(self, out):
        for p in range(self.pieces):
            out[p] = self.parts[self.g, self.mine, p]

        for cond, slot in ((self.g > 0, self.g), (self.g < self.G - 1, self.G)):

            @pl.when(cond)
            def _():
                for p in range(self.pieces):
                    self.inbox_wait(slot, p)
                    out[p] += self.inbox[slot, p]

    def finish(self):
        for o in range(self.G):
            for p in range(self.pieces):
                for j in range(1, self.R):
                    self.group_copy(o, j, p).wait_send()

            @pl.when(self.g != o)
            def _():
                for p in range(self.pieces):
                    self.lane_copy(o, p).wait_send()


def reduce_scratch(G, R, pieces, block):
    sem = pltpu.SemaphoreType.DMA
    block = (pieces, block[0] // pieces) + block[1:]
    return [
        pltpu.VMEM((G, R) + block, F32),
        pltpu.VMEM((R - 1, G) + block if R > 1 else (8, 128), F32),
        pltpu.VMEM((G + 1,) + block, F32),
        (sem((max(R - 1, 1), G, pieces)), sem((max(R - 1, 1), G, pieces)), sem((G, pieces)), sem((G + 1, pieces))),
    ]


def ffn_kernel(
    G,
    R,
    n3_ref,
    cot_ref,
    gate_ref,
    up_ref,
    down_ref,
    dn3_ref,
    out_ref,
    d_gate_ref,
    d_up_ref,
    d_down_ref,
    gate_parts,
    up_parts,
    down_parts,
    gate_in,
    up_in,
    down_in,
    rep_sems,
    n3_buf,
    n3_high,
    n3_low,
    inner_high,
    inner_low,
    grads_high,
    grads_low,
    wide_high,
    wide_low,
    tall_high,
    tall_low,
    dn3_parts,
    dn3_pool,
    dn3_inbox,
    dn3_sems,
    n3_sems,
):
    rep, f, g, r = my_place(R)
    T, D = n3_ref.shape
    F = gate_ref.shape[1]
    rows_each = R * T
    block = (R, pieces, T // pieces, D)
    Q = gate_parts.shape[0]
    greet(lane_peers(rep, g, r, G, R) + group_peers(rep, g, r, G, R) + everyone(rep, f, 1, Q))
    sums = [
        (gate_parts, gate_in, d_gate_ref),
        (up_parts, up_in, d_up_ref),
        (down_parts, down_in, d_down_ref),
    ]

    def rep_copy(a, j):
        to = lax.rem(rep + j, Q)
        sems = rep_sems[0].at[a, j - 1], rep_sems[1].at[a, j - 1]
        return remote(sums[a][0].at[to], sums[a][1].at[j - 1], *sems, (to, f))

    def to_replicas(a, value):
        sums[a][0][...] = value.reshape(sums[a][0].shape)
        for j in range(1, Q):
            rep_copy(a, j).start()

    chain = Chain(G, R, n3_buf, n3_sems)
    d_three = Reduce(G, R, dn3_parts, dn3_pool, dn3_inbox, dn3_sems)
    n3_buf[f] = n3_ref[...].reshape(pieces, T // pieces, D)
    chain.start()
    for index, ref in enumerate((gate_ref, up_ref, down_ref)):
        high, low = halves(ref[...])
        span = slice(index * F, (index + 1) * F)
        wide = index < 2
        wide_high[:, span] = high if wide else high.T
        wide_low[:, span] = low if wide else low.T
        tall_high[span, :] = high.T if wide else high
        tall_low[span, :] = low.T if wide else low

    @pl.loop(0, G)
    def _(t):
        src = chain.arrive(t)
        rows = pl.ds(pl.multiple_of(src * rows_each, rows_each), rows_each)
        n3 = halves(n3_buf[pl.ds(src * R, R)].reshape(rows_each, D))
        n3_high[rows, :], n3_low[rows, :] = n3
        pre = dot3(n3, (wide_high[:, : 2 * F], wide_low[:, : 2 * F]))
        gate_pre, up_pre = pre[:, :F], pre[:, F:]
        gelu_out, gelu_slope = gelu_parts(gate_pre)
        inner = halves(gelu_out * up_pre)
        inner_high[rows, :], inner_low[rows, :] = inner
        cot = halves(cot_ref[pl.ds(src * R, R)].reshape(rows_each, D))
        grad_inner = dot3(cot, (wide_high[:, 2 * F :], wide_low[:, 2 * F :]))
        grads = halves(
            jnp.concatenate([grad_inner * up_pre * gelu_slope, grad_inner * gelu_out], axis=1)
        )
        grads_high[rows, :], grads_low[rows, :] = grads
        dn3 = dot3(grads, (tall_high[: 2 * F, :], tall_low[: 2 * F, :]))
        dn3_parts[src] = dn3.reshape(block)
        d_three.offer(src)
        out = dot3(inner, (tall_high[2 * F :, :], tall_low[2 * F :, :]))
        out_ref[src] = out.reshape(block)
        d_three.pooled(src)

    S = G * rows_each
    tn = (((0,), (0,)), ((), ()))
    n3 = (n3_high[...], n3_low[...])
    to_replicas(0, dot3(n3, (grads_high[:, :F], grads_low[:, :F]), tn))
    d_three.hand_on(0)
    to_replicas(1, dot3(n3, (grads_high[:, F:], grads_low[:, F:]), tn))
    d_three.hand_on(1)
    cot = halves(cot_ref[...].reshape(S, D))
    to_replicas(2, dot3((inner_high[...], inner_low[...]), cot, tn))
    for index in range(2, G - 1):
        d_three.hand_on(index)
    d_three.collect(dn3_ref)
    for a in range(3):
        total = sums[a][0][rep]
        for j in range(1, Q):
            rep_copy(a, j).wait_recv()
            total = total + sums[a][1][j - 1]
        sums[a][2][...] = total
        for j in range(1, Q):
            rep_copy(a, j).wait_send()
    chain.finish()
    d_three.finish()


def ffn_stage(G, R, Q, n3, cot, gate, up, down, collective_id):
    T, D = n3.shape
    F = gate.shape[1]
    n = G * R
    S = n * T
    vm = pl.BlockSpec(memory_space=pltpu.VMEM)
    block = (pieces, T // pieces, D)
    shape = lambda *dims: jax.ShapeDtypeStruct(dims, F32)
    dn3, out, d_gate, d_up, d_down = pl.pallas_call(
        functools.partial(ffn_kernel, G, R),
        out_shape=[
            shape(*block),
            shape(G, R, *block),
            shape(D // Q, F),
            shape(D // Q, F),
            shape(F // Q, D),
        ],
        in_specs=[vm] * 5,
        out_specs=[vm] * 5,
        scratch_shapes=[
            pltpu.VMEM((Q, D // Q, F), F32),
            pltpu.VMEM((Q, D // Q, F), F32),
            pltpu.VMEM((Q, F // Q, D), F32),
            pltpu.VMEM((Q - 1, D // Q, F), F32),
            pltpu.VMEM((Q - 1, D // Q, F), F32),
            pltpu.VMEM((Q - 1, F // Q, D), F32),
            (pltpu.SemaphoreType.DMA((3, Q - 1)), pltpu.SemaphoreType.DMA((3, Q - 1))),
            pltpu.VMEM((n,) + block, F32),
            pltpu.VMEM((S, D), BF16),
            pltpu.VMEM((S, D), BF16),
            pltpu.VMEM((S, F), BF16),
            pltpu.VMEM((S, F), BF16),
            pltpu.VMEM((S, 2 * F), BF16),
            pltpu.VMEM((S, 2 * F), BF16),
            pltpu.VMEM((D, 3 * F), BF16),
            pltpu.VMEM((D, 3 * F), BF16),
            pltpu.VMEM((3 * F, D), BF16),
            pltpu.VMEM((3 * F, D), BF16),
        ]
        + reduce_scratch(G, R, pieces, (T, D))
        + [chain_sems(G, R, pieces)],
        compiler_params=pltpu.CompilerParams(
            collective_id=collective_id, has_side_effects=True, vmem_limit_bytes=vmem_bytes
        ),
    )(n3, cot, gate, up, down)
    return dn3.reshape(T, D), out, d_gate, d_up, d_down


class Fold:
    def __init__(self, G, R, Q, scratch, out, summed):
        self.G, self.R, self.Q = G, R, Q
        self.parts, self.pool, self.rep_in, self.lane_out, self.lane_in, self.sems = scratch
        self.A = self.parts.shape[0]
        self.out, self.summed = out, summed
        self.rep, self.f, self.g, self.r = my_place(R)
        self.groups = group_peers(self.rep, self.g, self.r, G, R)
        self.lanes = lane_peers(self.rep, self.g, self.r, G, R)
        self.to_rep = [lax.rem(self.rep + j, Q) for j in range(1, Q)]
        if G * R == 1:
            self.g = self.r = 0

    def group_copy(self, a, o, j):
        return remote(
            self.parts.at[a, o, lax.rem(self.r + j, self.R)],
            self.pool.at[j - 1, a, o],
            self.sems[0].at[j - 1, a, o],
            self.sems[1].at[j - 1, a, o],
            self.groups[j - 1],
        )

    def rep_copy(self, o, j):
        return remote(
            self.parts.at[:, o, self.r, self.to_rep[j - 1]],
            self.rep_in.at[j - 1, o],
            self.sems[2].at[j - 1, o],
            self.sems[3].at[j - 1, o],
            (self.to_rep[j - 1], self.f),
        )

    def lane_copy(self, k):
        return remote(
            self.lane_out.at[k],
            self.lane_in.at[k - 1],
            self.sems[4].at[k - 1],
            self.sems[5].at[k - 1],
            self.lanes[k - 1],
        )

    def back_copy(self, j):
        part = self.out.at[self.rep]
        return remote(
            part, part, self.sems[6].at[j - 1], self.sems[7].at[j - 1], (self.to_rep[j - 1], self.f)
        )

    def to_group(self, a):
        for o in range(self.G):
            for j in range(1, self.R):
                self.group_copy(a, o, j).start()

    def to_replicas(self):
        for o in range(self.G):
            for a in range(self.A):
                for j in range(1, self.R):
                    self.group_copy(a, o, j).wait_recv()
                    self.parts[a, o, self.r] += self.pool[j - 1, a, o]
            for j in range(1, self.Q):
                self.rep_copy(o, j).start()

    def to_owner(self):
        for k in range(self.G - 1, -1, -1):
            o = lax.rem(self.g + k, self.G)
            for j in range(1, self.Q):
                self.rep_wait(o, j)
            total = self.parts[:, o, self.r, self.rep]
            for j in range(1, self.Q):
                total = total + self.rep_in[j - 1, o]
            self.lane_out[k] = total
            if k > 0:
                self.lane_copy(k).start()

    def rep_wait(self, o, j):
        self.rep_copy(o, j).wait_recv()

    def to_everyone(self):
        if self.summed:
            total = self.lane_out[0]
            for k in range(1, self.G):
                self.lane_copy(k).wait_recv()
                total = total + self.lane_in[k - 1]
            self.out[self.rep] = total
        else:
            self.out[self.rep, self.g] = self.lane_out[0]
            for k in range(1, self.G):
                self.lane_copy(k).wait_recv()
                self.out[self.rep, lax.rem(self.g + self.G - k, self.G)] = self.lane_in[k - 1]
        for j in range(1, self.Q):
            self.back_copy(j).start()

    def finish(self):
        for j in range(1, self.Q):
            self.back_copy(j).wait()
        for o in range(self.G):
            for a in range(self.A):
                for j in range(1, self.R):
                    self.group_copy(a, o, j).wait_send()
            for j in range(1, self.Q):
                self.rep_copy(o, j).wait_send()
        for k in range(1, self.G):
            self.lane_copy(k).wait_send()


def fold_scratch(A, G, R, Q, m, W):
    sem = pltpu.SemaphoreType.DMA
    some, lanes = max(R - 1, 1), max(G - 1, 1)
    return (
        pltpu.VMEM((A, G, R, Q, m, W), F32),
        pltpu.VMEM((some, A, G, Q, m, W) if R > 1 else (1, 1, 1, 1, 8, 128), F32),
        pltpu.VMEM((Q - 1, G, A, m, W), F32),
        pltpu.VMEM((G, A, m, W), F32),
        pltpu.VMEM((lanes, A, m, W), F32),
        (
            sem((some, A, G)),
            sem((some, A, G)),
            sem((Q - 1, G)),
            sem((Q - 1, G)),
            sem((lanes,)),
            sem((lanes,)),
            sem((Q - 1,)),
            sem((Q - 1,)),
        ),
    )


def back_kernel(G, R, Q, H, dh, buckets, fused, names, *refs):
    m = named(names, refs)
    rep, f, g, r = my_place(R)
    n = G * R
    heads = H // G
    T, D = m.x.shape
    C = heads * dh
    Dn = D // n
    groups = group_peers(rep, g, r, G, R)
    reps = [(lax.rem(rep + j, Q), f) for j in range(1, Q)]
    greet(everyone(rep, f, n, Q))

    ffn_sums = ((m.d_gate_in, m.d_gate), (m.d_up_in, m.d_up), (m.d_down_in, m.d_down))

    def ffn_own(a):
        part, whole = ffn_sums[a]
        return pltpu.make_async_copy(part, whole.at[rep], m.ffn_sems[2].at[a])

    def ffn_copy(a, j):
        part, whole = ffn_sums[a]
        sems = m.ffn_sems[0].at[a, j - 1], m.ffn_sems[1].at[a, j - 1]
        return remote(part, whole.at[rep], *sems, reps[j - 1])

    for a in range(3):
        for j in range(1, Q):
            ffn_copy(a, j).start()
        ffn_own(a).start()
    out_sum = Reduce(G, R, *m.out_scratch, mode="far") if fused else None
    ckv_sum = Reduce(G, R, *m.ckv_scratch)
    du_parts, _, du_inbox, du_sems = m.du_scratch
    du_sum = Reduce(G, R, du_parts, None, du_inbox, du_sems)
    ckv_chain = Chain(G, R, m.ckv_all, m.ckv_chain_sems)
    d_wide = (m.d_wide0, m.d_wide1, m.d_wide2)
    wides = [Fold(G, R, Q, m.wide_scratch[a], d_wide[a], True) for a in range(3)] if fused else []
    d_w = Fold(G, R, Q, m.dw_scratch, m.d_w, False)
    d_cw = Fold(1, 1, Q, m.cw_scratch, m.d_ckv_w, True)

    def load(a):
        return pltpu.make_async_copy(m.wide.at[:, :, a], m.weight, m.load_sem)

    def weight():
        return m.weight[...].reshape(D, D)

    def give(a, value):
        if fused:
            wides[a].parts[0] = value.reshape(wides[a].parts.shape[1:])
            wides[a].to_group(0)
        else:
            d_wide[a][...] = value

    load(2).start()
    if fused:
        load_out = pltpu.make_async_copy(m.out_parts, out_sum.parts, m.out_sem)
        load_out.start()

    unit_three, scale_three = unit_of(m.middle[...])
    dn3 = m.dn3[...]
    d_gain = jnp.sum(dn3 * unit_three, axis=0, keepdims=True)
    m.d_middle[...] = m.cot[...] + unit_backward(dn3 * m.gain[...], unit_three, scale_three)
    if fused:
        load_out.wait()
        for o in range(G):
            out_sum.offer(o)
    load(2).wait()
    m.d_after[...] = mm_nt(m.d_middle[...], weight())
    load(1).start()
    enc_rows = ckv_sum.parts.shape[3]
    enc_count = n * enc_rows
    for h in range(0, H, 2):
        outs = []
        for a in (h, h + 1):
            span = slice(2 * a * dh, 2 * (a + 1) * dh)
            ckv = m.ckv[:, 0, :, span].reshape(enc_count, 2 * dh)
            probs = m.probs[a]
            grad = beside(m.d_after[:, a * dh : (a + 1) * dh], 1)
            d_probs = mm_nt(ckv, grad)
            delta = jnp.sum(probs * d_probs, axis=0, keepdims=True)
            d_scores = probs * (d_probs - delta)
            cq = beside(m.cq[:, a * dh : (a + 1) * dh], 0)
            d_ckv = mm(jnp.concatenate([d_scores, probs], axis=1), jnp.concatenate([cq, grad], axis=0))
            ckv_sum.parts[:, :, :, :, span] = d_ckv.reshape(G, R, 1, enc_rows, 2 * dh)
            outs.append(mm_tn(ckv, d_scores)[:dh, :].T)
        m.d_cq[:, h * dh : (h + 2) * dh] = jnp.concatenate(outs, axis=1)
    for o in range(G):
        ckv_sum.offer(o)
    if fused:
        out_sum.pooled(lookup(out_sum.far_first, g, 0))
    give(2, mm_tn(m.cflat[...], m.d_middle[...]))
    load(1).wait()
    unit_two, scale_two = unit_of(m.after[...])
    d_unit = mm_nt(m.d_cq[...], weight())
    load(0).start()
    m.d_after[...] = m.d_middle[...] + unit_backward(d_unit, unit_two, scale_two)
    for o in range(G):
        ckv_sum.pooled(o)
    if fused:
        wides[2].to_replicas()
    give(1, mm_tn(unit_two, m.d_cq[...]))
    load(0).wait()
    d_att = mm_nt(m.d_after[...], weight())
    for i in range(G):
        m.d_att[i] = d_att[:, i * C : (i + 1) * C]
        lane_send(G, R, i, m.d_att, m.grad, m.att_sems)
    if fused:
        for t in range(1, G):
            out_sum.pooled(lookup(out_sum.far_first, g, t))
        wides[1].to_replicas()
    attended = jnp.concatenate([m.rows[i] for i in range(G)], axis=1)
    give(0, mm_tn(attended, m.d_after[...]))
    if fused:
        out_sum.hand_on(0)
    make_strips(R, heads, T, m.vec, m.strip)
    m.near[...] = jnp.zeros_like(m.near)
    m.far[...] = jnp.zeros_like(m.far)
    ckv_sum.hand_on(0)
    if fused:
        wides[0].to_replicas()
    ckv_sum.hand_on(1)
    lane_wait(G, R, m.d_att, m.grad, m.att_sems)

    def dkv_copy(i, j):
        return remote(
            m.dkv_parts.at[i, lax.rem(r + j, R)],
            m.dkv_pool.at[j - 1, i],
            m.dkv_send.at[j - 1, i],
            m.dkv_recv.at[j - 1, i],
            groups[j - 1],
        )

    dqkv = m.dqkv

    def own_gradient(i):
        for j in range(1, R):
            dkv_copy(i, j).wait_recv()
        dkv = m.dkv_parts[i, r]
        for j in range(1, R):
            dkv = dkv + m.dkv_pool[j - 1, i]
        dqkv[i, :, : 2 * C] = dkv

    for i in range(G - 1, -1, -1):
        L = R * (i + 1) * T
        grad = m.grad[i]
        prod_t = (grad * m.att[i]).T
        dqs = []
        for h in range(heads):
            scores = strip_scores(R, T, i, r, h, L, m.kv, m.q, m.strip)
            probs = jnp.exp(scores - m.lse[i, h : h + 1, :])
            grad_h = beside(grad[:, h * dh : (h + 1) * dh], 1)
            delta = jnp.sum(prod_t[h * dh : (h + 1) * dh, :], axis=0, keepdims=True)
            d_scores = probs * (mm_nt(m.kv[h, :L, :], grad_h) - delta)
            q_h = m.q[h, i * T : (i + 1) * T, :]
            dkv = mm(
                jnp.concatenate([d_scores, probs], axis=1), jnp.concatenate([q_h, grad_h], axis=0)
            )
            if i == G - 1:
                m.dkv[h] = dkv
            else:
                m.dkv[h, :L, :] += dkv
            dqs.append(mm_tn(m.kv[h, :L, :], d_scores)[:dh, :].T)
            skip = 1 if i == 0 else 0
            width = (R + 1 - skip) * T
            m.near[h, skip * T :, :] += d_scores[L - width :, :]
            if width < L:
                m.far[h : h + 1, :] += jnp.sum(d_scores[: L - width, :], axis=0, keepdims=True)
        m.dqkv[i, :, 2 * C :] = jnp.concatenate(dqs, axis=1)
        for b in range(R):
            rows = slice((i * R + b) * T, (i * R + b + 1) * T)
            m.dkv_parts[i, b] = jnp.concatenate([m.dkv[h, rows, :] for h in range(heads)], axis=1)
        for j in range(1, R):
            dkv_copy(i, j).start()
        if i < G - 1:
            own_gradient(i + 1)
        if fused and i > 1:
            out_sum.hand_on(G - i)
        if i == 3:
            ckv_sum.hand_on(2)
        if i == 2:
            ckv_sum.collect(m.ckv_all.at[f])
            ckv_chain.start()
        if i == 1:
            ckv_chain.arrive(0)
            ckv_chain.arrive(1)
    own_gradient(0)
    if fused:
        wides[2].to_owner()
    w = m.w[...].reshape(D, 3 * C)
    for i in range(G):
        du_parts[i, 0] = mm_nt(dqkv[i], w).reshape(du_parts.shape[2:])
        du_sum.pooled(i)
    d_w.parts[0] = mm_tn(m.own[...], dqkv[...].reshape(G * T, 3 * C)).reshape(d_w.parts.shape[1:])
    d_w.to_group(0)
    if fused:
        wides[1].to_owner()
        wides[2].to_everyone()

    ids = jnp.broadcast_to(m.ids[0:1, :], (2 * T, 3 * T))
    ids = pltpu.roll(ids, 0, 1, stride=1, stride_axis=0)[:, :T]
    each = buckets // n
    tiny_parts = m.tiny_parts
    tiny_parts[...] = jnp.zeros_like(tiny_parts)
    for h in range(heads):
        pair = m.near[h, pl.ds(pl.multiple_of(r * T, T), 2 * T), :]
        far = m.far[h : h + 1, :]
        for idx in range(R - 1):
            block = jnp.sum(m.near[h, idx * T : (idx + 1) * T, :], axis=0, keepdims=True)
            far = far + jnp.where(idx < r, block, 0.0)
        for b in range(buckets):
            part = jnp.sum(jnp.where(ids == b, pair, 0.0), axis=0, keepdims=True)
            if b == buckets - 1:
                part = part + far
            row = h * each + b % each
            tiny_parts[b // each, row : row + 1, :] = part
    last = heads * each
    for o in range(n):
        tiny_parts[o, last : last + 1, :Dn] = d_gain[:, o * Dn : (o + 1) * Dn]
    tiny = Deal(n, tiny_parts, m.tiny_in, m.tiny_sems)
    tiny.start()

    du_sum.hand_on(0)
    d_w.to_replicas()
    ckv_chain.arrive(2)
    ckv_chain.arrive(3)
    if fused:
        wides[0].to_owner()
    d_w.to_owner()
    if fused:
        wides[1].to_everyone()
    du_sum.hand_on(1)
    d_ckv = m.ckv_all[...].reshape(enc_count, 2 * D)
    m.enc_parts[...] = mm_nt(d_ckv, m.ckv_w[...]).reshape(m.enc_parts.shape)
    d_enc = Deal(n, m.enc_parts, m.d_enc, m.enc_sems)
    d_enc.start()
    enc_cols = m.small_all[:, :enc_rows, :].reshape(enc_count, Dn)
    d_cw.parts[0, 0, 0] = mm_tn(enc_cols, d_ckv).reshape(d_cw.parts.shape[3:])
    d_cw.to_replicas()
    d_w.to_everyone()
    if fused:
        wides[0].to_everyone()
    for index in range(2, G - 1):
        du_sum.hand_on(index)
    tiny.arrive()
    for s in range(G):
        total = m.tiny_in[s * R]
        for j in range(1, R):
            total = total + m.tiny_in[s * R + j]
        m.tiny[rep, s] = total

    def tiny_copy(j):
        part = m.tiny.at[rep]
        return remote(part, part, m.tiny_rep_send.at[j - 1], m.tiny_rep_recv.at[j - 1], reps[j - 1])

    for j in range(1, Q):
        tiny_copy(j).start()
    d_cw.to_owner()
    d_cw.to_everyone()
    if fused:
        out_sum.collect(m.out)
        m.out[...] += m.middle[...].reshape(m.out.shape)
    du_sum.collect(m.du)
    unit_one, scale_one = unit_of(m.x[...])
    d_unit = m.du[...].reshape(T, D)
    m.d_x[...] = m.d_after[...] + unit_backward(d_unit, unit_one, scale_one)

    d_enc.arrive()
    for a in range(3):
        ffn_own(a).wait()
        for j in range(1, Q):
            ffn_copy(a, j).wait()
    for j in range(1, Q):
        tiny_copy(j).wait()
    tiny.finish()
    d_enc.finish()
    for i in range(G):
        for j in range(1, R):
            dkv_copy(i, j).wait_send()
    if fused:
        out_sum.finish()
        for fold in wides:
            fold.finish()
    ckv_sum.finish()
    du_sum.finish()
    ckv_chain.finish()
    d_w.finish()
    d_cw.finish()


def back_stage(G, R, Q, H, dh, buckets, near_ins, far_ins, collective_id):
    T, D = near_ins["x"].shape
    n = G * R
    S = n * T
    heads = H // G
    C = heads * dh
    Dn = D // n
    part = Dn // Q
    enc_rows = near_ins["ckv"].shape[2]
    block = (pieces, T // pieces, D)
    tiny_rows = -(-(heads * (buckets // n) + 1) // 8) * 8
    sem = pltpu.SemaphoreType.DMA
    some = max(R - 1, 1)
    fused = R <= 2
    far_outs = dict(
        d_gate=(Q,) + far_ins["d_gate_in"].shape,
        d_up=(Q,) + far_ins["d_up_in"].shape,
        d_down=(Q,) + far_ins["d_down_in"].shape,
    )
    outs = dict(
        d_x=(T, D),
        out=block,
        d_w=(Q, G, 1, part, 3 * C),
        d_wide0=(Q, 1, part, D) if fused else (D, D),
        d_wide1=(Q, 1, part, D) if fused else (D, D),
        d_wide2=(Q, 1, part, D) if fused else (D, D),
        d_ckv_w=(Q, 1, part, 2 * D),
        d_enc=(n, enc_rows, Dn),
        tiny=(Q, G, tiny_rows, T),
    )
    scratch = dict(
        d_middle=pltpu.VMEM((T, D), F32),
        d_cq=pltpu.VMEM((T, D), F32),
        d_after=pltpu.VMEM((T, D), F32),
        d_att=pltpu.VMEM((G, T, C), F32),
        weight=pltpu.VMEM((n, Q, part, D), F32),
        load_sem=sem,
        ffn_sems=(sem((3, Q - 1)), sem((3, Q - 1)), sem((3,))),
        out_sem=sem,
        strip=pltpu.VMEM((heads, 2 * R * T, T), F32),
        near=pltpu.VMEM((heads, (R + 1) * T, T), F32),
        far=pltpu.VMEM((8, T), F32),
        dkv=pltpu.VMEM((heads, S, 2 * dh), F32),
        dqkv=pltpu.VMEM((G, T, 3 * C), F32),
        grad=pltpu.VMEM((G, T, C), F32),
        dkv_parts=pltpu.VMEM((G, R, T, 2 * C), F32),
        dkv_pool=pltpu.VMEM((some, G, T, 2 * C), F32),
        dkv_send=sem((some, G)),
        dkv_recv=sem((some, G)),
        tiny_parts=pltpu.VMEM((n, tiny_rows, T), F32),
        tiny_in=pltpu.VMEM((n, tiny_rows, T), F32),
        tiny_sems=deal_sems(n),
        tiny_rep_send=sem((Q - 1,)),
        tiny_rep_recv=sem((Q - 1,)),
        enc_parts=pltpu.VMEM((n, enc_rows, Dn), F32),
        enc_sems=deal_sems(n),
        ckv_all=pltpu.VMEM((n, 1, enc_rows, 2 * D), F32),
        ckv_chain_sems=chain_sems(G, R, 1),
        att_sems=lane_sems(G),
        du=pltpu.VMEM(block, F32),
        ckv_scratch=tuple(reduce_scratch(G, R, 1, (enc_rows, 2 * D))),
        du_scratch=tuple(reduce_scratch(G, 1, pieces, (T, D))),
        dw_scratch=fold_scratch(1, G, R, Q, part, 3 * C),
        cw_scratch=fold_scratch(1, 1, 1, Q, part, 2 * D),
    )
    if fused:
        scratch |= dict(
            wide_scratch=tuple(fold_scratch(1, G, R, Q, part, D) for _ in range(3)),
            out_scratch=tuple(reduce_scratch(G, R, pieces, (T, D))),
        )
    results = call_stage(
        functools.partial(back_kernel, G, R, Q, H, dh, buckets, fused),
        near_ins,
        far_ins,
        outs,
        far_outs,
        scratch,
        collective_id,
    )
    if not fused:
        out = scatter(G, R, far_ins["out_parts"].reshape(G, R, T, D), True, True, collective_id + 1)
        results.out = out + near_ins["middle"]
        total = jnp.concatenate([results.d_wide0, results.d_wide1, results.d_wide2], axis=1)
        total = lax.psum_scatter(total, "fsdp", scatter_dimension=0, tiled=True)
        total = lax.psum(total, "rep")
        results.d_wide0, results.d_wide1, results.d_wide2 = jnp.split(total, 3, axis=1)
    return results


def last_kernel(Q, H, dh, names, *refs):
    m = named(names, refs)
    m.o_gate[...] = m.d_gate[...]
    m.o_up[...] = m.d_up[...]
    m.o_down[...] = m.d_down[...]
    m.o_x[...] = m.d_x[...]
    m.o_out[...] = m.out[...]
    G, part = m.d_w.shape[1], m.d_w.shape[3]
    heads = H // G
    C = heads * dh
    Dn, D = m.self_query.shape
    for q in range(Q):
        rows = slice(q * part, (q + 1) * part)
        for o in range(G):
            m.o_sq[rows, o * C : (o + 1) * C] = m.d_w[q, o, 0, :, 2 * C :]
            for h in range(heads):
                both = m.d_w[q, o, 0, :, 2 * h * dh : 2 * (h + 1) * dh]
                span = slice((o * heads + h) * dh, (o * heads + h + 1) * dh)
                m.o_sk[rows, span] = both[:, :dh]
                m.o_sv[rows, span] = both[:, dh:]
        for h in range(H):
            both = m.d_ckv_w[q, 0, :, 2 * h * dh : 2 * (h + 1) * dh]
            m.o_ck[rows, h * dh : (h + 1) * dh] = both[:, :dh]
            m.o_cv[rows, h * dh : (h + 1) * dh] = both[:, dh:]
        m.o_so[rows, :] = m.d_wide0[q, 0]
        m.o_cq[rows, :] = m.d_wide1[q, 0]
        m.o_co[rows, :] = m.d_wide2[q, 0]

    def row_sums(a):
        ones = jnp.ones((8, a.shape[1]), F32)
        return lax.dot_general(
            ones, a, (((1,), (1,)), ((), ())), precision=lax.Precision.HIGHEST, preferred_element_type=F32
        )[:1]

    products = m.o_sq[...] * m.self_query[...] + m.o_sk[...] * m.self_key[...] + m.o_sv[...] * m.self_value[...]
    m.o_g_self[...] = row_sums(products)
    m.o_g_cross[...] = row_sums(m.o_cq[...] * m.cross_query[...])
    for ref in (m.o_sq, m.o_sk, m.o_sv):
        ref[...] = ref[...] * m.self_gain[...]
    m.o_cq[...] = m.o_cq[...] * m.cross_gain[...]
    n = m.d_enc.shape[0]
    m.o_enc[...] = jnp.concatenate([m.d_enc[o] for o in range(n)], axis=1)
    each = m.o_bias.shape[0]
    tiny_rows = m.tiny.shape[2]
    last = heads * each
    g_ffn = jnp.zeros((1, Dn), F32)
    bias = jnp.zeros((each, H), F32)
    row = lax.broadcasted_iota(jnp.int32, (tiny_rows, H), 0)
    column = lax.broadcasted_iota(jnp.int32, (tiny_rows, H), 1)
    to = lax.broadcasted_iota(jnp.int32, (each, tiny_rows), 0)
    of = lax.broadcasted_iota(jnp.int32, (each, tiny_rows), 1)
    pick = jnp.where(jnp.logical_and(of < last, lax.rem(of, each) == to), 1.0, 0.0)
    for o in range(G):
        total = m.tiny[0, o]
        for q in range(1, Q):
            total = total + m.tiny[q, o]
        g_ffn = g_ffn + total[last : last + 1, :Dn]
        sums = jnp.sum(total, axis=1, keepdims=True)
        held = jnp.logical_and(row < last, column == o * heads + row // each)
        bias = bias + lax.dot_general(
            pick,
            jnp.where(held, sums, 0.0),
            (((1,), (0,)), ((), ())),
            precision=lax.Precision.HIGHEST,
            preferred_element_type=F32,
        )
    m.o_g_ffn[...] = g_ffn
    m.o_bias[...] = bias


def last_stage(Q, H, dh, each, near_ins):
    Dn, D = near_ins["self_query"].shape
    enc_rows = near_ins["d_enc"].shape[1]
    near = dict(o_sq=(Dn, D), o_sk=(Dn, D), o_sv=(Dn, D), o_so=(Dn, D), o_cq=(Dn, D), o_ck=(Dn, D))
    near |= dict(o_cv=(Dn, D), o_co=(Dn, D), o_enc=(enc_rows, D), o_bias=(each, H))
    near |= dict(o_g_self=(1, Dn), o_g_cross=(1, Dn), o_g_ffn=(1, Dn))
    near |= dict(o_gate=near_ins["d_gate"].shape, o_up=near_ins["d_up"].shape)
    near |= dict(o_down=near_ins["d_down"].shape, o_x=near_ins["d_x"].shape, o_out=near_ins["out"].shape)
    return call_stage(functools.partial(last_kernel, Q, H, dh), near_ins, {}, near, {}, {}, None)


def shards(
    n,
    inputs,
    encoder,
    self_gain,
    cross_gain,
    ffn_gain,
    self_query,
    self_key,
    self_value,
    self_output,
    position_bias,
    bucket_table,
    cross_query,
    cross_key,
    cross_value,
    cross_output,
    ffn_gate,
    ffn_up,
    ffn_down,
    cotangent,
):
    x = inputs[0]
    enc = encoder[0]
    cot = cotangent[0]
    T, D = x.shape
    buckets, H = position_bias.shape
    dh = D // H
    G = math.gcd(H, n)
    R = n // G
    heads = H // G
    C = heads * dh
    Dn = D // n
    enc_local = enc.shape[0]
    Q = lax.axis_size("rep")
    part = Dn // Q
    gains = jnp.stack([self_gain, cross_gain])

    def quarters(w):
        return w.reshape(Q, part, D)

    near_ins = dict(
        x=x,
        enc=enc,
        ffn_gain=ffn_gain.reshape(1, Dn),
        position_bias=position_bias,
        table=bucket_table.reshape(1, -1),
        gains=gains.reshape(2, Q, part, 1),
        cross_key=cross_key,
        cross_value=cross_value,
        cot=cot.reshape(pieces, T // pieces, D),
    )
    far_ins = dict(
        self_query=quarters(self_query),
        self_key=quarters(self_key),
        self_value=quarters(self_value),
        so=quarters(self_output),
        cq_w=quarters(cross_query),
        co=quarters(cross_output),
    )
    first = first_stage(G, R, Q, H, dh, near_ins, far_ins, 1)
    dn3, out_parts, d_gate, d_up, d_down = ffn_stage(
        G, R, Q, first.n3, first.cot_all, ffn_gate, ffn_up, ffn_down, 3
    )
    near_ins = dict(vars(first), x=x, cot=cot, dn3=dn3)
    del near_ins["wide"], near_ins["cot_all"], near_ins["n3"]
    far_ins = dict(
        wide=first.wide, out_parts=out_parts, d_gate_in=d_gate, d_up_in=d_up, d_down_in=d_down
    )
    back = back_stage(G, R, Q, H, dh, buckets, near_ins, far_ins, 5)

    near_ins = dict(
        d_gate=back.d_gate.reshape(ffn_gate.shape),
        d_up=back.d_up.reshape(ffn_up.shape),
        d_down=back.d_down.reshape(ffn_down.shape),
        d_x=back.d_x,
        out=back.out.reshape(T, D),
        d_w=back.d_w,
        d_ckv_w=back.d_ckv_w,
        d_wide0=back.d_wide0.reshape(Q, 1, part, D),
        d_wide1=back.d_wide1.reshape(Q, 1, part, D),
        d_wide2=back.d_wide2.reshape(Q, 1, part, D),
        d_enc=back.d_enc,
        tiny=back.tiny,
        self_query=self_query,
        self_key=self_key,
        self_value=self_value,
        cross_query=cross_query,
        self_gain=self_gain.reshape(Dn, 1),
        cross_gain=cross_gain.reshape(Dn, 1),
    )
    done = last_stage(Q, H, dh, buckets // n, near_ins)
    return (
        done.o_out[None],
        done.o_x[None],
        done.o_enc[None],
        done.o_g_self.reshape(Dn),
        done.o_g_cross.reshape(Dn),
        done.o_g_ffn.reshape(Dn),
        done.o_sq,
        done.o_sk,
        done.o_sv,
        done.o_so,
        done.o_bias,
        done.o_cq,
        done.o_ck,
        done.o_cv,
        done.o_co,
        done.o_gate,
        done.o_up,
        done.o_down,
    )


def solution(mesh):
    rows = P("rep", "fsdp", None)
    gain = P("fsdp")
    weight = P("fsdp", None)
    columns = P(None, "fsdp")
    args = (rows, rows, gain, gain, gain) + (weight,) * 4 + (P(), P()) + (weight,) * 4
    args += (columns, columns, weight, rows)
    outs = (rows, rows, rows, gain, gain, gain) + (weight,) * 9 + (columns, columns, weight)
    return jax.shard_map(
        functools.partial(shards, mesh.shape["fsdp"]),
        mesh=mesh,
        in_specs=args,
        out_specs=outs,
        check_vma=False,
    )
```

```python
import functools
import math
from types import SimpleNamespace

import jax
import jax.numpy as jnp
from jax import lax
from jax.experimental import pallas as pl
from jax.experimental.pallas import tpu as pltpu
from jax.sharding import PartitionSpec as P

HIGH = lax.Precision.HIGH
MESH = pl.DeviceIdType.MESH
F32 = jnp.float32
eps_norm = 1e-06
gelu_coef = math.sqrt(2.0 / math.pi)
masked_score = -1e30
vmem_bytes = 62 << 20
pieces = 2


def mm(a, b):
    return jnp.dot(a, b, precision=HIGH, preferred_element_type=F32)


def mm_tn(a, b):
    return lax.dot_general(
        a, b, (((0,), (0,)), ((), ())), precision=HIGH, preferred_element_type=F32
    )


def mm_nt(a, b):
    return lax.dot_general(
        a, b, (((1,), (1,)), ((), ())), precision=HIGH, preferred_element_type=F32
    )


BF16 = jnp.bfloat16


def halves(a):
    high = a.astype(BF16)
    return high, (a - high.astype(F32)).astype(BF16)


def dot3(a, b, dims=(((1,), (0,)), ((), ()))):
    def dot(x, y):
        return lax.dot_general(x, y, dims, preferred_element_type=F32)

    return dot(a[0], b[0]) + (dot(a[0], b[1]) + dot(a[1], b[0]))


def unit_of(rows):
    scale = lax.rsqrt(jnp.mean(rows * rows, axis=-1, keepdims=True) + eps_norm)
    return rows * scale, scale


def unit_backward(grad_unit, unit, scale):
    return scale * (grad_unit - unit * jnp.mean(grad_unit * unit, axis=-1, keepdims=True))


def gelu_parts(gate_pre):
    squared = gate_pre * gate_pre
    tangent = jnp.tanh(gelu_coef * (gate_pre + 0.044715 * squared * gate_pre))
    gelu_out = 0.5 * gate_pre * (1.0 + tangent)
    gelu_slope = 0.5 * (1.0 + tangent) + 0.5 * gate_pre * (1.0 - tangent * tangent) * gelu_coef * (
        1.0 + 3.0 * 0.044715 * squared
    )
    return (gelu_out, gelu_slope)


def my_place(R):
    rep = lax.axis_index("rep")
    f = lax.axis_index("fsdp")
    return rep, f, f // R, lax.rem(f, R)


def greet(peers):
    barrier = pltpu.get_barrier_semaphore()
    for peer in peers:
        pl.semaphore_signal(barrier, inc=1, device_id=peer, device_id_type=MESH)
    pl.semaphore_wait(barrier, len(peers))


def remote(src, dst, send_sem, recv_sem, peer):
    return pltpu.make_async_remote_copy(
        src_ref=src,
        dst_ref=dst,
        send_sem=send_sem,
        recv_sem=recv_sem,
        device_id=peer,
        device_id_type=MESH,
    )


def lane_peers(rep, g, r, G, R):
    return [(rep, lax.rem(g + k, G) * R + r) for k in range(1, G)]


def group_peers(rep, g, r, G, R):
    return [(rep, g * R + lax.rem(r + j, R)) for j in range(1, R)]


def comm_call(kernel, outs, ins, scratch, collective_id, vmem_ins=False, vmem_outs=False):
    def space(vmem):
        return pl.BlockSpec(memory_space=pltpu.VMEM if vmem else pl.ANY)

    return pl.pallas_call(
        kernel,
        out_shape=outs,
        in_specs=[space(vmem_ins)] * len(ins),
        out_specs=[space(vmem_outs)] * len(outs),
        scratch_shapes=scratch,
        compiler_params=pltpu.CompilerParams(
            collective_id=collective_id, has_side_effects=True, vmem_limit_bytes=vmem_bytes
        ),
    )(*ins)


def scatter_kernel(G, R, pooled, summed, x_ref, o_ref, *scratch):
    rep, f, g, r = my_place(R)
    lanes = lane_peers(rep, g, r, G, R)
    groups = group_peers(rep, g, r, G, R) if pooled else []
    if pooled:
        group_buf, group_send, group_recv = scratch[:3]
        scratch = scratch[3:]
    lane_out, lane_in, lane_send, lane_recv = scratch
    greet(lanes + groups)
    order = list(range(G - 1, -1, -1))
    group_copies = []
    if pooled:
        for k in order:
            for j in range(1, R):
                copy = remote(
                    x_ref.at[lax.rem(g + k, G), lax.rem(r + j, R)],
                    group_buf.at[j - 1, k],
                    group_send.at[j - 1, k],
                    group_recv.at[j - 1, k],
                    groups[j - 1],
                )
                copy.start()
                group_copies.append((j, k, copy))
    lane_copies = []
    for k in order:
        to = lax.rem(g + k, G)
        if pooled:
            for j, kk, copy in group_copies:
                if kk == k:
                    copy.wait_recv()
            total = x_ref[to, r]
            for j in range(1, R):
                total = total + group_buf[j - 1, k]
        else:
            total = x_ref[to]
        if k > 0:
            lane_out[k - 1] = total
            copy = remote(
                lane_out.at[k - 1], lane_in.at[k - 1], lane_send.at[k - 1], lane_recv.at[k - 1], lanes[k - 1]
            )
            copy.start()
            lane_copies.append((k, copy))
        elif summed:
            o_ref[...] = total
        else:
            o_ref[g] = total
    for k, copy in lane_copies:
        copy.wait_recv()
        if summed:
            o_ref[...] += lane_in[k - 1]
        else:
            o_ref[lax.rem(g + G - k, G)] = lane_in[k - 1]
    for _, copy in lane_copies:
        copy.wait_send()
    for _, _, copy in group_copies:
        copy.wait_send()


def scatter(G, R, x, pooled, summed, collective_id):
    block = x.shape[2:] if pooled else x.shape[1:]
    sem = pltpu.SemaphoreType.DMA
    scratch = []
    if pooled:
        scratch = [
            pltpu.VMEM((max(R - 1, 1), G) + block, F32),
            sem((max(R - 1, 1), G)),
            sem((max(R - 1, 1), G)),
        ]
    scratch += [
        pltpu.VMEM((G - 1,) + block, F32),
        pltpu.VMEM((G - 1,) + block, F32),
        sem((G - 1,)),
        sem((G - 1,)),
    ]
    out = jax.ShapeDtypeStruct(block if summed else (G,) + block, F32)
    return comm_call(
        functools.partial(scatter_kernel, G, R, pooled, summed),
        [out],
        [x],
        scratch,
        collective_id,
        vmem_ins=True,
        vmem_outs=True,
    )[0]


def named(names, refs):
    return SimpleNamespace(**dict(zip(names, refs, strict=True)))


def first_kernel(G, R, Q, H, dh, names, *refs):
    m = named(names, refs)
    rep, f, g, r = my_place(R)
    n = G * R
    heads = H // G
    T, D = m.x.shape
    C = heads * dh
    loads = []
    for index, ref in enumerate((m.self_key, m.self_value, m.self_query, m.so, m.cq_w, m.co)):
        copy = pltpu.make_async_copy(ref.at[rep], m.w_in.at[index], m.load_sems.at[index])
        copy.start()
        loads.append(copy)
    greet(everyone(rep, f, n, Q))

    save, saves = mover(m.keep_sems)
    enc_rows = m.enc.shape[0]
    Dn = D // n
    small = Deal(n, m.small_parts, m.small_all, m.small_sems)
    weights = Spread(G, R, Q, lambda k: m.w_mine.at[lax.rem(g + k, G)], m.w, m.w_sems)
    wide = Spread(G, R, Q, lambda k: m.w_in.at[pl.ds(3, 3)], m.wide, m.wide_sems)
    chain = Chain(G, R, m.x_buf, m.x_sems)
    cot_chain = Chain(G, R, m.cot_all, m.cot_sems)
    ckv_sum = Reduce(G, R, *m.ckv_scratch)
    ckv_chain = Chain(G, R, m.ckv, m.ckv_chain_sems)
    for copy in loads:
        copy.wait()
    part = m.w_in.shape[1]
    self_gain = as_column(m.self_gain[...], rep * part, part)
    for o in range(G):
        for h in range(heads):
            span = slice((o * heads + h) * dh, (o * heads + h + 1) * dh)
            both = jnp.concatenate([m.w_in[0, :, span], m.w_in[1, :, span]], axis=1)
            m.w_mine[o, :, 2 * h * dh : 2 * (h + 1) * dh] = both * self_gain
        m.w_mine[o, :, 2 * C :] = m.w_in[2, :, o * C : (o + 1) * C] * self_gain
    m.w_in[4] = m.w_in[4] * as_column(m.cross_gain[...], rep * part, part)
    weights.start()
    m.x_buf[f] = m.x[...].reshape(pieces, T // pieces, D)
    chain.start()
    for o in range(n):
        m.small_parts[o, :enc_rows, :] = m.enc[:, o * Dn : (o + 1) * Dn]
        m.small_parts[o, enc_rows:, :] = jnp.broadcast_to(m.ffn_gain[...], (8, Dn))
    small.start()
    cot_own = pltpu.make_async_copy(m.cot, m.cot_all.at[f], m.cot_own_sem)
    cot_own.start()
    for h in range(H):
        span = slice(h * dh, (h + 1) * dh)
        both = jnp.concatenate([m.cross_key[:, span], m.cross_value[:, span]], axis=1)
        m.ckv_w[:, 2 * h * dh : 2 * (h + 1) * dh] = both
    bias_rows(G, heads, T, g, m)
    make_strips(R, heads, T, m.vec, m.strip)
    weights.across()
    wide.own_start()
    small.arrive()
    ckv_parts = ckv_sum.parts
    enc_cols = m.small_all[:, :enc_rows, :].reshape(n * enc_rows, Dn)
    ckv_parts[...] = mm(enc_cols, m.ckv_w[...]).reshape(ckv_parts.shape)
    gain = jnp.concatenate([m.small_all[s, enc_rows : enc_rows + 1, :] for s in range(n)], axis=1)
    m.gain[...] = gain
    for o in range(G):
        ckv_sum.offer(o)
    chain.forward(1)
    wide.lanes_start()
    weights.share()
    for o in range(G):
        ckv_sum.pooled(o)
    weights.arrive()
    chain.forward(2)
    save((m.w, m.w_far), (m.vec, m.vec_far), (m.ids, m.ids_far), (m.ckv_w, m.ckv_w_far))
    save((m.small_all, m.small_all_far), (m.gain, m.gain_far))
    w = m.w[...].reshape(D, 3 * C)
    for t in range(G):
        if t > 0:
            wide.across_from(G - t)
        if t == G - 1:
            for d in range(3, G):
                chain.forward(d)
        src = chain.settle(t)
        if t > 0:
            ckv_sum.hand_on(t - 1)
        unit, _ = unit_of(m.x_buf[pl.ds(src * R, R)].reshape(R * T, D))
        rows = pl.ds(pl.multiple_of(src * (R * T), R * T), R * T)
        m.unit[...] = unit
        mine = m.unit[pl.ds(pl.multiple_of(r * T, T), T), :]
        mine_rows = pl.ds(pl.multiple_of(src * T, T), T)
        m.own[mine_rows, :] = mine
        kv = mm(unit, w[:, : 2 * C])
        q = mm(mine, w[:, 2 * C :])
        for h in range(heads):
            m.kv[h, rows, :] = kv[:, 2 * h * dh : 2 * (h + 1) * dh]
            m.q[h, mine_rows, :] = beside(q[:, h * dh : (h + 1) * dh], 0)
    save((m.own, m.own_far), (m.q, m.q_far), (m.kv, m.kv_far))
    ckv_sum.collect(m.ckv.at[f])
    ckv_chain.start()
    cot_own.wait()
    cot_chain.start()
    for i in range(G):
        L = R * (i + 1) * T
        outs = []
        for h in range(heads):
            scores = strip_scores(R, T, i, r, h, L, m.kv, m.q, m.strip)
            top = jnp.max(scores, axis=0, keepdims=True)
            probs = jnp.exp(scores - top)
            total = jnp.sum(probs, axis=0, keepdims=True)
            out_t = mm_tn(m.kv[h, :L, :], probs)[dh:, :] / total
            outs.append(out_t.T)
            m.lse[i, h : h + 1, :] = top + jnp.log(total)
        m.att[i] = jnp.concatenate(outs, axis=1)
        lane_send(G, R, i, m.att, m.rows, m.att_sems)
        ckv_chain.arrive(i)
        if i > 0:
            wide.share_from(G + 1 - i if i > 1 else 0)
        if i == G - 2:
            cot_chain.arrive(0)
            cot_chain.arrive(1)
    save((m.att, m.att_far), (m.lse, m.lse_far), (m.ckv, m.ckv_far))
    wide.share_from(1)
    lane_wait(G, R, m.att, m.rows, m.att_sems)
    cot_chain.arrive(2)
    wide.arrive()
    save((m.rows, m.rows_far), (m.wide, m.wide_far))

    attended = jnp.concatenate([m.rows[i] for i in range(G)], axis=1)
    after = m.x[...] + mm(attended, m.wide[:, :, 0].reshape(D, D))
    m.after[...] = after
    unit_two, _ = unit_of(after)
    m.cq[...] = mm(unit_two, m.wide[:, :, 1].reshape(D, D))
    save((m.after, m.after_far), (m.cq, m.cq_far))
    enc_count = n * enc_rows
    for h in range(0, H, 2):
        outs = []
        for a in (h, h + 1):
            ckv = m.ckv[:, 0, :, 2 * a * dh : 2 * (a + 1) * dh].reshape(enc_count, 2 * dh)
            scores = mm_nt(ckv, beside(m.cq[:, a * dh : (a + 1) * dh], 0))
            probs = jnp.exp(scores - jnp.max(scores, axis=0, keepdims=True))
            probs = probs / jnp.sum(probs, axis=0, keepdims=True)
            m.probs[a] = probs
            outs.append(mm_tn(ckv, probs)[dh:, :].T)
        m.cflat[:, h * dh : (h + 2) * dh] = jnp.concatenate(outs, axis=1)
    save((m.cflat, m.cflat_far), (m.probs, m.probs_far))
    middle = after + mm(m.cflat[...], m.wide[:, :, 2].reshape(D, D))
    m.middle[...] = middle
    unit_three, _ = unit_of(middle)
    m.n3[...] = unit_three * gain
    save((m.middle, m.middle_far), (m.n3, m.n3_far))
    cot_chain.arrive(3)

    small.finish()
    weights.finish()
    chain.finish()
    cot_chain.finish()
    ckv_sum.finish()
    ckv_chain.finish()
    wide.finish()
    wait_all(saves)


def as_column(row, start, count):
    n = row.shape[1]
    at = lax.broadcasted_iota(jnp.int32, (count, n), 0) + start
    pick = jnp.where(at == lax.broadcasted_iota(jnp.int32, (count, n), 1), 1.0, 0.0)
    return jnp.sum(pick * row, axis=1, keepdims=True)


def bias_rows(G, heads, T, g, m):
    buckets = m.position_bias.shape[1]
    late, early = m.table[:, T : 2 * T], m.table[:, :T]
    row = jnp.concatenate([late, jnp.zeros_like(late), early], axis=1)
    lane = lax.broadcasted_iota(jnp.int32, (1, 3 * T), 1)
    after = jnp.logical_and(lane >= T, lane < 2 * T)
    m.ids[...] = jnp.broadcast_to(jnp.where(after, -1, row).astype(F32), m.ids.shape)
    bucket = lax.broadcasted_iota(jnp.int32, (buckets, 3 * T), 0)
    onehot = jnp.where(bucket == row, 1.0, 0.0)
    bias = m.position_bias[...]
    every = lax.dot_general(
        bias - bias[:, buckets - 1 :],
        onehot,
        (((1,), (0,)), ((), ())),
        precision=lax.Precision.HIGHEST,
        preferred_element_type=F32,
    )
    every = jnp.where(after, masked_score, every)
    m.vec[...] = jnp.zeros_like(m.vec)
    for h in range(heads):
        one = every[h : h + 1]
        for i in range(1, G):
            one = jnp.where(g == i, every[i * heads + h : i * heads + h + 1], one)
        m.vec[h : h + 1, :] = one


def beside(a, at):
    zero = jnp.zeros_like(a)
    return jnp.concatenate([zero, a] if at else [a, zero], axis=1)


def lane_send(G, R, i, src_ref, dst_ref, sems):
    rep, f, g, r = my_place(R)

    @pl.when(g == i)
    def _():
        pltpu.make_async_copy(src_ref.at[i], dst_ref.at[i], sems[2]).start()

    @pl.when(g != i)
    def _():
        remote(src_ref.at[i], dst_ref.at[g], sems[0].at[i], sems[1].at[g], (rep, i * R + r)).start()


def lane_wait(G, R, src_ref, dst_ref, sems):
    rep, f, g, r = my_place(R)
    pltpu.make_async_copy(src_ref.at[g], dst_ref.at[g], sems[2]).wait()
    for i in range(G):

        @pl.when(g != i)
        def _():
            copy = remote(src_ref.at[i], dst_ref.at[i], sems[0].at[i], sems[1].at[i], (rep, i * R + r))
            copy.wait_send()
            copy.wait_recv()


def lane_sems(G):
    sem = pltpu.SemaphoreType.DMA
    return (sem((G,)), sem((G,)), sem)


class Spread:
    def __init__(self, G, R, Q, source, out, sems):
        self.sizes = (G, R, Q)
        self.source, self.out, self.sems = source, out, sems
        rep, f, g, r = my_place(R)
        self.place = (rep, f, g, r)
        self.lanes = lane_peers(rep, g, r, G, R)
        self.groups = group_peers(rep, g, r, G, R)
        self.reps = [(lax.rem(rep + j, Q), f) for j in range(1, Q)]

    def slot(self, k):
        G, R, Q = self.sizes
        _, _, g, r = self.place
        return lax.rem(g + G - k, G) * R + r

    def lane_copy(self, k):
        rep, f = self.place[:2]
        return remote(
            self.source(k), self.out.at[f, rep], self.sems[0].at[k - 1], self.sems[1].at[k - 1], self.lanes[k - 1]
        )

    def rep_copy(self, k, j):
        part = self.out.at[self.slot(k), self.place[0]]
        return remote(part, part, self.sems[2].at[k, j - 1], self.sems[3].at[k, j - 1], self.reps[j - 1])

    def group_copy(self, k, j):
        part = self.out.at[self.slot(k)]
        return remote(part, part, self.sems[4].at[k, j - 1], self.sems[5].at[k, j - 1], self.groups[j - 1])

    def start(self):
        self.lanes_start()
        self.own_start()

    def lanes_start(self):
        for k in range(self.sizes[0] - 1, 0, -1):
            self.lane_copy(k).start()

    def own_start(self):
        rep, f = self.place[:2]
        self.out[f, rep] = self.source(0)[...]
        for j in range(1, self.sizes[2]):
            self.rep_copy(0, j).start()

    def across_from(self, k):
        self.lane_copy(k).wait_recv()
        for j in range(1, self.sizes[2]):
            self.rep_copy(k, j).start()

    def across(self):
        for k in range(1, self.sizes[0]):
            self.across_from(k)

    def share_from(self, k):
        for j in range(1, self.sizes[2]):
            self.rep_copy(k, j).wait_recv()
        for j in range(1, self.sizes[1]):
            self.group_copy(k, j).start()

    def share(self):
        for k in range(self.sizes[0]):
            self.share_from(k)

    def arrive(self):
        G, R, Q = self.sizes
        for k in range(G):
            for j in range(1, R):
                self.group_copy(k, j).wait_recv()

    def finish(self):
        G, R, Q = self.sizes
        for k in range(G):
            if k > 0:
                self.lane_copy(k).wait_send()
            for j in range(1, Q):
                self.rep_copy(k, j).wait_send()
            for j in range(1, R):
                self.group_copy(k, j).wait_send()


class Deal:
    def __init__(self, n, parts, out, sems):
        self.n, self.parts, self.out, self.sems = n, parts, out, sems
        self.rep, self.f = lax.axis_index("rep"), lax.axis_index("fsdp")

    def copy(self, k):
        to = lax.rem(self.f + k, self.n)
        return remote(
            self.parts.at[to],
            self.out.at[self.f],
            self.sems[0].at[k - 1],
            self.sems[1].at[k - 1],
            (self.rep, to),
        )

    def start(self):
        for k in range(1, self.n):
            self.copy(k).start()
        self.out[self.f] = self.parts[self.f]

    def arrive(self):
        for k in range(1, self.n):
            self.copy(k).wait_recv()

    def finish(self):
        for k in range(1, self.n):
            self.copy(k).wait_send()


def deal_sems(n):
    sem = pltpu.SemaphoreType.DMA
    return (sem((n - 1,)), sem((n - 1,)))


def everyone(rep, f, n, Q):
    return [(rep, lax.rem(f + k, n)) for k in range(1, n)] + [
        (lax.rem(rep + j, Q), f) for j in range(1, Q)
    ]


def spread_sems(G, R, Q):
    sem = pltpu.SemaphoreType.DMA
    return (
        sem((G - 1,)),
        sem((G - 1,)),
        sem((G, Q - 1)),
        sem((G, Q - 1)),
        sem((G, R - 1)),
        sem((G, R - 1)),
    )


def lookup(table, i, t):
    rows, columns = len(table), len(table[0])
    flat = i * columns + t
    value = table[0][0] + 0 * flat
    for a in range(rows):
        for b in range(columns):
            if table[a][b] != table[0][0]:
                value = jnp.where(flat == a * columns + b, table[a][b], value)
    return value


class Chain:
    def __init__(self, G, R, buf, sems):
        self.G, self.R, self.buf, self.sems = G, R, buf, sems
        self.pieces = buf.shape[1]
        self.rep, self.f, self.g, self.r = my_place(R)
        self.groups = group_peers(self.rep, self.g, self.r, G, R)
        self.order, self.first, self.second = [], [], []
        for i in range(G):
            order = sorted(range(G), key=lambda s: (abs(s - i), s))
            self.order.append(order)
            far = [abs(s - i) for s in order]
            fresh = [t > 0 and far[t] != far[t - 1] for t in range(G)]
            paired = [fresh[t] and t + 1 < G and far[t + 1] == far[t] for t in range(G)]
            self.first.append([order[t] if fresh[t] else -1 for t in range(G)])
            self.second.append([order[t + 1] if paired[t] else -1 for t in range(G)])

    def part(self, src, p):
        return self.buf.at[src * self.R + self.r, p]

    def step(self, src, side, p):
        part = self.part(src, p)
        to = (self.rep, (self.g + side) * self.R + self.r)
        way = 0 if side > 0 else 1
        return remote(part, part, self.sems[0].at[way, src, p], self.sems[1].at[src, p], to)

    def group_copy(self, src, j, p):
        part = self.part(src, p)
        return remote(
            part, part, self.sems[2].at[j - 1, src, p], self.sems[3].at[j - 1, src, p], self.groups[j - 1]
        )

    def sends(self, src):
        right = jnp.logical_and(src <= self.g, self.g < self.G - 1)
        left = jnp.logical_and(src >= self.g, self.g > 0)
        return ((1, right), (-1, left))

    def onward(self, src, p):
        for side, cond in self.sends(src):

            @pl.when(cond)
            def _():
                self.step(src, side, p).start()

        for j in range(1, self.R):
            self.group_copy(src, j, p).start()

    def start(self):
        for p in range(self.pieces):
            self.onward(self.g, p)

    def forward(self, d):
        for src in (self.g - d, self.g + d):

            @pl.when(jnp.logical_and(src >= 0, src < self.G))
            def _():
                for p in range(self.pieces):
                    self.step(src, 1, p).wait_recv()
                    self.onward(src, p)

    def settle(self, t):
        src = lookup(self.order, self.g, t)
        for j in range(1, self.R):
            for p in range(self.pieces):
                self.group_copy(src, j, p).wait_recv()
        return src

    def arrive(self, t):
        for table in (self.first, self.second):
            came = lookup(table, self.g, t)

            @pl.when(came >= 0)
            def _():
                for p in range(self.pieces):
                    self.step(came, 1, p).wait_recv()
                    self.onward(came, p)

        return self.settle(t)

    def finish(self):
        for src in range(self.G):
            for p in range(self.pieces):
                for side, cond in self.sends(src):

                    @pl.when(cond)
                    def _():
                        self.step(src, side, p).wait_send()

                for j in range(1, self.R):
                    self.group_copy(src, j, p).wait_send()


def chain_sems(G, R, pieces):
    sem = pltpu.SemaphoreType.DMA
    return (sem((2, G, pieces)), sem((G, pieces)), sem((R - 1, G, pieces)), sem((R - 1, G, pieces)))


def make_strips(R, heads, T, vec_ref, strip_ref):
    for h in range(heads):
        vec = jnp.broadcast_to(vec_ref[h : h + 1, :], (2 * T, 3 * T))
        pair = pltpu.roll(vec, 0, 1, stride=1, stride_axis=0)[:, :T]
        if R > 1:
            strip_ref[h, : (R - 1) * T, :] = jnp.zeros(((R - 1) * T, T), F32)
            strip_ref[h, (R + 1) * T :, :] = jnp.full(((R - 1) * T, T), masked_score, F32)
        strip_ref[h, (R - 1) * T : (R + 1) * T, :] = pair


def strip_scores(R, T, i, r, h, L, kv_ref, q_ref, strip_ref):
    scores = mm_nt(kv_ref[h, :L, :], q_ref[h, i * T : (i + 1) * T, :])
    skip = 1 if i == 0 else 0
    width = (R + 1 - skip) * T
    start = pl.multiple_of((R - 1 - r + skip) * T, T)
    near = scores[L - width :, :] + strip_ref[h, pl.ds(start, width), :]
    if width == L:
        return near
    return jnp.concatenate([scores[: L - width, :], near], axis=0)


def mover(sems):
    started = []

    def start(*pairs):
        batch = []
        for src, dst in pairs:
            batch.append(pltpu.make_async_copy(src, dst, sems.at[len(started)]))
            batch[-1].start()
            started.append(batch[-1])
        return batch

    return start, started


def wait_all(copies):
    for copy in copies:
        copy.wait()


def call_stage(
    kernel, near_ins, far_ins, near_outs, far_outs, scratch, collective_id, fetched=None, kept=None
):
    vm = pl.BlockSpec(memory_space=pltpu.VMEM)
    hbm = pl.BlockSpec(memory_space=pl.ANY)
    fetched, kept = fetched or {}, kept or {}
    outs = near_outs | far_outs | kept
    names = tuple(near_ins) + tuple(far_ins) + tuple(f"{k}_far" for k in fetched)
    names += tuple(near_outs) + tuple(far_outs) + tuple(f"{k}_far" for k in kept)
    scratch = dict(scratch)
    scratch |= {k: pltpu.VMEM(value.shape, value.dtype) for k, value in fetched.items()}
    scratch |= {k: pltpu.VMEM(shape, F32) for k, shape in kept.items()}
    if fetched:
        scratch |= dict(fetch_sems=pltpu.SemaphoreType.DMA((len(fetched),)))
    if kept:
        scratch |= dict(keep_sems=pltpu.SemaphoreType.DMA((len(kept),)))
    names += tuple(scratch)
    results = pl.pallas_call(
        functools.partial(kernel, names),
        out_shape=[jax.ShapeDtypeStruct(shape, F32) for shape in outs.values()],
        in_specs=[vm] * len(near_ins) + [hbm] * (len(far_ins) + len(fetched)),
        out_specs=[vm] * len(near_outs) + [hbm] * (len(far_outs) + len(kept)),
        scratch_shapes=list(scratch.values()),
        compiler_params=pltpu.CompilerParams(
            collective_id=collective_id,
            has_side_effects=collective_id is not None,
            vmem_limit_bytes=vmem_bytes,
        ),
    )(*near_ins.values(), *far_ins.values(), *fetched.values())
    return named(tuple(outs), results)


def first_stage(G, R, Q, H, dh, near_ins, far_ins, collective_id):
    T, D = near_ins["x"].shape
    n = G * R
    S = n * T
    heads = H // G
    C = heads * dh
    enc_rows = near_ins["enc"].shape[0]
    part = D // n // Q
    block = (pieces, T // pieces, D)
    outs = dict(
        att=(G, T, C),
        rows=(G, T, C),
        q=(heads, G * T, 2 * dh),
        kv=(heads, S, 2 * dh),
        lse=(G, 8, T),
        w=(n, Q, part, 3 * C),
        own=(G * T, D),
        small_all=(n, enc_rows + 8, D // n),
        vec=(8, 3 * T),
        ids=(8, 3 * T),
        ckv_w=(D // n, 2 * D),
        ckv=(n, 1, enc_rows, 2 * D),
        gain=(1, D),
        after=(T, D),
        middle=(T, D),
        n3=(T, D),
        cq=(T, D),
        cflat=(T, D),
        probs=(H, n * enc_rows, T),
        wide=(n, Q, 3, part, D),
    )
    far_outs = dict(cot_all=(n,) + block)
    scratch = dict(
        x_buf=pltpu.VMEM((n,) + block, F32),
        unit=pltpu.VMEM((R * T, D), F32),
        strip=pltpu.VMEM((heads, 2 * R * T, T), F32),
        x_sems=chain_sems(G, R, pieces),
        cot_sems=chain_sems(G, R, pieces),
        cot_own_sem=pltpu.SemaphoreType.DMA,
        w_in=pltpu.VMEM((6, part, D), F32),
        w_mine=pltpu.VMEM((G, part, 3 * C), F32),
        small_parts=pltpu.VMEM((n, enc_rows + 8, D // n), F32),
        load_sems=pltpu.SemaphoreType.DMA((6,)),
        w_sems=spread_sems(G, R, Q),
        wide_sems=spread_sems(G, R, Q),
        att_sems=lane_sems(G),
        small_sems=deal_sems(n),
        ckv_scratch=tuple(reduce_scratch(G, R, 1, (enc_rows, 2 * D))),
        ckv_chain_sems=chain_sems(G, R, 1),
    )
    return call_stage(
        functools.partial(first_kernel, G, R, Q, H, dh),
        near_ins,
        far_ins,
        {},
        far_outs,
        scratch,
        collective_id,
        kept=outs,
    )


class Reduce:
    def __init__(self, G, R, parts, pool, inbox, sems, mode="near"):
        self.G, self.parts, self.pool, self.inbox, self.sems = G, parts, pool, inbox, sems
        self.pieces = parts.shape[2]
        self.rep, self.f, self.g, self.r = my_place(R)
        self.stride = R
        self.R = R if pool is not None else 1
        self.mine = self.r if pool is not None else 0
        self.groups = group_peers(self.rep, self.g, self.r, G, R)
        orders = []
        for g in range(G):
            due = {o: o + g if o > g else (G - 1 - o) + (G - 1 - g) for o in range(G) if o != g}
            if mode == "far":
                due = {o: G - 1 - o + g if o > g else o + G - 1 - g for o in due}
            held = [o for o in due if (g > 0 if o > g else g < G - 1)]
            orders.append((sorted(held, key=lambda o: due[o]) + [-1] * G)[: G - 1])
        self.orders = orders
        self.far_first = [sorted(range(G), key=lambda o: -abs(o - i)) for i in range(G)]

    def group_copy(self, o, j, p):
        other = lax.rem(self.r + j, self.R)
        return remote(
            self.parts.at[o, other, p],
            self.pool.at[j - 1, o, p],
            self.sems[0].at[j - 1, o, p],
            self.sems[1].at[j - 1, o, p],
            self.groups[j - 1],
        )

    def lane_copy(self, o, p):
        right = o > self.g
        to = jnp.where(right, self.g + 1, self.g - 1)
        last_left = jnp.logical_and(jnp.logical_not(right), to == o)
        slot = jnp.where(last_left, self.G, o)
        part = self.parts.at[o, self.mine, p]
        peer = (self.rep, to * self.stride + self.r)
        return remote(part, self.inbox.at[slot, p], self.sems[2].at[o, p], self.sems[3].at[slot, p], peer)

    def inbox_wait(self, slot, p):
        remote(
            self.parts.at[0, self.mine, p],
            self.inbox.at[slot, p],
            self.sems[2].at[0, p],
            self.sems[3].at[slot, p],
            (self.rep, self.f),
        ).wait_recv()

    def offer(self, o):
        for p in range(self.pieces):
            for j in range(1, self.R):
                self.group_copy(o, j, p).start()

    def pooled(self, o):
        first = jnp.logical_or(
            jnp.logical_and(o > self.g, self.g == 0),
            jnp.logical_and(o < self.g, self.g == self.G - 1),
        )
        for p in range(self.pieces):
            for j in range(1, self.R):
                self.group_copy(o, j, p).wait_recv()
            if self.R > 1:
                total = self.parts[o, self.mine, p]
                for j in range(1, self.R):
                    total = total + self.pool[j - 1, o, p]
                self.parts[o, self.mine, p] = total

            @pl.when(first)
            def _():
                self.lane_copy(o, p).start()

    def hand_on(self, index):
        o = lookup(self.orders, self.g, index)

        @pl.when(o >= 0)
        def _():
            for p in range(self.pieces):
                self.inbox_wait(o, p)
                self.parts[o, self.mine, p] += self.inbox[o, p]
                self.lane_copy(o, p).start()

    def collect(self, out):
        for p in range(self.pieces):
            out[p] = self.parts[self.g, self.mine, p]

        for cond, slot in ((self.g > 0, self.g), (self.g < self.G - 1, self.G)):

            @pl.when(cond)
            def _():
                for p in range(self.pieces):
                    self.inbox_wait(slot, p)
                    out[p] += self.inbox[slot, p]

    def finish(self):
        for o in range(self.G):
            for p in range(self.pieces):
                for j in range(1, self.R):
                    self.group_copy(o, j, p).wait_send()

            @pl.when(self.g != o)
            def _():
                for p in range(self.pieces):
                    self.lane_copy(o, p).wait_send()


def reduce_scratch(G, R, pieces, block):
    sem = pltpu.SemaphoreType.DMA
    block = (pieces, block[0] // pieces) + block[1:]
    return [
        pltpu.VMEM((G, R) + block, F32),
        pltpu.VMEM((R - 1, G) + block if R > 1 else (8, 128), F32),
        pltpu.VMEM((G + 1,) + block, F32),
        (sem((max(R - 1, 1), G, pieces)), sem((max(R - 1, 1), G, pieces)), sem((G, pieces)), sem((G + 1, pieces))),
    ]


def ffn_kernel(
    G,
    R,
    n3_ref,
    cot_far,
    gate_far,
    up_far,
    down_far,
    dn3_ref,
    out_far,
    d_gate_ref,
    d_up_ref,
    d_down_ref,
    gate_parts,
    up_parts,
    down_parts,
    gate_in,
    up_in,
    down_in,
    rep_sems,
    cot_ref,
    gate_ref,
    up_ref,
    down_ref,
    out_ref,
    fetch_sems,
    out_sems,
    n3_buf,
    n3_high,
    n3_low,
    inner_high,
    inner_low,
    grads_high,
    grads_low,
    wide_high,
    wide_low,
    tall_high,
    tall_low,
    dn3_parts,
    dn3_pool,
    dn3_inbox,
    dn3_sems,
    n3_sems,
):
    rep, f, g, r = my_place(R)
    T, D = n3_ref.shape
    F = gate_ref.shape[1]
    rows_each = R * T
    block = (R, pieces, T // pieces, D)
    Q = gate_parts.shape[0]
    fetch, _ = mover(fetch_sems)
    weights = fetch((gate_far, gate_ref), (up_far, up_ref), (down_far, down_ref))
    cot_fetch = fetch((cot_far, cot_ref))
    greet(lane_peers(rep, g, r, G, R) + group_peers(rep, g, r, G, R) + everyone(rep, f, 1, Q))
    sums = [
        (gate_parts, gate_in, d_gate_ref),
        (up_parts, up_in, d_up_ref),
        (down_parts, down_in, d_down_ref),
    ]

    def rep_copy(a, j):
        to = lax.rem(rep + j, Q)
        sems = rep_sems[0].at[a, j - 1], rep_sems[1].at[a, j - 1]
        return remote(sums[a][0].at[to], sums[a][1].at[j - 1], *sems, (to, f))

    def to_replicas(a, value):
        sums[a][0][...] = value.reshape(sums[a][0].shape)
        for j in range(1, Q):
            rep_copy(a, j).start()

    chain = Chain(G, R, n3_buf, n3_sems)
    d_three = Reduce(G, R, dn3_parts, dn3_pool, dn3_inbox, dn3_sems)
    n3_buf[f] = n3_ref[...].reshape(pieces, T // pieces, D)
    chain.start()
    wait_all(weights)
    for index, ref in enumerate((gate_ref, up_ref, down_ref)):
        high, low = halves(ref[...])
        span = slice(index * F, (index + 1) * F)
        wide = index < 2
        wide_high[:, span] = high if wide else high.T
        wide_low[:, span] = low if wide else low.T
        tall_high[span, :] = high.T if wide else high
        tall_low[span, :] = low.T if wide else low
    wait_all(cot_fetch)

    @pl.loop(0, G)
    def _(t):
        src = chain.arrive(t)
        rows = pl.ds(pl.multiple_of(src * rows_each, rows_each), rows_each)
        n3 = halves(n3_buf[pl.ds(src * R, R)].reshape(rows_each, D))
        n3_high[rows, :], n3_low[rows, :] = n3
        pre = dot3(n3, (wide_high[:, : 2 * F], wide_low[:, : 2 * F]))
        gate_pre, up_pre = pre[:, :F], pre[:, F:]
        gelu_out, gelu_slope = gelu_parts(gate_pre)
        inner = halves(gelu_out * up_pre)
        inner_high[rows, :], inner_low[rows, :] = inner
        cot = halves(cot_ref[pl.ds(src * R, R)].reshape(rows_each, D))
        grad_inner = dot3(cot, (wide_high[:, 2 * F :], wide_low[:, 2 * F :]))
        grads = halves(
            jnp.concatenate([grad_inner * up_pre * gelu_slope, grad_inner * gelu_out], axis=1)
        )
        grads_high[rows, :], grads_low[rows, :] = grads
        dn3 = dot3(grads, (tall_high[: 2 * F, :], tall_low[: 2 * F, :]))
        dn3_parts[src] = dn3.reshape(block)
        d_three.offer(src)
        out = dot3(inner, (tall_high[2 * F :, :], tall_low[2 * F :, :]))
        out_ref[src] = out.reshape(block)
        pltpu.make_async_copy(out_ref.at[src], out_far.at[src], out_sems.at[src]).start()
        d_three.pooled(src)

    S = G * rows_each
    tn = (((0,), (0,)), ((), ()))
    n3 = (n3_high[...], n3_low[...])
    to_replicas(0, dot3(n3, (grads_high[:, :F], grads_low[:, :F]), tn))
    d_three.hand_on(0)
    to_replicas(1, dot3(n3, (grads_high[:, F:], grads_low[:, F:]), tn))
    d_three.hand_on(1)
    cot = halves(cot_ref[...].reshape(S, D))
    to_replicas(2, dot3((inner_high[...], inner_low[...]), cot, tn))
    for index in range(2, G - 1):
        d_three.hand_on(index)
    d_three.collect(dn3_ref)
    for a in range(3):
        total = sums[a][0][rep]
        for j in range(1, Q):
            rep_copy(a, j).wait_recv()
            total = total + sums[a][1][j - 1]
        sums[a][2][...] = total
        for j in range(1, Q):
            rep_copy(a, j).wait_send()
    chain.finish()
    d_three.finish()
    for o in range(G):
        pltpu.make_async_copy(out_ref.at[o], out_far.at[o], out_sems.at[o]).wait()


def ffn_stage(G, R, Q, n3, cot, gate, up, down, collective_id):
    T, D = n3.shape
    F = gate.shape[1]
    n = G * R
    S = n * T
    vm = pl.BlockSpec(memory_space=pltpu.VMEM)
    hbm = pl.BlockSpec(memory_space=pl.ANY)
    block = (pieces, T // pieces, D)
    shape = lambda *dims: jax.ShapeDtypeStruct(dims, F32)
    dn3, out, d_gate, d_up, d_down = pl.pallas_call(
        functools.partial(ffn_kernel, G, R),
        out_shape=[
            shape(*block),
            shape(G, R, *block),
            shape(D // Q, F),
            shape(D // Q, F),
            shape(F // Q, D),
        ],
        in_specs=[vm] + [hbm] * 4,
        out_specs=[vm, hbm] + [vm] * 3,
        scratch_shapes=[
            pltpu.VMEM((Q, D // Q, F), F32),
            pltpu.VMEM((Q, D // Q, F), F32),
            pltpu.VMEM((Q, F // Q, D), F32),
            pltpu.VMEM((Q - 1, D // Q, F), F32),
            pltpu.VMEM((Q - 1, D // Q, F), F32),
            pltpu.VMEM((Q - 1, F // Q, D), F32),
            (pltpu.SemaphoreType.DMA((3, Q - 1)), pltpu.SemaphoreType.DMA((3, Q - 1))),
            pltpu.VMEM((n,) + block, F32),
            pltpu.VMEM((D, F), F32),
            pltpu.VMEM((D, F), F32),
            pltpu.VMEM((F, D), F32),
            pltpu.VMEM((G, R) + block, F32),
            pltpu.SemaphoreType.DMA((4,)),
            pltpu.SemaphoreType.DMA((G,)),
            pltpu.VMEM((n,) + block, F32),
            pltpu.VMEM((S, D), BF16),
            pltpu.VMEM((S, D), BF16),
            pltpu.VMEM((S, F), BF16),
            pltpu.VMEM((S, F), BF16),
            pltpu.VMEM((S, 2 * F), BF16),
            pltpu.VMEM((S, 2 * F), BF16),
            pltpu.VMEM((D, 3 * F), BF16),
            pltpu.VMEM((D, 3 * F), BF16),
            pltpu.VMEM((3 * F, D), BF16),
            pltpu.VMEM((3 * F, D), BF16),
        ]
        + reduce_scratch(G, R, pieces, (T, D))
        + [chain_sems(G, R, pieces)],
        compiler_params=pltpu.CompilerParams(
            collective_id=collective_id, has_side_effects=True, vmem_limit_bytes=vmem_bytes
        ),
    )(n3, cot, gate, up, down)
    return dn3.reshape(T, D), out, d_gate, d_up, d_down


class Fold:
    def __init__(self, G, R, Q, scratch, out, summed):
        self.G, self.R, self.Q = G, R, Q
        self.parts, self.pool, self.rep_in, self.lane_out, self.lane_in, self.sems = scratch
        self.A = self.parts.shape[0]
        self.out, self.summed = out, summed
        self.rep, self.f, self.g, self.r = my_place(R)
        self.groups = group_peers(self.rep, self.g, self.r, G, R)
        self.lanes = lane_peers(self.rep, self.g, self.r, G, R)
        self.to_rep = [lax.rem(self.rep + j, Q) for j in range(1, Q)]
        if G * R == 1:
            self.g = self.r = 0

    def group_copy(self, a, o, j):
        return remote(
            self.parts.at[a, o, lax.rem(self.r + j, self.R)],
            self.pool.at[j - 1, a, o],
            self.sems[0].at[j - 1, a, o],
            self.sems[1].at[j - 1, a, o],
            self.groups[j - 1],
        )

    def rep_copy(self, o, j):
        return remote(
            self.parts.at[:, o, self.r, self.to_rep[j - 1]],
            self.rep_in.at[j - 1, o],
            self.sems[2].at[j - 1, o],
            self.sems[3].at[j - 1, o],
            (self.to_rep[j - 1], self.f),
        )

    def lane_copy(self, k):
        return remote(
            self.lane_out.at[k],
            self.lane_in.at[k - 1],
            self.sems[4].at[k - 1],
            self.sems[5].at[k - 1],
            self.lanes[k - 1],
        )

    def back_copy(self, j):
        part = self.out.at[self.rep]
        return remote(
            part, part, self.sems[6].at[j - 1], self.sems[7].at[j - 1], (self.to_rep[j - 1], self.f)
        )

    def to_group(self, a):
        for o in range(self.G):
            for j in range(1, self.R):
                self.group_copy(a, o, j).start()

    def to_replicas(self):
        for o in range(self.G):
            for a in range(self.A):
                for j in range(1, self.R):
                    self.group_copy(a, o, j).wait_recv()
                    self.parts[a, o, self.r] += self.pool[j - 1, a, o]
            for j in range(1, self.Q):
                self.rep_copy(o, j).start()

    def to_owner(self):
        for k in range(self.G - 1, -1, -1):
            o = lax.rem(self.g + k, self.G)
            for j in range(1, self.Q):
                self.rep_wait(o, j)
            total = self.parts[:, o, self.r, self.rep]
            for j in range(1, self.Q):
                total = total + self.rep_in[j - 1, o]
            self.lane_out[k] = total
            if k > 0:
                self.lane_copy(k).start()

    def rep_wait(self, o, j):
        self.rep_copy(o, j).wait_recv()

    def to_everyone(self):
        if self.summed:
            total = self.lane_out[0]
            for k in range(1, self.G):
                self.lane_copy(k).wait_recv()
                total = total + self.lane_in[k - 1]
            self.out[self.rep] = total
        else:
            self.out[self.rep, self.g] = self.lane_out[0]
            for k in range(1, self.G):
                self.lane_copy(k).wait_recv()
                self.out[self.rep, lax.rem(self.g + self.G - k, self.G)] = self.lane_in[k - 1]
        for j in range(1, self.Q):
            self.back_copy(j).start()

    def finish(self):
        for j in range(1, self.Q):
            self.back_copy(j).wait()
        for o in range(self.G):
            for a in range(self.A):
                for j in range(1, self.R):
                    self.group_copy(a, o, j).wait_send()
            for j in range(1, self.Q):
                self.rep_copy(o, j).wait_send()
        for k in range(1, self.G):
            self.lane_copy(k).wait_send()


def fold_scratch(A, G, R, Q, m, W):
    sem = pltpu.SemaphoreType.DMA
    some, lanes = max(R - 1, 1), max(G - 1, 1)
    return (
        pltpu.VMEM((A, G, R, Q, m, W), F32),
        pltpu.VMEM((some, A, G, Q, m, W) if R > 1 else (1, 1, 1, 1, 8, 128), F32),
        pltpu.VMEM((Q - 1, G, A, m, W), F32),
        pltpu.VMEM((G, A, m, W), F32),
        pltpu.VMEM((lanes, A, m, W), F32),
        (
            sem((some, A, G)),
            sem((some, A, G)),
            sem((Q - 1, G)),
            sem((Q - 1, G)),
            sem((lanes,)),
            sem((lanes,)),
            sem((Q - 1,)),
            sem((Q - 1,)),
        ),
    )


def back_kernel(G, R, Q, H, dh, buckets, fused, names, *refs):
    m = named(names, refs)
    rep, f, g, r = my_place(R)
    n = G * R
    heads = H // G
    T, D = m.x.shape
    C = heads * dh
    Dn = D // n
    groups = group_peers(rep, g, r, G, R)
    reps = [(lax.rem(rep + j, Q), f) for j in range(1, Q)]
    fetch, _ = mover(m.fetch_sems)
    ones = fetch((m.dn3_far, m.dn3), (m.middle_far, m.middle), (m.cot_far, m.cot), (m.gain_far, m.gain))

    def load(a):
        return pltpu.make_async_copy(m.wide.at[:, :, a], m.weight, m.load_sem)

    load(2).start()
    if fused:
        load_out = pltpu.make_async_copy(m.out_parts, m.out_scratch[0], m.out_sem)
        load_out.start()
    twos = fetch((m.ckv_far, m.ckv), (m.probs_far, m.probs), (m.cq_far, m.cq), (m.cflat_far, m.cflat))
    twos += fetch((m.after_far, m.after), (m.rows_far, m.rows), (m.vec_far, m.vec), (m.ids_far, m.ids))
    threes = fetch((m.kv_far, m.kv), (m.q_far, m.q), (m.lse_far, m.lse), (m.att_far, m.att))
    fours = fetch((m.w_far, m.w), (m.own_far, m.own), (m.ckv_w_far, m.ckv_w), (m.x_far, m.x))
    fours += fetch((m.small_all_far, m.small_all))
    greet(everyone(rep, f, n, Q))

    ffn_sums = ((m.d_gate_in, m.d_gate), (m.d_up_in, m.d_up), (m.d_down_in, m.d_down))

    def ffn_own(a):
        part, whole = ffn_sums[a]
        return pltpu.make_async_copy(part, whole.at[rep], m.ffn_sems[2].at[a])

    def ffn_copy(a, j):
        part, whole = ffn_sums[a]
        sems = m.ffn_sems[0].at[a, j - 1], m.ffn_sems[1].at[a, j - 1]
        return remote(part, whole.at[rep], *sems, reps[j - 1])

    for a in range(3):
        for j in range(1, Q):
            ffn_copy(a, j).start()
        ffn_own(a).start()
    out_sum = Reduce(G, R, *m.out_scratch, mode="far") if fused else None
    ckv_sum = Reduce(G, R, *m.ckv_scratch)
    du_parts, _, du_inbox, du_sems = m.du_scratch
    du_sum = Reduce(G, R, du_parts, None, du_inbox, du_sems)
    ckv_chain = Chain(G, R, m.ckv_all, m.ckv_chain_sems)
    d_wide = (m.d_wide0, m.d_wide1, m.d_wide2)
    wides = [Fold(G, R, Q, m.wide_scratch[a], d_wide[a], True) for a in range(3)] if fused else []
    d_w = Fold(G, R, Q, m.dw_scratch, m.d_w, False)
    d_cw = Fold(1, 1, Q, m.cw_scratch, m.d_ckv_w, True)

    def weight():
        return m.weight[...].reshape(D, D)

    def give(a, value):
        if fused:
            wides[a].parts[0] = value.reshape(wides[a].parts.shape[1:])
            wides[a].to_group(0)
        else:
            d_wide[a][...] = value


    wait_all(ones)
    unit_three, scale_three = unit_of(m.middle[...])
    dn3 = m.dn3[...]
    d_gain = jnp.sum(dn3 * unit_three, axis=0, keepdims=True)
    m.d_middle[...] = m.cot[...] + unit_backward(dn3 * m.gain[...], unit_three, scale_three)
    if fused:
        load_out.wait()
        for o in range(G):
            out_sum.offer(o)
    load(2).wait()
    m.d_after[...] = mm_nt(m.d_middle[...], weight())
    load(1).start()
    wait_all(twos)
    enc_rows = ckv_sum.parts.shape[3]
    enc_count = n * enc_rows
    for h in range(0, H, 2):
        outs = []
        for a in (h, h + 1):
            span = slice(2 * a * dh, 2 * (a + 1) * dh)
            ckv = m.ckv[:, 0, :, span].reshape(enc_count, 2 * dh)
            probs = m.probs[a]
            grad = beside(m.d_after[:, a * dh : (a + 1) * dh], 1)
            d_probs = mm_nt(ckv, grad)
            delta = jnp.sum(probs * d_probs, axis=0, keepdims=True)
            d_scores = probs * (d_probs - delta)
            cq = beside(m.cq[:, a * dh : (a + 1) * dh], 0)
            d_ckv = mm(jnp.concatenate([d_scores, probs], axis=1), jnp.concatenate([cq, grad], axis=0))
            ckv_sum.parts[:, :, :, :, span] = d_ckv.reshape(G, R, 1, enc_rows, 2 * dh)
            outs.append(mm_tn(ckv, d_scores)[:dh, :].T)
        m.d_cq[:, h * dh : (h + 2) * dh] = jnp.concatenate(outs, axis=1)
    for o in range(G):
        ckv_sum.offer(o)
    if fused:
        out_sum.pooled(lookup(out_sum.far_first, g, 0))
    give(2, mm_tn(m.cflat[...], m.d_middle[...]))
    load(1).wait()
    unit_two, scale_two = unit_of(m.after[...])
    d_unit = mm_nt(m.d_cq[...], weight())
    load(0).start()
    m.d_after[...] = m.d_middle[...] + unit_backward(d_unit, unit_two, scale_two)
    for o in range(G):
        ckv_sum.pooled(o)
    if fused:
        wides[2].to_replicas()
    give(1, mm_tn(unit_two, m.d_cq[...]))
    load(0).wait()
    d_att = mm_nt(m.d_after[...], weight())
    for i in range(G):
        m.d_att[i] = d_att[:, i * C : (i + 1) * C]
        lane_send(G, R, i, m.d_att, m.grad, m.att_sems)
    if fused:
        for t in range(1, G):
            out_sum.pooled(lookup(out_sum.far_first, g, t))
        wides[1].to_replicas()
    attended = jnp.concatenate([m.rows[i] for i in range(G)], axis=1)
    give(0, mm_tn(attended, m.d_after[...]))
    if fused:
        out_sum.hand_on(0)
    wait_all(threes)
    make_strips(R, heads, T, m.vec, m.strip)
    m.near[...] = jnp.zeros_like(m.near)
    m.far[...] = jnp.zeros_like(m.far)
    ckv_sum.hand_on(0)
    if fused:
        wides[0].to_replicas()
    ckv_sum.hand_on(1)
    lane_wait(G, R, m.d_att, m.grad, m.att_sems)

    def dkv_copy(i, j):
        return remote(
            m.dkv_parts.at[i, lax.rem(r + j, R)],
            m.dkv_pool.at[j - 1, i],
            m.dkv_send.at[j - 1, i],
            m.dkv_recv.at[j - 1, i],
            groups[j - 1],
        )

    dqkv = m.dqkv

    def own_gradient(i):
        for j in range(1, R):
            dkv_copy(i, j).wait_recv()
        dkv = m.dkv_parts[i, r]
        for j in range(1, R):
            dkv = dkv + m.dkv_pool[j - 1, i]
        dqkv[i, :, : 2 * C] = dkv

    for i in range(G - 1, -1, -1):
        L = R * (i + 1) * T
        grad = m.grad[i]
        prod_t = (grad * m.att[i]).T
        dqs = []
        for h in range(heads):
            scores = strip_scores(R, T, i, r, h, L, m.kv, m.q, m.strip)
            probs = jnp.exp(scores - m.lse[i, h : h + 1, :])
            grad_h = beside(grad[:, h * dh : (h + 1) * dh], 1)
            delta = jnp.sum(prod_t[h * dh : (h + 1) * dh, :], axis=0, keepdims=True)
            d_scores = probs * (mm_nt(m.kv[h, :L, :], grad_h) - delta)
            q_h = m.q[h, i * T : (i + 1) * T, :]
            dkv = mm(
                jnp.concatenate([d_scores, probs], axis=1), jnp.concatenate([q_h, grad_h], axis=0)
            )
            if i == G - 1:
                m.dkv[h] = dkv
            else:
                m.dkv[h, :L, :] += dkv
            dqs.append(mm_tn(m.kv[h, :L, :], d_scores)[:dh, :].T)
            skip = 1 if i == 0 else 0
            width = (R + 1 - skip) * T
            m.near[h, skip * T :, :] += d_scores[L - width :, :]
            if width < L:
                m.far[h : h + 1, :] += jnp.sum(d_scores[: L - width, :], axis=0, keepdims=True)
        m.dqkv[i, :, 2 * C :] = jnp.concatenate(dqs, axis=1)
        for b in range(R):
            rows = slice((i * R + b) * T, (i * R + b + 1) * T)
            m.dkv_parts[i, b] = jnp.concatenate([m.dkv[h, rows, :] for h in range(heads)], axis=1)
        for j in range(1, R):
            dkv_copy(i, j).start()
        if i < G - 1:
            own_gradient(i + 1)
        if i == 3:
            ckv_sum.hand_on(2)
        if i == 2:
            ckv_sum.collect(m.ckv_all.at[f])
            ckv_chain.start()
        if i == 1:
            ckv_chain.arrive(0)
            ckv_chain.arrive(1)
    own_gradient(0)
    wait_all(fours)
    if fused:
        for index in range(1, G - 1):
            out_sum.hand_on(index)
        wides[2].to_owner()
    w = m.w[...].reshape(D, 3 * C)
    for i in range(G):
        du_parts[i, 0] = mm_nt(dqkv[i], w).reshape(du_parts.shape[2:])
        du_sum.pooled(i)
    d_w.parts[0] = mm_tn(m.own[...], dqkv[...].reshape(G * T, 3 * C)).reshape(d_w.parts.shape[1:])
    d_w.to_group(0)
    if fused:
        wides[1].to_owner()
        wides[2].to_everyone()

    ids = jnp.broadcast_to(m.ids[0:1, :], (2 * T, 3 * T))
    ids = pltpu.roll(ids, 0, 1, stride=1, stride_axis=0)[:, :T]
    each = buckets // n
    tiny_parts = m.tiny_parts
    tiny_parts[...] = jnp.zeros_like(tiny_parts)
    for h in range(heads):
        pair = m.near[h, pl.ds(pl.multiple_of(r * T, T), 2 * T), :]
        far = m.far[h : h + 1, :]
        for idx in range(R - 1):
            block = jnp.sum(m.near[h, idx * T : (idx + 1) * T, :], axis=0, keepdims=True)
            far = far + jnp.where(idx < r, block, 0.0)
        for b in range(buckets):
            part = jnp.sum(jnp.where(ids == b, pair, 0.0), axis=0, keepdims=True)
            if b == buckets - 1:
                part = part + far
            row = h * each + b % each
            tiny_parts[b // each, row : row + 1, :] = part
    last = heads * each
    for o in range(n):
        tiny_parts[o, last : last + 1, :Dn] = d_gain[:, o * Dn : (o + 1) * Dn]
    tiny = Deal(n, tiny_parts, m.tiny_in, m.tiny_sems)
    tiny.start()

    du_sum.hand_on(0)
    d_w.to_replicas()
    ckv_chain.arrive(2)
    ckv_chain.arrive(3)
    if fused:
        wides[0].to_owner()
    d_w.to_owner()
    if fused:
        wides[1].to_everyone()
    du_sum.hand_on(1)
    d_ckv = m.ckv_all[...].reshape(enc_count, 2 * D)
    m.enc_parts[...] = mm_nt(d_ckv, m.ckv_w[...]).reshape(m.enc_parts.shape)
    d_enc = Deal(n, m.enc_parts, m.d_enc, m.enc_sems)
    d_enc.start()
    enc_cols = m.small_all[:, :enc_rows, :].reshape(enc_count, Dn)
    d_cw.parts[0, 0, 0] = mm_tn(enc_cols, d_ckv).reshape(d_cw.parts.shape[3:])
    d_cw.to_replicas()
    d_w.to_everyone()
    if fused:
        wides[0].to_everyone()
    for index in range(2, G - 1):
        du_sum.hand_on(index)
    tiny.arrive()
    for s in range(G):
        total = m.tiny_in[s * R]
        for j in range(1, R):
            total = total + m.tiny_in[s * R + j]
        m.tiny[rep, s] = total

    def tiny_copy(j):
        part = m.tiny.at[rep]
        return remote(part, part, m.tiny_rep_send.at[j - 1], m.tiny_rep_recv.at[j - 1], reps[j - 1])

    for j in range(1, Q):
        tiny_copy(j).start()
    d_cw.to_owner()
    d_cw.to_everyone()
    if fused:
        out_sum.collect(m.out)
        m.out[...] += m.middle[...].reshape(m.out.shape)
    du_sum.collect(m.du)
    unit_one, scale_one = unit_of(m.x[...])
    d_unit = m.du[...].reshape(T, D)
    m.d_x[...] = m.d_after[...] + unit_backward(d_unit, unit_one, scale_one)

    d_enc.arrive()
    for a in range(3):
        ffn_own(a).wait()
        for j in range(1, Q):
            ffn_copy(a, j).wait()
    for j in range(1, Q):
        tiny_copy(j).wait()
    tiny.finish()
    d_enc.finish()
    for i in range(G):
        for j in range(1, R):
            dkv_copy(i, j).wait_send()
    if fused:
        out_sum.finish()
        for fold in wides:
            fold.finish()
    ckv_sum.finish()
    du_sum.finish()
    ckv_chain.finish()
    d_w.finish()
    d_cw.finish()


def back_stage(G, R, Q, H, dh, buckets, near_ins, far_ins, collective_id):
    T, D = near_ins["x"].shape
    n = G * R
    S = n * T
    heads = H // G
    C = heads * dh
    Dn = D // n
    part = Dn // Q
    enc_rows = near_ins["ckv"].shape[2]
    block = (pieces, T // pieces, D)
    tiny_rows = -(-(heads * (buckets // n) + 1) // 8) * 8
    sem = pltpu.SemaphoreType.DMA
    some = max(R - 1, 1)
    fused = R <= 2
    far_outs = dict(
        d_gate=(Q,) + far_ins["d_gate_in"].shape,
        d_up=(Q,) + far_ins["d_up_in"].shape,
        d_down=(Q,) + far_ins["d_down_in"].shape,
    )
    outs = dict(
        d_x=(T, D),
        out=block,
        d_w=(Q, G, 1, part, 3 * C),
        d_wide0=(Q, 1, part, D) if fused else (D, D),
        d_wide1=(Q, 1, part, D) if fused else (D, D),
        d_wide2=(Q, 1, part, D) if fused else (D, D),
        d_ckv_w=(Q, 1, part, 2 * D),
        d_enc=(n, enc_rows, Dn),
        tiny=(Q, G, tiny_rows, T),
    )
    scratch = dict(
        d_middle=pltpu.VMEM((T, D), F32),
        d_cq=pltpu.VMEM((T, D), F32),
        d_after=pltpu.VMEM((T, D), F32),
        d_att=pltpu.VMEM((G, T, C), F32),
        weight=pltpu.VMEM((n, Q, part, D), F32),
        load_sem=sem,
        ffn_sems=(sem((3, Q - 1)), sem((3, Q - 1)), sem((3,))),
        out_sem=sem,
        strip=pltpu.VMEM((heads, 2 * R * T, T), F32),
        near=pltpu.VMEM((heads, (R + 1) * T, T), F32),
        far=pltpu.VMEM((8, T), F32),
        dkv=pltpu.VMEM((heads, S, 2 * dh), F32),
        dqkv=pltpu.VMEM((G, T, 3 * C), F32),
        grad=pltpu.VMEM((G, T, C), F32),
        dkv_parts=pltpu.VMEM((G, R, T, 2 * C), F32),
        dkv_pool=pltpu.VMEM((some, G, T, 2 * C), F32),
        dkv_send=sem((some, G)),
        dkv_recv=sem((some, G)),
        tiny_parts=pltpu.VMEM((n, tiny_rows, T), F32),
        tiny_in=pltpu.VMEM((n, tiny_rows, T), F32),
        tiny_sems=deal_sems(n),
        tiny_rep_send=sem((Q - 1,)),
        tiny_rep_recv=sem((Q - 1,)),
        enc_parts=pltpu.VMEM((n, enc_rows, Dn), F32),
        enc_sems=deal_sems(n),
        ckv_all=pltpu.VMEM((n, 1, enc_rows, 2 * D), F32),
        ckv_chain_sems=chain_sems(G, R, 1),
        att_sems=lane_sems(G),
        du=pltpu.VMEM(block, F32),
        ckv_scratch=tuple(reduce_scratch(G, R, 1, (enc_rows, 2 * D))),
        du_scratch=tuple(reduce_scratch(G, 1, pieces, (T, D))),
        dw_scratch=fold_scratch(1, G, R, Q, part, 3 * C),
        cw_scratch=fold_scratch(1, 1, 1, Q, part, 2 * D),
    )
    if fused:
        scratch |= dict(
            wide_scratch=tuple(fold_scratch(1, G, R, Q, part, D) for _ in range(3)),
            out_scratch=tuple(reduce_scratch(G, R, pieces, (T, D))),
        )
    results = call_stage(
        functools.partial(back_kernel, G, R, Q, H, dh, buckets, fused),
        {},
        far_ins,
        outs,
        far_outs,
        scratch,
        collective_id,
        fetched=near_ins,
    )
    if not fused:
        out = scatter(G, R, far_ins["out_parts"].reshape(G, R, T, D), True, True, collective_id + 1)
        results.out = out + near_ins["middle"]
        total = jnp.concatenate([results.d_wide0, results.d_wide1, results.d_wide2], axis=1)
        total = lax.psum_scatter(total, "fsdp", scatter_dimension=0, tiled=True)
        total = lax.psum(total, "rep")
        results.d_wide0, results.d_wide1, results.d_wide2 = jnp.split(total, 3, axis=1)
    return results


def last_kernel(Q, H, dh, names, *refs):
    m = named(names, refs)
    m.o_gate[...] = m.d_gate[...]
    m.o_up[...] = m.d_up[...]
    m.o_down[...] = m.d_down[...]
    m.o_x[...] = m.d_x[...]
    m.o_out[...] = m.out[...]
    G, part = m.d_w.shape[1], m.d_w.shape[3]
    heads = H // G
    C = heads * dh
    Dn, D = m.self_query.shape
    for q in range(Q):
        rows = slice(q * part, (q + 1) * part)
        for o in range(G):
            m.o_sq[rows, o * C : (o + 1) * C] = m.d_w[q, o, 0, :, 2 * C :]
            for h in range(heads):
                both = m.d_w[q, o, 0, :, 2 * h * dh : 2 * (h + 1) * dh]
                span = slice((o * heads + h) * dh, (o * heads + h + 1) * dh)
                m.o_sk[rows, span] = both[:, :dh]
                m.o_sv[rows, span] = both[:, dh:]
        for h in range(H):
            both = m.d_ckv_w[q, 0, :, 2 * h * dh : 2 * (h + 1) * dh]
            m.o_ck[rows, h * dh : (h + 1) * dh] = both[:, :dh]
            m.o_cv[rows, h * dh : (h + 1) * dh] = both[:, dh:]
        m.o_so[rows, :] = m.d_wide0[q, 0]
        m.o_cq[rows, :] = m.d_wide1[q, 0]
        m.o_co[rows, :] = m.d_wide2[q, 0]

    def row_sums(a):
        ones = jnp.ones((8, a.shape[1]), F32)
        return lax.dot_general(
            ones, a, (((1,), (1,)), ((), ())), precision=lax.Precision.HIGHEST, preferred_element_type=F32
        )[:1]

    products = m.o_sq[...] * m.self_query[...] + m.o_sk[...] * m.self_key[...] + m.o_sv[...] * m.self_value[...]
    m.o_g_self[...] = row_sums(products)
    m.o_g_cross[...] = row_sums(m.o_cq[...] * m.cross_query[...])
    self_gain = as_column(m.self_gain[...], 0, Dn)
    for ref in (m.o_sq, m.o_sk, m.o_sv):
        ref[...] = ref[...] * self_gain
    m.o_cq[...] = m.o_cq[...] * as_column(m.cross_gain[...], 0, Dn)
    n = m.d_enc.shape[0]
    m.o_enc[...] = jnp.concatenate([m.d_enc[o] for o in range(n)], axis=1)
    each = m.o_bias.shape[0]
    tiny_rows = m.tiny.shape[2]
    last = heads * each
    g_ffn = jnp.zeros((1, Dn), F32)
    bias = jnp.zeros((each, H), F32)
    row = lax.broadcasted_iota(jnp.int32, (tiny_rows, H), 0)
    column = lax.broadcasted_iota(jnp.int32, (tiny_rows, H), 1)
    to = lax.broadcasted_iota(jnp.int32, (each, tiny_rows), 0)
    of = lax.broadcasted_iota(jnp.int32, (each, tiny_rows), 1)
    pick = jnp.where(jnp.logical_and(of < last, lax.rem(of, each) == to), 1.0, 0.0)
    for o in range(G):
        total = m.tiny[0, o]
        for q in range(1, Q):
            total = total + m.tiny[q, o]
        g_ffn = g_ffn + total[last : last + 1, :Dn]
        sums = jnp.sum(total, axis=1, keepdims=True)
        held = jnp.logical_and(row < last, column == o * heads + row // each)
        bias = bias + lax.dot_general(
            pick,
            jnp.where(held, sums, 0.0),
            (((1,), (0,)), ((), ())),
            precision=lax.Precision.HIGHEST,
            preferred_element_type=F32,
        )
    m.o_g_ffn[...] = g_ffn
    m.o_bias[...] = bias


def last_stage(Q, H, dh, each, near_ins):
    Dn, D = near_ins["self_query"].shape
    enc_rows = near_ins["d_enc"].shape[1]
    near = dict(o_sq=(Dn, D), o_sk=(Dn, D), o_sv=(Dn, D), o_so=(Dn, D), o_cq=(Dn, D), o_ck=(Dn, D))
    near |= dict(o_cv=(Dn, D), o_co=(Dn, D), o_enc=(enc_rows, D), o_bias=(each, H))
    near |= dict(o_g_self=(1, Dn), o_g_cross=(1, Dn), o_g_ffn=(1, Dn))
    near |= dict(o_gate=near_ins["d_gate"].shape, o_up=near_ins["d_up"].shape)
    near |= dict(o_down=near_ins["d_down"].shape, o_x=near_ins["d_x"].shape, o_out=near_ins["out"].shape)
    return call_stage(functools.partial(last_kernel, Q, H, dh), near_ins, {}, near, {}, {}, None)


def shards(
    n,
    inputs,
    encoder,
    self_gain,
    cross_gain,
    ffn_gain,
    self_query,
    self_key,
    self_value,
    self_output,
    position_bias,
    bucket_table,
    cross_query,
    cross_key,
    cross_value,
    cross_output,
    ffn_gate,
    ffn_up,
    ffn_down,
    cotangent,
):
    x = inputs[0]
    enc = encoder[0]
    cot = cotangent[0]
    T, D = x.shape
    buckets, H = position_bias.shape
    dh = D // H
    G = math.gcd(H, n)
    R = n // G
    heads = H // G
    C = heads * dh
    Dn = D // n
    enc_local = enc.shape[0]
    Q = lax.axis_size("rep")
    part = Dn // Q

    def quarters(w):
        return w.reshape(Q, part, D)

    near_ins = dict(
        x=x,
        enc=enc,
        ffn_gain=ffn_gain.reshape(1, Dn),
        position_bias=position_bias.T,
        table=bucket_table.reshape(1, -1),
        self_gain=self_gain.reshape(1, Dn),
        cross_gain=cross_gain.reshape(1, Dn),
        cross_key=cross_key,
        cross_value=cross_value,
        cot=cot.reshape(pieces, T // pieces, D),
    )
    far_ins = dict(
        self_query=quarters(self_query),
        self_key=quarters(self_key),
        self_value=quarters(self_value),
        so=quarters(self_output),
        cq_w=quarters(cross_query),
        co=quarters(cross_output),
    )
    first = first_stage(G, R, Q, H, dh, near_ins, far_ins, 1)
    dn3, out_parts, d_gate, d_up, d_down = ffn_stage(
        G, R, Q, first.n3, first.cot_all, ffn_gate, ffn_up, ffn_down, 3
    )
    near_ins = dict(vars(first), x=x, cot=cot, dn3=dn3)
    del near_ins["wide"], near_ins["cot_all"], near_ins["n3"]
    far_ins = dict(
        wide=first.wide, out_parts=out_parts, d_gate_in=d_gate, d_up_in=d_up, d_down_in=d_down
    )
    back = back_stage(G, R, Q, H, dh, buckets, near_ins, far_ins, 5)

    near_ins = dict(
        d_gate=back.d_gate.reshape(ffn_gate.shape),
        d_up=back.d_up.reshape(ffn_up.shape),
        d_down=back.d_down.reshape(ffn_down.shape),
        d_x=back.d_x,
        out=back.out.reshape(T, D),
        d_w=back.d_w,
        d_ckv_w=back.d_ckv_w,
        d_wide0=back.d_wide0.reshape(Q, 1, part, D),
        d_wide1=back.d_wide1.reshape(Q, 1, part, D),
        d_wide2=back.d_wide2.reshape(Q, 1, part, D),
        d_enc=back.d_enc,
        tiny=back.tiny,
        self_query=self_query,
        self_key=self_key,
        self_value=self_value,
        cross_query=cross_query,
        self_gain=self_gain.reshape(1, Dn),
        cross_gain=cross_gain.reshape(1, Dn),
    )
    done = last_stage(Q, H, dh, buckets // n, near_ins)
    return (
        done.o_out[None],
        done.o_x[None],
        done.o_enc[None],
        done.o_g_self.reshape(Dn),
        done.o_g_cross.reshape(Dn),
        done.o_g_ffn.reshape(Dn),
        done.o_sq,
        done.o_sk,
        done.o_sv,
        done.o_so,
        done.o_bias,
        done.o_cq,
        done.o_ck,
        done.o_cv,
        done.o_co,
        done.o_gate,
        done.o_up,
        done.o_down,
    )


def solution(mesh):
    rows = P("rep", "fsdp", None)
    gain = P("fsdp")
    weight = P("fsdp", None)
    columns = P(None, "fsdp")
    args = (rows, rows, gain, gain, gain) + (weight,) * 4 + (P(), P()) + (weight,) * 4
    args += (columns, columns, weight, rows)
    outs = (rows, rows, rows, gain, gain, gain) + (weight,) * 9 + (columns, columns, weight)
    return jax.shard_map(
        functools.partial(shards, mesh.shape["fsdp"]),
        mesh=mesh,
        in_specs=args,
        out_specs=outs,
        check_vma=False,
    )
```

```python
import functools
import math
from types import SimpleNamespace

import jax
import jax.numpy as jnp
from jax import lax
from jax.experimental import pallas as pl
from jax.experimental.pallas import tpu as pltpu
from jax.sharding import PartitionSpec as P

HIGH = lax.Precision.HIGH
MESH = pl.DeviceIdType.MESH
F32 = jnp.float32
eps_norm = 1e-06
gelu_coef = math.sqrt(2.0 / math.pi)
masked_score = -1e30
vmem_bytes = 62 << 20
pieces = 4


def mm(a, b):
    return jnp.dot(a, b, precision=HIGH, preferred_element_type=F32)


def mm_tn(a, b):
    return lax.dot_general(
        a, b, (((0,), (0,)), ((), ())), precision=HIGH, preferred_element_type=F32
    )


def mm_nt(a, b):
    return lax.dot_general(
        a, b, (((1,), (1,)), ((), ())), precision=HIGH, preferred_element_type=F32
    )


BF16 = jnp.bfloat16


def halves(a):
    high = a.astype(BF16)
    return high, (a - high.astype(F32)).astype(BF16)


def dot3(a, b, dims=(((1,), (0,)), ((), ()))):
    def dot(x, y):
        return lax.dot_general(x, y, dims, preferred_element_type=F32)

    return dot(a[0], b[0]) + (dot(a[0], b[1]) + dot(a[1], b[0]))


def unit_of(rows):
    scale = lax.rsqrt(jnp.mean(rows * rows, axis=-1, keepdims=True) + eps_norm)
    return rows * scale, scale


def unit_backward(grad_unit, unit, scale):
    return scale * (grad_unit - unit * jnp.mean(grad_unit * unit, axis=-1, keepdims=True))


def gelu_parts(gate_pre):
    squared = gate_pre * gate_pre
    tangent = jnp.tanh(gelu_coef * (gate_pre + 0.044715 * squared * gate_pre))
    gelu_out = 0.5 * gate_pre * (1.0 + tangent)
    gelu_slope = 0.5 * (1.0 + tangent) + 0.5 * gate_pre * (1.0 - tangent * tangent) * gelu_coef * (
        1.0 + 3.0 * 0.044715 * squared
    )
    return (gelu_out, gelu_slope)


def my_place(R):
    rep = lax.axis_index("rep")
    f = lax.axis_index("fsdp")
    return rep, f, f // R, lax.rem(f, R)


def greet(peers):
    barrier = pltpu.get_barrier_semaphore()
    for peer in peers:
        pl.semaphore_signal(barrier, inc=1, device_id=peer, device_id_type=MESH)
    pl.semaphore_wait(barrier, len(peers))


def remote(src, dst, send_sem, recv_sem, peer):
    return pltpu.make_async_remote_copy(
        src_ref=src,
        dst_ref=dst,
        send_sem=send_sem,
        recv_sem=recv_sem,
        device_id=peer,
        device_id_type=MESH,
    )


def lane_peers(rep, g, r, G, R):
    return [(rep, lax.rem(g + k, G) * R + r) for k in range(1, G)]


def group_peers(rep, g, r, G, R):
    return [(rep, g * R + lax.rem(r + j, R)) for j in range(1, R)]


def comm_call(kernel, outs, ins, scratch, collective_id, vmem_ins=False, vmem_outs=False):
    def space(vmem):
        return pl.BlockSpec(memory_space=pltpu.VMEM if vmem else pl.ANY)

    return pl.pallas_call(
        kernel,
        out_shape=outs,
        in_specs=[space(vmem_ins)] * len(ins),
        out_specs=[space(vmem_outs)] * len(outs),
        scratch_shapes=scratch,
        compiler_params=pltpu.CompilerParams(
            collective_id=collective_id, has_side_effects=True, vmem_limit_bytes=vmem_bytes
        ),
    )(*ins)


def scatter_kernel(G, R, pooled, summed, x_ref, o_ref, *scratch):
    rep, f, g, r = my_place(R)
    lanes = lane_peers(rep, g, r, G, R)
    groups = group_peers(rep, g, r, G, R) if pooled else []
    if pooled:
        group_buf, group_send, group_recv = scratch[:3]
        scratch = scratch[3:]
    lane_out, lane_in, lane_send, lane_recv = scratch
    greet(lanes + groups)
    order = list(range(G - 1, -1, -1))
    group_copies = []
    if pooled:
        for k in order:
            for j in range(1, R):
                copy = remote(
                    x_ref.at[lax.rem(g + k, G), lax.rem(r + j, R)],
                    group_buf.at[j - 1, k],
                    group_send.at[j - 1, k],
                    group_recv.at[j - 1, k],
                    groups[j - 1],
                )
                copy.start()
                group_copies.append((j, k, copy))
    lane_copies = []
    for k in order:
        to = lax.rem(g + k, G)
        if pooled:
            for j, kk, copy in group_copies:
                if kk == k:
                    copy.wait_recv()
            total = x_ref[to, r]
            for j in range(1, R):
                total = total + group_buf[j - 1, k]
        else:
            total = x_ref[to]
        if k > 0:
            lane_out[k - 1] = total
            copy = remote(
                lane_out.at[k - 1], lane_in.at[k - 1], lane_send.at[k - 1], lane_recv.at[k - 1], lanes[k - 1]
            )
            copy.start()
            lane_copies.append((k, copy))
        elif summed:
            o_ref[...] = total
        else:
            o_ref[g] = total
    for k, copy in lane_copies:
        copy.wait_recv()
        if summed:
            o_ref[...] += lane_in[k - 1]
        else:
            o_ref[lax.rem(g + G - k, G)] = lane_in[k - 1]
    for _, copy in lane_copies:
        copy.wait_send()
    for _, _, copy in group_copies:
        copy.wait_send()


def scatter(G, R, x, pooled, summed, collective_id):
    block = x.shape[2:] if pooled else x.shape[1:]
    sem = pltpu.SemaphoreType.DMA
    scratch = []
    if pooled:
        scratch = [
            pltpu.VMEM((max(R - 1, 1), G) + block, F32),
            sem((max(R - 1, 1), G)),
            sem((max(R - 1, 1), G)),
        ]
    scratch += [
        pltpu.VMEM((G - 1,) + block, F32),
        pltpu.VMEM((G - 1,) + block, F32),
        sem((G - 1,)),
        sem((G - 1,)),
    ]
    out = jax.ShapeDtypeStruct(block if summed else (G,) + block, F32)
    return comm_call(
        functools.partial(scatter_kernel, G, R, pooled, summed),
        [out],
        [x],
        scratch,
        collective_id,
        vmem_ins=True,
        vmem_outs=True,
    )[0]


def named(names, refs):
    return SimpleNamespace(**dict(zip(names, refs, strict=True)))


def first_kernel(G, R, Q, H, dh, names, *refs):
    m = named(names, refs)
    rep, f, g, r = my_place(R)
    n = G * R
    heads = H // G
    T, D = m.x.shape
    C = heads * dh
    loads = []
    for index, ref in enumerate((m.self_key, m.self_value, m.self_query, m.so, m.cq_w, m.co)):
        copy = pltpu.make_async_copy(ref.at[rep], m.w_in.at[index], m.load_sems.at[index])
        copy.start()
        loads.append(copy)
    greet(everyone(rep, f, n, Q))

    save, saves = mover(m.keep_sems)
    enc_rows = m.enc.shape[0]
    Dn = D // n
    small = Deal(n, m.small_parts, m.small_all, m.small_sems)
    weights = Spread(G, R, Q, lambda k: m.w_mine.at[lax.rem(g + k, G)], m.w, m.w_sems)
    wide = Spread(G, R, Q, lambda k: m.w_in.at[pl.ds(3, 3)], m.wide, m.wide_sems)
    chain = Chain(G, R, m.x_buf, m.x_sems)
    cot_chain = Chain(G, R, m.cot_all, m.cot_sems)
    ckv_sum = Reduce(G, R, *m.ckv_scratch)
    ckv_chain = Chain(G, R, m.ckv, m.ckv_chain_sems)
    for copy in loads:
        copy.wait()
    part = m.w_in.shape[1]
    self_gain = as_column(m.self_gain[...], rep * part, part)
    for o in range(G):
        for h in range(heads):
            span = slice((o * heads + h) * dh, (o * heads + h + 1) * dh)
            both = jnp.concatenate([m.w_in[0, :, span], m.w_in[1, :, span]], axis=1)
            m.w_mine[o, :, 2 * h * dh : 2 * (h + 1) * dh] = both * self_gain
        m.w_mine[o, :, 2 * C :] = m.w_in[2, :, o * C : (o + 1) * C] * self_gain
    m.w_in[4] = m.w_in[4] * as_column(m.cross_gain[...], rep * part, part)
    weights.start()
    m.x_buf[f] = m.x[...].reshape(pieces, T // pieces, D)
    chain.start()
    for o in range(n):
        m.small_parts[o, :enc_rows, :] = m.enc[:, o * Dn : (o + 1) * Dn]
        m.small_parts[o, enc_rows:, :] = jnp.broadcast_to(m.ffn_gain[...], (8, Dn))
    small.start()
    cot_own = pltpu.make_async_copy(m.cot, m.cot_all.at[f], m.cot_own_sem)
    cot_own.start()
    for h in range(H):
        span = slice(h * dh, (h + 1) * dh)
        both = jnp.concatenate([m.cross_key[:, span], m.cross_value[:, span]], axis=1)
        m.ckv_w[:, 2 * h * dh : 2 * (h + 1) * dh] = both
    bias_rows(G, heads, T, g, m)
    make_strips(R, heads, T, m.vec, m.strip)
    weights.across()
    wide.own_start()
    small.arrive()
    ckv_parts = ckv_sum.parts
    enc_cols = m.small_all[:, :enc_rows, :].reshape(n * enc_rows, Dn)
    ckv_parts[...] = mm(enc_cols, m.ckv_w[...]).reshape(ckv_parts.shape)
    gain = jnp.concatenate([m.small_all[s, enc_rows : enc_rows + 1, :] for s in range(n)], axis=1)
    m.gain[...] = gain
    for o in range(G):
        ckv_sum.offer(o)
    chain.forward(1)
    wide.lanes_start()
    weights.share()
    for o in range(G):
        ckv_sum.pooled(o)
    weights.arrive()
    chain.forward(2)
    save((m.w, m.w_far), (m.vec, m.vec_far), (m.ids, m.ids_far), (m.ckv_w, m.ckv_w_far))
    save((m.small_all, m.small_all_far), (m.gain, m.gain_far))
    w = m.w[...].reshape(D, 3 * C)
    for t in range(G):
        if t > 0:
            wide.across_from(G - t)
        if t == G - 1:
            for d in range(3, G):
                chain.forward(d)
        src = chain.settle(t)
        if t > 0:
            ckv_sum.hand_on(t - 1)
        unit, _ = unit_of(m.x_buf[pl.ds(src * R, R)].reshape(R * T, D))
        rows = pl.ds(pl.multiple_of(src * (R * T), R * T), R * T)
        m.unit[...] = unit
        mine = m.unit[pl.ds(pl.multiple_of(r * T, T), T), :]
        mine_rows = pl.ds(pl.multiple_of(src * T, T), T)
        m.own[mine_rows, :] = mine
        kv = mm(unit, w[:, : 2 * C])
        q = mm(mine, w[:, 2 * C :])
        for h in range(heads):
            m.kv[h, rows, :] = kv[:, 2 * h * dh : 2 * (h + 1) * dh]
            m.q[h, mine_rows, :] = beside(q[:, h * dh : (h + 1) * dh], 0)
    save((m.own, m.own_far), (m.q, m.q_far), (m.kv, m.kv_far))
    ckv_sum.collect(m.ckv.at[f])
    ckv_chain.start()
    cot_own.wait()
    cot_chain.start()
    for i in range(G):
        L = R * (i + 1) * T
        outs = []
        for h in range(heads):
            scores = strip_scores(R, T, i, r, h, L, m.kv, m.q, m.strip)
            top = jnp.max(scores, axis=0, keepdims=True)
            probs = jnp.exp(scores - top)
            total = jnp.sum(probs, axis=0, keepdims=True)
            out_t = mm_tn(m.kv[h, :L, :], probs)[dh:, :] / total
            outs.append(out_t.T)
            m.lse[i, h : h + 1, :] = top + jnp.log(total)
        m.att[i] = jnp.concatenate(outs, axis=1)
        lane_send(G, R, i, m.att, m.rows, m.att_sems)
        ckv_chain.arrive(i)
        if i > 0:
            wide.share_from(G + 1 - i if i > 1 else 0)
        if i == G - 2:
            cot_chain.arrive(0)
            cot_chain.arrive(1)
    save((m.att, m.att_far), (m.lse, m.lse_far), (m.ckv, m.ckv_far))
    wide.share_from(1)
    lane_wait(G, R, m.att, m.rows, m.att_sems)
    cot_chain.arrive(2)
    wide.arrive()
    save((m.rows, m.rows_far), (m.wide, m.wide_far))

    attended = jnp.concatenate([m.rows[i] for i in range(G)], axis=1)
    after = m.x[...] + mm(attended, m.wide[:, :, 0].reshape(D, D))
    m.after[...] = after
    unit_two, _ = unit_of(after)
    m.cq[...] = mm(unit_two, m.wide[:, :, 1].reshape(D, D))
    save((m.after, m.after_far), (m.cq, m.cq_far))
    enc_count = n * enc_rows
    for h in range(0, H, 2):
        outs = []
        for a in (h, h + 1):
            ckv = m.ckv[:, 0, :, 2 * a * dh : 2 * (a + 1) * dh].reshape(enc_count, 2 * dh)
            scores = mm_nt(ckv, beside(m.cq[:, a * dh : (a + 1) * dh], 0))
            probs = jnp.exp(scores - jnp.max(scores, axis=0, keepdims=True))
            probs = probs / jnp.sum(probs, axis=0, keepdims=True)
            m.probs[a] = probs
            outs.append(mm_tn(ckv, probs)[dh:, :].T)
        m.cflat[:, h * dh : (h + 2) * dh] = jnp.concatenate(outs, axis=1)
    save((m.cflat, m.cflat_far), (m.probs, m.probs_far))
    middle = after + mm(m.cflat[...], m.wide[:, :, 2].reshape(D, D))
    m.middle[...] = middle
    unit_three, _ = unit_of(middle)
    m.n3[...] = unit_three * gain
    save((m.middle, m.middle_far), (m.n3, m.n3_far))
    cot_chain.arrive(3)

    small.finish()
    weights.finish()
    chain.finish()
    cot_chain.finish()
    ckv_sum.finish()
    ckv_chain.finish()
    wide.finish()
    wait_all(saves)


def as_column(row, start, count):
    n = row.shape[1]
    at = lax.broadcasted_iota(jnp.int32, (count, n), 0) + start
    pick = jnp.where(at == lax.broadcasted_iota(jnp.int32, (count, n), 1), 1.0, 0.0)
    return jnp.sum(pick * row, axis=1, keepdims=True)


def bias_rows(G, heads, T, g, m):
    buckets = m.position_bias.shape[1]
    late, early = m.table[:, T : 2 * T], m.table[:, :T]
    row = jnp.concatenate([late, jnp.zeros_like(late), early], axis=1)
    lane = lax.broadcasted_iota(jnp.int32, (1, 3 * T), 1)
    after = jnp.logical_and(lane >= T, lane < 2 * T)
    m.ids[...] = jnp.broadcast_to(jnp.where(after, -1, row).astype(F32), m.ids.shape)
    bucket = lax.broadcasted_iota(jnp.int32, (buckets, 3 * T), 0)
    onehot = jnp.where(bucket == row, 1.0, 0.0)
    bias = m.position_bias[...]
    every = lax.dot_general(
        bias - bias[:, buckets - 1 :],
        onehot,
        (((1,), (0,)), ((), ())),
        precision=lax.Precision.HIGHEST,
        preferred_element_type=F32,
    )
    every = jnp.where(after, masked_score, every)
    m.vec[...] = jnp.zeros_like(m.vec)
    for h in range(heads):
        one = every[h : h + 1]
        for i in range(1, G):
            one = jnp.where(g == i, every[i * heads + h : i * heads + h + 1], one)
        m.vec[h : h + 1, :] = one


def beside(a, at):
    zero = jnp.zeros_like(a)
    return jnp.concatenate([zero, a] if at else [a, zero], axis=1)


def lane_send(G, R, i, src_ref, dst_ref, sems):
    rep, f, g, r = my_place(R)

    @pl.when(g == i)
    def _():
        pltpu.make_async_copy(src_ref.at[i], dst_ref.at[i], sems[2]).start()

    @pl.when(g != i)
    def _():
        remote(src_ref.at[i], dst_ref.at[g], sems[0].at[i], sems[1].at[g], (rep, i * R + r)).start()


def lane_wait(G, R, src_ref, dst_ref, sems):
    rep, f, g, r = my_place(R)
    pltpu.make_async_copy(src_ref.at[g], dst_ref.at[g], sems[2]).wait()
    for i in range(G):

        @pl.when(g != i)
        def _():
            copy = remote(src_ref.at[i], dst_ref.at[i], sems[0].at[i], sems[1].at[i], (rep, i * R + r))
            copy.wait_send()
            copy.wait_recv()


def lane_sems(G):
    sem = pltpu.SemaphoreType.DMA
    return (sem((G,)), sem((G,)), sem)


class Spread:
    def __init__(self, G, R, Q, source, out, sems):
        self.sizes = (G, R, Q)
        self.source, self.out, self.sems = source, out, sems
        rep, f, g, r = my_place(R)
        self.place = (rep, f, g, r)
        self.lanes = lane_peers(rep, g, r, G, R)
        self.groups = group_peers(rep, g, r, G, R)
        self.reps = [(lax.rem(rep + j, Q), f) for j in range(1, Q)]

    def slot(self, k):
        G, R, Q = self.sizes
        _, _, g, r = self.place
        return lax.rem(g + G - k, G) * R + r

    def lane_copy(self, k):
        rep, f = self.place[:2]
        return remote(
            self.source(k), self.out.at[f, rep], self.sems[0].at[k - 1], self.sems[1].at[k - 1], self.lanes[k - 1]
        )

    def rep_copy(self, k, j):
        part = self.out.at[self.slot(k), self.place[0]]
        return remote(part, part, self.sems[2].at[k, j - 1], self.sems[3].at[k, j - 1], self.reps[j - 1])

    def group_copy(self, k, j):
        part = self.out.at[self.slot(k)]
        return remote(part, part, self.sems[4].at[k, j - 1], self.sems[5].at[k, j - 1], self.groups[j - 1])

    def start(self):
        self.lanes_start()
        self.own_start()

    def lanes_start(self):
        for k in range(self.sizes[0] - 1, 0, -1):
            self.lane_copy(k).start()

    def own_start(self):
        rep, f = self.place[:2]
        self.out[f, rep] = self.source(0)[...]
        for j in range(1, self.sizes[2]):
            self.rep_copy(0, j).start()

    def across_from(self, k):
        self.lane_copy(k).wait_recv()
        for j in range(1, self.sizes[2]):
            self.rep_copy(k, j).start()

    def across(self):
        for k in range(1, self.sizes[0]):
            self.across_from(k)

    def share_from(self, k):
        for j in range(1, self.sizes[2]):
            self.rep_copy(k, j).wait_recv()
        for j in range(1, self.sizes[1]):
            self.group_copy(k, j).start()

    def share(self):
        for k in range(self.sizes[0]):
            self.share_from(k)

    def arrive(self):
        G, R, Q = self.sizes
        for k in range(G):
            for j in range(1, R):
                self.group_copy(k, j).wait_recv()

    def finish(self):
        G, R, Q = self.sizes
        for k in range(G):
            if k > 0:
                self.lane_copy(k).wait_send()
            for j in range(1, Q):
                self.rep_copy(k, j).wait_send()
            for j in range(1, R):
                self.group_copy(k, j).wait_send()


class Deal:
    def __init__(self, n, parts, out, sems):
        self.n, self.parts, self.out, self.sems = n, parts, out, sems
        self.rep, self.f = lax.axis_index("rep"), lax.axis_index("fsdp")

    def copy(self, k):
        to = lax.rem(self.f + k, self.n)
        return remote(
            self.parts.at[to],
            self.out.at[self.f],
            self.sems[0].at[k - 1],
            self.sems[1].at[k - 1],
            (self.rep, to),
        )

    def start(self):
        for k in range(1, self.n):
            self.copy(k).start()
        self.out[self.f] = self.parts[self.f]

    def arrive(self):
        for k in range(1, self.n):
            self.copy(k).wait_recv()

    def finish(self):
        for k in range(1, self.n):
            self.copy(k).wait_send()


def deal_sems(n):
    sem = pltpu.SemaphoreType.DMA
    return (sem((n - 1,)), sem((n - 1,)))


def everyone(rep, f, n, Q):
    return [(rep, lax.rem(f + k, n)) for k in range(1, n)] + [
        (lax.rem(rep + j, Q), f) for j in range(1, Q)
    ]


def spread_sems(G, R, Q):
    sem = pltpu.SemaphoreType.DMA
    return (
        sem((G - 1,)),
        sem((G - 1,)),
        sem((G, Q - 1)),
        sem((G, Q - 1)),
        sem((G, R - 1)),
        sem((G, R - 1)),
    )


def lookup(table, i, t):
    rows, columns = len(table), len(table[0])
    flat = i * columns + t
    value = table[0][0] + 0 * flat
    for a in range(rows):
        for b in range(columns):
            if table[a][b] != table[0][0]:
                value = jnp.where(flat == a * columns + b, table[a][b], value)
    return value


class Chain:
    def __init__(self, G, R, buf, sems):
        self.G, self.R, self.buf, self.sems = G, R, buf, sems
        self.pieces = buf.shape[1]
        self.rep, self.f, self.g, self.r = my_place(R)
        self.groups = group_peers(self.rep, self.g, self.r, G, R)
        self.order, self.first, self.second = [], [], []
        for i in range(G):
            order = sorted(range(G), key=lambda s: (abs(s - i), s))
            self.order.append(order)
            far = [abs(s - i) for s in order]
            fresh = [t > 0 and far[t] != far[t - 1] for t in range(G)]
            paired = [fresh[t] and t + 1 < G and far[t + 1] == far[t] for t in range(G)]
            self.first.append([order[t] if fresh[t] else -1 for t in range(G)])
            self.second.append([order[t + 1] if paired[t] else -1 for t in range(G)])

    def part(self, src, p):
        return self.buf.at[src * self.R + self.r, p]

    def step(self, src, side, p):
        part = self.part(src, p)
        to = (self.rep, (self.g + side) * self.R + self.r)
        way = 0 if side > 0 else 1
        return remote(part, part, self.sems[0].at[way, src, p], self.sems[1].at[src, p], to)

    def group_copy(self, src, j, p):
        part = self.part(src, p)
        return remote(
            part, part, self.sems[2].at[j - 1, src, p], self.sems[3].at[j - 1, src, p], self.groups[j - 1]
        )

    def sends(self, src):
        right = jnp.logical_and(src <= self.g, self.g < self.G - 1)
        left = jnp.logical_and(src >= self.g, self.g > 0)
        return ((1, right), (-1, left))

    def onward(self, src, p):
        for side, cond in self.sends(src):

            @pl.when(cond)
            def _():
                self.step(src, side, p).start()

        for j in range(1, self.R):
            self.group_copy(src, j, p).start()

    def start(self):
        for p in range(self.pieces):
            self.onward(self.g, p)

    def forward(self, d):
        for src in (self.g - d, self.g + d):

            @pl.when(jnp.logical_and(src >= 0, src < self.G))
            def _():
                for p in range(self.pieces):
                    self.step(src, 1, p).wait_recv()
                    self.onward(src, p)

    def settle(self, t):
        src = lookup(self.order, self.g, t)
        for j in range(1, self.R):
            for p in range(self.pieces):
                self.group_copy(src, j, p).wait_recv()
        return src

    def arrive(self, t):
        for table in (self.first, self.second):
            came = lookup(table, self.g, t)

            @pl.when(came >= 0)
            def _():
                for p in range(self.pieces):
                    self.step(came, 1, p).wait_recv()
                    self.onward(came, p)

        return self.settle(t)

    def finish(self):
        for src in range(self.G):
            for p in range(self.pieces):
                for side, cond in self.sends(src):

                    @pl.when(cond)
                    def _():
                        self.step(src, side, p).wait_send()

                for j in range(1, self.R):
                    self.group_copy(src, j, p).wait_send()


def chain_sems(G, R, pieces):
    sem = pltpu.SemaphoreType.DMA
    return (sem((2, G, pieces)), sem((G, pieces)), sem((R - 1, G, pieces)), sem((R - 1, G, pieces)))


def make_strips(R, heads, T, vec_ref, strip_ref):
    for h in range(heads):
        vec = jnp.broadcast_to(vec_ref[h : h + 1, :], (2 * T, 3 * T))
        pair = pltpu.roll(vec, 0, 1, stride=1, stride_axis=0)[:, :T]
        if R > 1:
            strip_ref[h, : (R - 1) * T, :] = jnp.zeros(((R - 1) * T, T), F32)
            strip_ref[h, (R + 1) * T :, :] = jnp.full(((R - 1) * T, T), masked_score, F32)
        strip_ref[h, (R - 1) * T : (R + 1) * T, :] = pair


def strip_scores(R, T, i, r, h, L, kv_ref, q_ref, strip_ref):
    scores = mm_nt(kv_ref[h, :L, :], q_ref[h, i * T : (i + 1) * T, :])
    skip = 1 if i == 0 else 0
    width = (R + 1 - skip) * T
    start = pl.multiple_of((R - 1 - r + skip) * T, T)
    near = scores[L - width :, :] + strip_ref[h, pl.ds(start, width), :]
    if width == L:
        return near
    return jnp.concatenate([scores[: L - width, :], near], axis=0)


def mover(sems):
    started = []

    def start(*pairs):
        batch = []
        for src, dst in pairs:
            batch.append(pltpu.make_async_copy(src, dst, sems.at[len(started)]))
            batch[-1].start()
            started.append(batch[-1])
        return batch

    return start, started


def wait_all(copies):
    for copy in copies:
        copy.wait()


def call_stage(
    kernel, near_ins, far_ins, near_outs, far_outs, scratch, collective_id, fetched=None, kept=None
):
    vm = pl.BlockSpec(memory_space=pltpu.VMEM)
    hbm = pl.BlockSpec(memory_space=pl.ANY)
    fetched, kept = fetched or {}, kept or {}
    outs = near_outs | far_outs | kept
    names = tuple(near_ins) + tuple(far_ins) + tuple(f"{k}_far" for k in fetched)
    names += tuple(near_outs) + tuple(far_outs) + tuple(f"{k}_far" for k in kept)
    scratch = dict(scratch)
    scratch |= {k: pltpu.VMEM(value.shape, value.dtype) for k, value in fetched.items()}
    scratch |= {k: pltpu.VMEM(shape, F32) for k, shape in kept.items()}
    if fetched:
        scratch |= dict(fetch_sems=pltpu.SemaphoreType.DMA((len(fetched),)))
    if kept:
        scratch |= dict(keep_sems=pltpu.SemaphoreType.DMA((len(kept),)))
    names += tuple(scratch)
    results = pl.pallas_call(
        functools.partial(kernel, names),
        out_shape=[jax.ShapeDtypeStruct(shape, F32) for shape in outs.values()],
        in_specs=[vm] * len(near_ins) + [hbm] * (len(far_ins) + len(fetched)),
        out_specs=[vm] * len(near_outs) + [hbm] * (len(far_outs) + len(kept)),
        scratch_shapes=list(scratch.values()),
        compiler_params=pltpu.CompilerParams(
            collective_id=collective_id,
            has_side_effects=collective_id is not None,
            vmem_limit_bytes=vmem_bytes,
        ),
    )(*near_ins.values(), *far_ins.values(), *fetched.values())
    return named(tuple(outs), results)


def first_stage(G, R, Q, H, dh, near_ins, far_ins, collective_id):
    T, D = near_ins["x"].shape
    n = G * R
    S = n * T
    heads = H // G
    C = heads * dh
    enc_rows = near_ins["enc"].shape[0]
    part = D // n // Q
    block = (pieces, T // pieces, D)
    outs = dict(
        att=(G, T, C),
        rows=(G, T, C),
        q=(heads, G * T, 2 * dh),
        kv=(heads, S, 2 * dh),
        lse=(G, 8, T),
        w=(n, Q, part, 3 * C),
        own=(G * T, D),
        small_all=(n, enc_rows + 8, D // n),
        vec=(8, 3 * T),
        ids=(8, 3 * T),
        ckv_w=(D // n, 2 * D),
        ckv=(n, 1, enc_rows, 2 * D),
        gain=(1, D),
        after=(T, D),
        middle=(T, D),
        n3=(T, D),
        cq=(T, D),
        cflat=(T, D),
        probs=(H, n * enc_rows, T),
        wide=(n, Q, 3, part, D),
    )
    far_outs = dict(cot_all=(n,) + block)
    scratch = dict(
        x_buf=pltpu.VMEM((n,) + block, F32),
        unit=pltpu.VMEM((R * T, D), F32),
        strip=pltpu.VMEM((heads, 2 * R * T, T), F32),
        x_sems=chain_sems(G, R, pieces),
        cot_sems=chain_sems(G, R, pieces),
        cot_own_sem=pltpu.SemaphoreType.DMA,
        w_in=pltpu.VMEM((6, part, D), F32),
        w_mine=pltpu.VMEM((G, part, 3 * C), F32),
        small_parts=pltpu.VMEM((n, enc_rows + 8, D // n), F32),
        load_sems=pltpu.SemaphoreType.DMA((6,)),
        w_sems=spread_sems(G, R, Q),
        wide_sems=spread_sems(G, R, Q),
        att_sems=lane_sems(G),
        small_sems=deal_sems(n),
        ckv_scratch=tuple(reduce_scratch(G, R, 1, (enc_rows, 2 * D))),
        ckv_chain_sems=chain_sems(G, R, 1),
    )
    return call_stage(
        functools.partial(first_kernel, G, R, Q, H, dh),
        near_ins,
        far_ins,
        {},
        far_outs,
        scratch,
        collective_id,
        kept=outs,
    )


class Reduce:
    def __init__(self, G, R, parts, pool, inbox, sems, mode="near"):
        self.G, self.parts, self.pool, self.inbox, self.sems = G, parts, pool, inbox, sems
        self.pieces = parts.shape[2]
        self.rep, self.f, self.g, self.r = my_place(R)
        self.stride = R
        self.R = R if pool is not None else 1
        self.mine = self.r if pool is not None else 0
        self.groups = group_peers(self.rep, self.g, self.r, G, R)
        orders = []
        for g in range(G):
            due = {o: o + g if o > g else (G - 1 - o) + (G - 1 - g) for o in range(G) if o != g}
            if mode == "far":
                due = {o: G - 1 - o + g if o > g else o + G - 1 - g for o in due}
            held = [o for o in due if (g > 0 if o > g else g < G - 1)]
            orders.append((sorted(held, key=lambda o: due[o]) + [-1] * G)[: G - 1])
        self.orders = orders
        self.far_first = [sorted(range(G), key=lambda o: -abs(o - i)) for i in range(G)]

    def group_copy(self, o, j, p):
        other = lax.rem(self.r + j, self.R)
        return remote(
            self.parts.at[o, other, p],
            self.pool.at[j - 1, o, p],
            self.sems[0].at[j - 1, o, p],
            self.sems[1].at[j - 1, o, p],
            self.groups[j - 1],
        )

    def lane_copy(self, o, p):
        right = o > self.g
        to = jnp.where(right, self.g + 1, self.g - 1)
        last_left = jnp.logical_and(jnp.logical_not(right), to == o)
        slot = jnp.where(last_left, self.G, o)
        part = self.parts.at[o, self.mine, p]
        peer = (self.rep, to * self.stride + self.r)
        return remote(part, self.inbox.at[slot, p], self.sems[2].at[o, p], self.sems[3].at[slot, p], peer)

    def inbox_wait(self, slot, p):
        remote(
            self.parts.at[0, self.mine, p],
            self.inbox.at[slot, p],
            self.sems[2].at[0, p],
            self.sems[3].at[slot, p],
            (self.rep, self.f),
        ).wait_recv()

    def offer(self, o):
        for p in range(self.pieces):
            for j in range(1, self.R):
                self.group_copy(o, j, p).start()

    def pooled(self, o):
        first = jnp.logical_or(
            jnp.logical_and(o > self.g, self.g == 0),
            jnp.logical_and(o < self.g, self.g == self.G - 1),
        )
        for p in range(self.pieces):
            for j in range(1, self.R):
                self.group_copy(o, j, p).wait_recv()
            if self.R > 1:
                total = self.parts[o, self.mine, p]
                for j in range(1, self.R):
                    total = total + self.pool[j - 1, o, p]
                self.parts[o, self.mine, p] = total

            @pl.when(first)
            def _():
                self.lane_copy(o, p).start()

    def hand_on(self, index):
        o = lookup(self.orders, self.g, index)

        @pl.when(o >= 0)
        def _():
            for p in range(self.pieces):
                self.inbox_wait(o, p)
                self.parts[o, self.mine, p] += self.inbox[o, p]
                self.lane_copy(o, p).start()

    def collect(self, out):
        for p in range(self.pieces):
            out[p] = self.parts[self.g, self.mine, p]

        for cond, slot in ((self.g > 0, self.g), (self.g < self.G - 1, self.G)):

            @pl.when(cond)
            def _():
                for p in range(self.pieces):
                    self.inbox_wait(slot, p)
                    out[p] += self.inbox[slot, p]

    def finish(self):
        for o in range(self.G):
            for p in range(self.pieces):
                for j in range(1, self.R):
                    self.group_copy(o, j, p).wait_send()

            @pl.when(self.g != o)
            def _():
                for p in range(self.pieces):
                    self.lane_copy(o, p).wait_send()


def reduce_scratch(G, R, pieces, block):
    sem = pltpu.SemaphoreType.DMA
    block = (pieces, block[0] // pieces) + block[1:]
    return [
        pltpu.VMEM((G, R) + block, F32),
        pltpu.VMEM((R - 1, G) + block if R > 1 else (8, 128), F32),
        pltpu.VMEM((G + 1,) + block, F32),
        (sem((max(R - 1, 1), G, pieces)), sem((max(R - 1, 1), G, pieces)), sem((G, pieces)), sem((G + 1, pieces))),
    ]


def ffn_kernel(
    G,
    R,
    n3_ref,
    cot_far,
    gate_far,
    up_far,
    down_far,
    dn3_ref,
    out_far,
    d_gate_ref,
    d_up_ref,
    d_down_ref,
    gate_parts,
    up_parts,
    down_parts,
    gate_in,
    up_in,
    down_in,
    rep_sems,
    cot_ref,
    gate_ref,
    up_ref,
    down_ref,
    out_ref,
    fetch_sems,
    out_sems,
    n3_buf,
    n3_high,
    n3_low,
    inner_high,
    inner_low,
    grads_high,
    grads_low,
    wide_high,
    wide_low,
    tall_high,
    tall_low,
    dn3_parts,
    dn3_pool,
    dn3_inbox,
    dn3_sems,
    n3_sems,
):
    rep, f, g, r = my_place(R)
    T, D = n3_ref.shape
    F = gate_ref.shape[1]
    rows_each = R * T
    block = (R, pieces, T // pieces, D)
    Q = gate_parts.shape[0]
    fetch, _ = mover(fetch_sems)
    weights = fetch((gate_far, gate_ref), (up_far, up_ref), (down_far, down_ref))
    cot_fetch = fetch((cot_far, cot_ref))
    greet(lane_peers(rep, g, r, G, R) + group_peers(rep, g, r, G, R) + everyone(rep, f, 1, Q))
    sums = [
        (gate_parts, gate_in, d_gate_ref),
        (up_parts, up_in, d_up_ref),
        (down_parts, down_in, d_down_ref),
    ]

    def rep_copy(a, j):
        to = lax.rem(rep + j, Q)
        sems = rep_sems[0].at[a, j - 1], rep_sems[1].at[a, j - 1]
        return remote(sums[a][0].at[to], sums[a][1].at[j - 1], *sems, (to, f))

    def to_replicas(a, value):
        sums[a][0][...] = value.reshape(sums[a][0].shape)
        for j in range(1, Q):
            rep_copy(a, j).start()

    chain = Chain(G, R, n3_buf, n3_sems)
    d_three = Reduce(G, R, dn3_parts, dn3_pool, dn3_inbox, dn3_sems)
    n3_buf[f] = n3_ref[...].reshape(pieces, T // pieces, D)
    chain.start()
    wait_all(weights)
    for index, ref in enumerate((gate_ref, up_ref, down_ref)):
        high, low = halves(ref[...])
        span = slice(index * F, (index + 1) * F)
        wide = index < 2
        wide_high[:, span] = high if wide else high.T
        wide_low[:, span] = low if wide else low.T
        tall_high[span, :] = high.T if wide else high
        tall_low[span, :] = low.T if wide else low
    wait_all(cot_fetch)

    @pl.loop(0, G)
    def _(t):
        src = chain.arrive(t)
        rows = pl.ds(pl.multiple_of(src * rows_each, rows_each), rows_each)
        n3 = halves(n3_buf[pl.ds(src * R, R)].reshape(rows_each, D))
        n3_high[rows, :], n3_low[rows, :] = n3
        pre = dot3(n3, (wide_high[:, : 2 * F], wide_low[:, : 2 * F]))
        gate_pre, up_pre = pre[:, :F], pre[:, F:]
        gelu_out, gelu_slope = gelu_parts(gate_pre)
        inner = halves(gelu_out * up_pre)
        inner_high[rows, :], inner_low[rows, :] = inner
        cot = halves(cot_ref[pl.ds(src * R, R)].reshape(rows_each, D))
        grad_inner = dot3(cot, (wide_high[:, 2 * F :], wide_low[:, 2 * F :]))
        grads = halves(
            jnp.concatenate([grad_inner * up_pre * gelu_slope, grad_inner * gelu_out], axis=1)
        )
        grads_high[rows, :], grads_low[rows, :] = grads
        dn3 = dot3(grads, (tall_high[: 2 * F, :], tall_low[: 2 * F, :]))
        dn3_parts[src] = dn3.reshape(block)
        d_three.offer(src)
        out = dot3(inner, (tall_high[2 * F :, :], tall_low[2 * F :, :]))
        out_ref[src] = out.reshape(block)
        pltpu.make_async_copy(out_ref.at[src], out_far.at[src], out_sems.at[src]).start()
        d_three.pooled(src)

    S = G * rows_each
    tn = (((0,), (0,)), ((), ()))
    n3 = (n3_high[...], n3_low[...])
    to_replicas(0, dot3(n3, (grads_high[:, :F], grads_low[:, :F]), tn))
    d_three.hand_on(0)
    to_replicas(1, dot3(n3, (grads_high[:, F:], grads_low[:, F:]), tn))
    d_three.hand_on(1)
    cot = halves(cot_ref[...].reshape(S, D))
    to_replicas(2, dot3((inner_high[...], inner_low[...]), cot, tn))
    for index in range(2, G - 1):
        d_three.hand_on(index)
    d_three.collect(dn3_ref)
    for a in range(3):
        total = sums[a][0][rep]
        for j in range(1, Q):
            rep_copy(a, j).wait_recv()
            total = total + sums[a][1][j - 1]
        sums[a][2][...] = total
        for j in range(1, Q):
            rep_copy(a, j).wait_send()
    chain.finish()
    d_three.finish()
    for o in range(G):
        pltpu.make_async_copy(out_ref.at[o], out_far.at[o], out_sems.at[o]).wait()


def ffn_stage(G, R, Q, n3, cot, gate, up, down, collective_id):
    T, D = n3.shape
    F = gate.shape[1]
    n = G * R
    S = n * T
    vm = pl.BlockSpec(memory_space=pltpu.VMEM)
    hbm = pl.BlockSpec(memory_space=pl.ANY)
    block = (pieces, T // pieces, D)
    shape = lambda *dims: jax.ShapeDtypeStruct(dims, F32)
    dn3, out, d_gate, d_up, d_down = pl.pallas_call(
        functools.partial(ffn_kernel, G, R),
        out_shape=[
            shape(*block),
            shape(G, R, *block),
            shape(D // Q, F),
            shape(D // Q, F),
            shape(F // Q, D),
        ],
        in_specs=[vm] + [hbm] * 4,
        out_specs=[vm, hbm] + [vm] * 3,
        scratch_shapes=[
            pltpu.VMEM((Q, D // Q, F), F32),
            pltpu.VMEM((Q, D // Q, F), F32),
            pltpu.VMEM((Q, F // Q, D), F32),
            pltpu.VMEM((Q - 1, D // Q, F), F32),
            pltpu.VMEM((Q - 1, D // Q, F), F32),
            pltpu.VMEM((Q - 1, F // Q, D), F32),
            (pltpu.SemaphoreType.DMA((3, Q - 1)), pltpu.SemaphoreType.DMA((3, Q - 1))),
            pltpu.VMEM((n,) + block, F32),
            pltpu.VMEM((D, F), F32),
            pltpu.VMEM((D, F), F32),
            pltpu.VMEM((F, D), F32),
            pltpu.VMEM((G, R) + block, F32),
            pltpu.SemaphoreType.DMA((4,)),
            pltpu.SemaphoreType.DMA((G,)),
            pltpu.VMEM((n,) + block, F32),
            pltpu.VMEM((S, D), BF16),
            pltpu.VMEM((S, D), BF16),
            pltpu.VMEM((S, F), BF16),
            pltpu.VMEM((S, F), BF16),
            pltpu.VMEM((S, 2 * F), BF16),
            pltpu.VMEM((S, 2 * F), BF16),
            pltpu.VMEM((D, 3 * F), BF16),
            pltpu.VMEM((D, 3 * F), BF16),
            pltpu.VMEM((3 * F, D), BF16),
            pltpu.VMEM((3 * F, D), BF16),
        ]
        + reduce_scratch(G, R, pieces, (T, D))
        + [chain_sems(G, R, pieces)],
        compiler_params=pltpu.CompilerParams(
            collective_id=collective_id, has_side_effects=True, vmem_limit_bytes=vmem_bytes
        ),
    )(n3, cot, gate, up, down)
    return dn3.reshape(T, D), out, d_gate, d_up, d_down


class Fold:
    def __init__(self, G, R, Q, scratch, out, summed):
        self.G, self.R, self.Q = G, R, Q
        self.parts, self.pool, self.rep_in, self.lane_out, self.lane_in, self.sems = scratch
        self.A = self.parts.shape[0]
        self.out, self.summed = out, summed
        self.rep, self.f, self.g, self.r = my_place(R)
        self.groups = group_peers(self.rep, self.g, self.r, G, R)
        self.lanes = lane_peers(self.rep, self.g, self.r, G, R)
        self.to_rep = [lax.rem(self.rep + j, Q) for j in range(1, Q)]
        if G * R == 1:
            self.g = self.r = 0

    def group_copy(self, a, o, j):
        return remote(
            self.parts.at[a, o, lax.rem(self.r + j, self.R)],
            self.pool.at[j - 1, a, o],
            self.sems[0].at[j - 1, a, o],
            self.sems[1].at[j - 1, a, o],
            self.groups[j - 1],
        )

    def rep_copy(self, o, j):
        return remote(
            self.parts.at[:, o, self.r, self.to_rep[j - 1]],
            self.rep_in.at[j - 1, o],
            self.sems[2].at[j - 1, o],
            self.sems[3].at[j - 1, o],
            (self.to_rep[j - 1], self.f),
        )

    def lane_copy(self, k):
        return remote(
            self.lane_out.at[k],
            self.lane_in.at[k - 1],
            self.sems[4].at[k - 1],
            self.sems[5].at[k - 1],
            self.lanes[k - 1],
        )

    def back_copy(self, j):
        part = self.out.at[self.rep]
        return remote(
            part, part, self.sems[6].at[j - 1], self.sems[7].at[j - 1], (self.to_rep[j - 1], self.f)
        )

    def to_group(self, a):
        for o in range(self.G):
            for j in range(1, self.R):
                self.group_copy(a, o, j).start()

    def to_replicas(self):
        for o in range(self.G):
            for a in range(self.A):
                for j in range(1, self.R):
                    self.group_copy(a, o, j).wait_recv()
                    self.parts[a, o, self.r] += self.pool[j - 1, a, o]
            for j in range(1, self.Q):
                self.rep_copy(o, j).start()

    def to_owner(self):
        for k in range(self.G - 1, -1, -1):
            o = lax.rem(self.g + k, self.G)
            for j in range(1, self.Q):
                self.rep_wait(o, j)
            total = self.parts[:, o, self.r, self.rep]
            for j in range(1, self.Q):
                total = total + self.rep_in[j - 1, o]
            self.lane_out[k] = total
            if k > 0:
                self.lane_copy(k).start()

    def rep_wait(self, o, j):
        self.rep_copy(o, j).wait_recv()

    def to_everyone(self):
        if self.summed:
            total = self.lane_out[0]
            for k in range(1, self.G):
                self.lane_copy(k).wait_recv()
                total = total + self.lane_in[k - 1]
            self.out[self.rep] = total
        else:
            self.out[self.rep, self.g] = self.lane_out[0]
            for k in range(1, self.G):
                self.lane_copy(k).wait_recv()
                self.out[self.rep, lax.rem(self.g + self.G - k, self.G)] = self.lane_in[k - 1]
        for j in range(1, self.Q):
            self.back_copy(j).start()

    def finish(self):
        for j in range(1, self.Q):
            self.back_copy(j).wait()
        for o in range(self.G):
            for a in range(self.A):
                for j in range(1, self.R):
                    self.group_copy(a, o, j).wait_send()
            for j in range(1, self.Q):
                self.rep_copy(o, j).wait_send()
        for k in range(1, self.G):
            self.lane_copy(k).wait_send()


def fold_scratch(A, G, R, Q, m, W):
    sem = pltpu.SemaphoreType.DMA
    some, lanes = max(R - 1, 1), max(G - 1, 1)
    return (
        pltpu.VMEM((A, G, R, Q, m, W), F32),
        pltpu.VMEM((some, A, G, Q, m, W) if R > 1 else (1, 1, 1, 1, 8, 128), F32),
        pltpu.VMEM((Q - 1, G, A, m, W), F32),
        pltpu.VMEM((G, A, m, W), F32),
        pltpu.VMEM((lanes, A, m, W), F32),
        (
            sem((some, A, G)),
            sem((some, A, G)),
            sem((Q - 1, G)),
            sem((Q - 1, G)),
            sem((lanes,)),
            sem((lanes,)),
            sem((Q - 1,)),
            sem((Q - 1,)),
        ),
    )


def back_kernel(G, R, Q, H, dh, buckets, fused, names, *refs):
    m = named(names, refs)
    rep, f, g, r = my_place(R)
    n = G * R
    heads = H // G
    T, D = m.x.shape
    C = heads * dh
    Dn = D // n
    groups = group_peers(rep, g, r, G, R)
    reps = [(lax.rem(rep + j, Q), f) for j in range(1, Q)]
    fetch, _ = mover(m.fetch_sems)
    ones = fetch((m.dn3_far, m.dn3), (m.middle_far, m.middle), (m.cot_far, m.cot), (m.gain_far, m.gain))

    def load(a):
        return pltpu.make_async_copy(m.wide.at[:, :, a], m.weight, m.load_sem)

    load(2).start()
    if fused:
        load_out = pltpu.make_async_copy(m.out_parts, m.out_scratch[0], m.out_sem)
        load_out.start()
    twos = fetch((m.ckv_far, m.ckv), (m.probs_far, m.probs), (m.cq_far, m.cq), (m.cflat_far, m.cflat))
    twos += fetch((m.after_far, m.after), (m.rows_far, m.rows), (m.vec_far, m.vec), (m.ids_far, m.ids))
    threes = fetch((m.kv_far, m.kv), (m.q_far, m.q), (m.lse_far, m.lse), (m.att_far, m.att))
    fours = fetch((m.w_far, m.w), (m.own_far, m.own), (m.ckv_w_far, m.ckv_w), (m.x_far, m.x))
    fours += fetch((m.small_all_far, m.small_all))
    greet(everyone(rep, f, n, Q))

    ffn_sums = ((m.d_gate_in, m.d_gate), (m.d_up_in, m.d_up), (m.d_down_in, m.d_down))

    def ffn_own(a):
        part, whole = ffn_sums[a]
        return pltpu.make_async_copy(part, whole.at[rep], m.ffn_sems[2].at[a])

    def ffn_copy(a, j):
        part, whole = ffn_sums[a]
        sems = m.ffn_sems[0].at[a, j - 1], m.ffn_sems[1].at[a, j - 1]
        return remote(part, whole.at[rep], *sems, reps[j - 1])

    for a in range(3):
        for j in range(1, Q):
            ffn_copy(a, j).start()
        ffn_own(a).start()
    out_sum = Reduce(G, R, *m.out_scratch, mode="far") if fused else None
    ckv_sum = Reduce(G, R, *m.ckv_scratch)
    du_parts, _, du_inbox, du_sems = m.du_scratch
    du_sum = Reduce(G, R, du_parts, None, du_inbox, du_sems)
    ckv_chain = Chain(G, R, m.ckv_all, m.ckv_chain_sems)
    d_wide = (m.d_wide0, m.d_wide1, m.d_wide2)
    wides = [Fold(G, R, Q, m.wide_scratch[a], d_wide[a], True) for a in range(3)] if fused else []
    d_w = Fold(G, R, Q, m.dw_scratch, m.d_w, False)
    d_cw = Fold(1, 1, Q, m.cw_scratch, m.d_ckv_w, True)

    def weight():
        return m.weight[...].reshape(D, D)

    def give(a, value):
        if fused:
            wides[a].parts[0] = value.reshape(wides[a].parts.shape[1:])
            wides[a].to_group(0)
        else:
            d_wide[a][...] = value


    wait_all(ones)
    unit_three, scale_three = unit_of(m.middle[...])
    dn3 = m.dn3[...]
    d_gain = jnp.sum(dn3 * unit_three, axis=0, keepdims=True)
    m.d_middle[...] = m.cot[...] + unit_backward(dn3 * m.gain[...], unit_three, scale_three)
    if fused:
        load_out.wait()
        for o in range(G):
            out_sum.offer(o)
    load(2).wait()
    m.d_after[...] = mm_nt(m.d_middle[...], weight())
    load(1).start()
    wait_all(twos)
    enc_rows = ckv_sum.parts.shape[3]
    enc_count = n * enc_rows
    for h in range(0, H, 2):
        outs = []
        for a in (h, h + 1):
            span = slice(2 * a * dh, 2 * (a + 1) * dh)
            ckv = m.ckv[:, 0, :, span].reshape(enc_count, 2 * dh)
            probs = m.probs[a]
            grad = beside(m.d_after[:, a * dh : (a + 1) * dh], 1)
            d_probs = mm_nt(ckv, grad)
            delta = jnp.sum(probs * d_probs, axis=0, keepdims=True)
            d_scores = probs * (d_probs - delta)
            cq = beside(m.cq[:, a * dh : (a + 1) * dh], 0)
            d_ckv = mm(jnp.concatenate([d_scores, probs], axis=1), jnp.concatenate([cq, grad], axis=0))
            ckv_sum.parts[:, :, :, :, span] = d_ckv.reshape(G, R, 1, enc_rows, 2 * dh)
            outs.append(mm_tn(ckv, d_scores)[:dh, :].T)
        m.d_cq[:, h * dh : (h + 2) * dh] = jnp.concatenate(outs, axis=1)
    for o in range(G):
        ckv_sum.offer(o)
    if fused:
        out_sum.pooled(lookup(out_sum.far_first, g, 0))
    give(2, mm_tn(m.cflat[...], m.d_middle[...]))
    load(1).wait()
    unit_two, scale_two = unit_of(m.after[...])
    d_unit = mm_nt(m.d_cq[...], weight())
    load(0).start()
    m.d_after[...] = m.d_middle[...] + unit_backward(d_unit, unit_two, scale_two)
    for o in range(G):
        ckv_sum.pooled(o)
    if fused:
        wides[2].to_replicas()
    give(1, mm_tn(unit_two, m.d_cq[...]))
    load(0).wait()
    d_att = mm_nt(m.d_after[...], weight())
    for i in range(G):
        m.d_att[i] = d_att[:, i * C : (i + 1) * C]
        lane_send(G, R, i, m.d_att, m.grad, m.att_sems)
    if fused:
        for t in range(1, G):
            out_sum.pooled(lookup(out_sum.far_first, g, t))
        wides[1].to_replicas()
    attended = jnp.concatenate([m.rows[i] for i in range(G)], axis=1)
    give(0, mm_tn(attended, m.d_after[...]))
    if fused:
        out_sum.hand_on(0)
    wait_all(threes)
    make_strips(R, heads, T, m.vec, m.strip)
    m.near[...] = jnp.zeros_like(m.near)
    m.far[...] = jnp.zeros_like(m.far)
    ckv_sum.hand_on(0)
    if fused:
        wides[0].to_replicas()
    ckv_sum.hand_on(1)
    lane_wait(G, R, m.d_att, m.grad, m.att_sems)

    def dkv_copy(i, j):
        return remote(
            m.dkv_parts.at[i, lax.rem(r + j, R)],
            m.dkv_pool.at[j - 1, i],
            m.dkv_send.at[j - 1, i],
            m.dkv_recv.at[j - 1, i],
            groups[j - 1],
        )

    dqkv = m.dqkv

    def own_gradient(i):
        for j in range(1, R):
            dkv_copy(i, j).wait_recv()
        dkv = m.dkv_parts[i, r]
        for j in range(1, R):
            dkv = dkv + m.dkv_pool[j - 1, i]
        dqkv[i, :, : 2 * C] = dkv

    for i in range(G - 1, -1, -1):
        L = R * (i + 1) * T
        grad = m.grad[i]
        prod_t = (grad * m.att[i]).T
        dqs = []
        for h in range(heads):
            scores = strip_scores(R, T, i, r, h, L, m.kv, m.q, m.strip)
            probs = jnp.exp(scores - m.lse[i, h : h + 1, :])
            grad_h = beside(grad[:, h * dh : (h + 1) * dh], 1)
            delta = jnp.sum(prod_t[h * dh : (h + 1) * dh, :], axis=0, keepdims=True)
            d_scores = probs * (mm_nt(m.kv[h, :L, :], grad_h) - delta)
            q_h = m.q[h, i * T : (i + 1) * T, :]
            dkv = mm(
                jnp.concatenate([d_scores, probs], axis=1), jnp.concatenate([q_h, grad_h], axis=0)
            )
            if i == G - 1:
                m.dkv[h] = dkv
            else:
                m.dkv[h, :L, :] += dkv
            dqs.append(mm_tn(m.kv[h, :L, :], d_scores)[:dh, :].T)
            skip = 1 if i == 0 else 0
            width = (R + 1 - skip) * T
            m.near[h, skip * T :, :] += d_scores[L - width :, :]
            if width < L:
                m.far[h : h + 1, :] += jnp.sum(d_scores[: L - width, :], axis=0, keepdims=True)
        m.dqkv[i, :, 2 * C :] = jnp.concatenate(dqs, axis=1)
        for b in range(R):
            rows = slice((i * R + b) * T, (i * R + b + 1) * T)
            m.dkv_parts[i, b] = jnp.concatenate([m.dkv[h, rows, :] for h in range(heads)], axis=1)
        for j in range(1, R):
            dkv_copy(i, j).start()
        if i < G - 1:
            own_gradient(i + 1)
        if i == 3:
            ckv_sum.hand_on(2)
        if i == 2:
            ckv_sum.collect(m.ckv_all.at[f])
            ckv_chain.start()
        if i == 1:
            ckv_chain.arrive(0)
            ckv_chain.arrive(1)
    own_gradient(0)
    wait_all(fours)
    if fused:
        for index in range(1, G - 1):
            out_sum.hand_on(index)
        wides[2].to_owner()
    w = m.w[...].reshape(D, 3 * C)
    for i in range(G):
        du_parts[i, 0] = mm_nt(dqkv[i], w).reshape(du_parts.shape[2:])
        du_sum.pooled(i)
    d_w.parts[0] = mm_tn(m.own[...], dqkv[...].reshape(G * T, 3 * C)).reshape(d_w.parts.shape[1:])
    d_w.to_group(0)
    if fused:
        wides[1].to_owner()
        wides[2].to_everyone()

    ids = jnp.broadcast_to(m.ids[0:1, :], (2 * T, 3 * T))
    ids = pltpu.roll(ids, 0, 1, stride=1, stride_axis=0)[:, :T]
    each = buckets // n
    tiny_parts = m.tiny_parts
    tiny_parts[...] = jnp.zeros_like(tiny_parts)
    for h in range(heads):
        pair = m.near[h, pl.ds(pl.multiple_of(r * T, T), 2 * T), :]
        far = m.far[h : h + 1, :]
        for idx in range(R - 1):
            block = jnp.sum(m.near[h, idx * T : (idx + 1) * T, :], axis=0, keepdims=True)
            far = far + jnp.where(idx < r, block, 0.0)
        for b in range(buckets):
            part = jnp.sum(jnp.where(ids == b, pair, 0.0), axis=0, keepdims=True)
            if b == buckets - 1:
                part = part + far
            row = h * each + b % each
            tiny_parts[b // each, row : row + 1, :] = part
    last = heads * each
    for o in range(n):
        tiny_parts[o, last : last + 1, :Dn] = d_gain[:, o * Dn : (o + 1) * Dn]
    tiny = Deal(n, tiny_parts, m.tiny_in, m.tiny_sems)
    tiny.start()

    du_sum.hand_on(0)
    d_w.to_replicas()
    ckv_chain.arrive(2)
    ckv_chain.arrive(3)
    if fused:
        wides[0].to_owner()
    d_w.to_owner()
    if fused:
        wides[1].to_everyone()
    du_sum.hand_on(1)
    d_ckv = m.ckv_all[...].reshape(enc_count, 2 * D)
    m.enc_parts[...] = mm_nt(d_ckv, m.ckv_w[...]).reshape(m.enc_parts.shape)
    d_enc = Deal(n, m.enc_parts, m.d_enc, m.enc_sems)
    d_enc.start()
    enc_cols = m.small_all[:, :enc_rows, :].reshape(enc_count, Dn)
    d_cw.parts[0, 0, 0] = mm_tn(enc_cols, d_ckv).reshape(d_cw.parts.shape[3:])
    d_cw.to_replicas()
    d_w.to_everyone()
    if fused:
        wides[0].to_everyone()
    for index in range(2, G - 1):
        du_sum.hand_on(index)
    tiny.arrive()
    for s in range(G):
        total = m.tiny_in[s * R]
        for j in range(1, R):
            total = total + m.tiny_in[s * R + j]
        m.tiny[rep, s] = total

    def tiny_copy(j):
        part = m.tiny.at[rep]
        return remote(part, part, m.tiny_rep_send.at[j - 1], m.tiny_rep_recv.at[j - 1], reps[j - 1])

    for j in range(1, Q):
        tiny_copy(j).start()
    d_cw.to_owner()
    d_cw.to_everyone()
    if fused:
        out_sum.collect(m.out)
        m.out[...] += m.middle[...].reshape(m.out.shape)
    du_sum.collect(m.du)
    unit_one, scale_one = unit_of(m.x[...])
    d_unit = m.du[...].reshape(T, D)
    m.d_x[...] = m.d_after[...] + unit_backward(d_unit, unit_one, scale_one)

    d_enc.arrive()
    for a in range(3):
        ffn_own(a).wait()
        for j in range(1, Q):
            ffn_copy(a, j).wait()
    for j in range(1, Q):
        tiny_copy(j).wait()
    tiny.finish()
    d_enc.finish()
    for i in range(G):
        for j in range(1, R):
            dkv_copy(i, j).wait_send()
    if fused:
        out_sum.finish()
        for fold in wides:
            fold.finish()
    ckv_sum.finish()
    du_sum.finish()
    ckv_chain.finish()
    d_w.finish()
    d_cw.finish()


def back_stage(G, R, Q, H, dh, buckets, near_ins, far_ins, collective_id):
    T, D = near_ins["x"].shape
    n = G * R
    S = n * T
    heads = H // G
    C = heads * dh
    Dn = D // n
    part = Dn // Q
    enc_rows = near_ins["ckv"].shape[2]
    block = (pieces, T // pieces, D)
    tiny_rows = -(-(heads * (buckets // n) + 1) // 8) * 8
    sem = pltpu.SemaphoreType.DMA
    some = max(R - 1, 1)
    fused = R <= 2
    far_outs = dict(
        d_gate=(Q,) + far_ins["d_gate_in"].shape,
        d_up=(Q,) + far_ins["d_up_in"].shape,
        d_down=(Q,) + far_ins["d_down_in"].shape,
    )
    outs = dict(
        d_x=(T, D),
        out=block,
        d_w=(Q, G, 1, part, 3 * C),
        d_wide0=(Q, 1, part, D) if fused else (D, D),
        d_wide1=(Q, 1, part, D) if fused else (D, D),
        d_wide2=(Q, 1, part, D) if fused else (D, D),
        d_ckv_w=(Q, 1, part, 2 * D),
        d_enc=(n, enc_rows, Dn),
        tiny=(Q, G, tiny_rows, T),
    )
    scratch = dict(
        d_middle=pltpu.VMEM((T, D), F32),
        d_cq=pltpu.VMEM((T, D), F32),
        d_after=pltpu.VMEM((T, D), F32),
        d_att=pltpu.VMEM((G, T, C), F32),
        weight=pltpu.VMEM((n, Q, part, D), F32),
        load_sem=sem,
        ffn_sems=(sem((3, Q - 1)), sem((3, Q - 1)), sem((3,))),
        out_sem=sem,
        strip=pltpu.VMEM((heads, 2 * R * T, T), F32),
        near=pltpu.VMEM((heads, (R + 1) * T, T), F32),
        far=pltpu.VMEM((8, T), F32),
        dkv=pltpu.VMEM((heads, S, 2 * dh), F32),
        dqkv=pltpu.VMEM((G, T, 3 * C), F32),
        grad=pltpu.VMEM((G, T, C), F32),
        dkv_parts=pltpu.VMEM((G, R, T, 2 * C), F32),
        dkv_pool=pltpu.VMEM((some, G, T, 2 * C), F32),
        dkv_send=sem((some, G)),
        dkv_recv=sem((some, G)),
        tiny_parts=pltpu.VMEM((n, tiny_rows, T), F32),
        tiny_in=pltpu.VMEM((n, tiny_rows, T), F32),
        tiny_sems=deal_sems(n),
        tiny_rep_send=sem((Q - 1,)),
        tiny_rep_recv=sem((Q - 1,)),
        enc_parts=pltpu.VMEM((n, enc_rows, Dn), F32),
        enc_sems=deal_sems(n),
        ckv_all=pltpu.VMEM((n, 1, enc_rows, 2 * D), F32),
        ckv_chain_sems=chain_sems(G, R, 1),
        att_sems=lane_sems(G),
        du=pltpu.VMEM(block, F32),
        ckv_scratch=tuple(reduce_scratch(G, R, 1, (enc_rows, 2 * D))),
        du_scratch=tuple(reduce_scratch(G, 1, pieces, (T, D))),
        dw_scratch=fold_scratch(1, G, R, Q, part, 3 * C),
        cw_scratch=fold_scratch(1, 1, 1, Q, part, 2 * D),
    )
    if fused:
        scratch |= dict(
            wide_scratch=tuple(fold_scratch(1, G, R, Q, part, D) for _ in range(3)),
            out_scratch=tuple(reduce_scratch(G, R, pieces, (T, D))),
        )
    results = call_stage(
        functools.partial(back_kernel, G, R, Q, H, dh, buckets, fused),
        {},
        far_ins,
        outs,
        far_outs,
        scratch,
        collective_id,
        fetched=near_ins,
    )
    if not fused:
        out = scatter(G, R, far_ins["out_parts"].reshape(G, R, T, D), True, True, collective_id + 1)
        results.out = out + near_ins["middle"]
        total = jnp.concatenate([results.d_wide0, results.d_wide1, results.d_wide2], axis=1)
        total = lax.psum_scatter(total, "fsdp", scatter_dimension=0, tiled=True)
        total = lax.psum(total, "rep")
        results.d_wide0, results.d_wide1, results.d_wide2 = jnp.split(total, 3, axis=1)
    return results


def last_kernel(Q, H, dh, names, *refs):
    m = named(names, refs)
    m.o_gate[...] = m.d_gate[...]
    m.o_up[...] = m.d_up[...]
    m.o_down[...] = m.d_down[...]
    m.o_x[...] = m.d_x[...]
    m.o_out[...] = m.out[...]
    G, part = m.d_w.shape[1], m.d_w.shape[3]
    heads = H // G
    C = heads * dh
    Dn, D = m.self_query.shape
    for q in range(Q):
        rows = slice(q * part, (q + 1) * part)
        for o in range(G):
            m.o_sq[rows, o * C : (o + 1) * C] = m.d_w[q, o, 0, :, 2 * C :]
            for h in range(heads):
                both = m.d_w[q, o, 0, :, 2 * h * dh : 2 * (h + 1) * dh]
                span = slice((o * heads + h) * dh, (o * heads + h + 1) * dh)
                m.o_sk[rows, span] = both[:, :dh]
                m.o_sv[rows, span] = both[:, dh:]
        for h in range(H):
            both = m.d_ckv_w[q, 0, :, 2 * h * dh : 2 * (h + 1) * dh]
            m.o_ck[rows, h * dh : (h + 1) * dh] = both[:, :dh]
            m.o_cv[rows, h * dh : (h + 1) * dh] = both[:, dh:]
        m.o_so[rows, :] = m.d_wide0[q, 0]
        m.o_cq[rows, :] = m.d_wide1[q, 0]
        m.o_co[rows, :] = m.d_wide2[q, 0]

    def row_sums(a):
        ones = jnp.ones((8, a.shape[1]), F32)
        return lax.dot_general(
            ones, a, (((1,), (1,)), ((), ())), precision=lax.Precision.HIGHEST, preferred_element_type=F32
        )[:1]

    products = m.o_sq[...] * m.self_query[...] + m.o_sk[...] * m.self_key[...] + m.o_sv[...] * m.self_value[...]
    m.o_g_self[...] = row_sums(products)
    m.o_g_cross[...] = row_sums(m.o_cq[...] * m.cross_query[...])
    self_gain = as_column(m.self_gain[...], 0, Dn)
    for ref in (m.o_sq, m.o_sk, m.o_sv):
        ref[...] = ref[...] * self_gain
    m.o_cq[...] = m.o_cq[...] * as_column(m.cross_gain[...], 0, Dn)
    n = m.d_enc.shape[0]
    m.o_enc[...] = jnp.concatenate([m.d_enc[o] for o in range(n)], axis=1)
    each = m.o_bias.shape[0]
    tiny_rows = m.tiny.shape[2]
    last = heads * each
    g_ffn = jnp.zeros((1, Dn), F32)
    bias = jnp.zeros((each, H), F32)
    row = lax.broadcasted_iota(jnp.int32, (tiny_rows, H), 0)
    column = lax.broadcasted_iota(jnp.int32, (tiny_rows, H), 1)
    to = lax.broadcasted_iota(jnp.int32, (each, tiny_rows), 0)
    of = lax.broadcasted_iota(jnp.int32, (each, tiny_rows), 1)
    pick = jnp.where(jnp.logical_and(of < last, lax.rem(of, each) == to), 1.0, 0.0)
    for o in range(G):
        total = m.tiny[0, o]
        for q in range(1, Q):
            total = total + m.tiny[q, o]
        g_ffn = g_ffn + total[last : last + 1, :Dn]
        sums = jnp.sum(total, axis=1, keepdims=True)
        held = jnp.logical_and(row < last, column == o * heads + row // each)
        bias = bias + lax.dot_general(
            pick,
            jnp.where(held, sums, 0.0),
            (((1,), (0,)), ((), ())),
            precision=lax.Precision.HIGHEST,
            preferred_element_type=F32,
        )
    m.o_g_ffn[...] = g_ffn
    m.o_bias[...] = bias


def last_stage(Q, H, dh, each, near_ins):
    Dn, D = near_ins["self_query"].shape
    enc_rows = near_ins["d_enc"].shape[1]
    near = dict(o_sq=(Dn, D), o_sk=(Dn, D), o_sv=(Dn, D), o_so=(Dn, D), o_cq=(Dn, D), o_ck=(Dn, D))
    near |= dict(o_cv=(Dn, D), o_co=(Dn, D), o_enc=(enc_rows, D), o_bias=(each, H))
    near |= dict(o_g_self=(1, Dn), o_g_cross=(1, Dn), o_g_ffn=(1, Dn))
    near |= dict(o_gate=near_ins["d_gate"].shape, o_up=near_ins["d_up"].shape)
    near |= dict(o_down=near_ins["d_down"].shape, o_x=near_ins["d_x"].shape, o_out=near_ins["out"].shape)
    return call_stage(functools.partial(last_kernel, Q, H, dh), near_ins, {}, near, {}, {}, None)


def shards(
    n,
    inputs,
    encoder,
    self_gain,
    cross_gain,
    ffn_gain,
    self_query,
    self_key,
    self_value,
    self_output,
    position_bias,
    bucket_table,
    cross_query,
    cross_key,
    cross_value,
    cross_output,
    ffn_gate,
    ffn_up,
    ffn_down,
    cotangent,
):
    x = inputs[0]
    enc = encoder[0]
    cot = cotangent[0]
    T, D = x.shape
    buckets, H = position_bias.shape
    dh = D // H
    G = math.gcd(H, n)
    R = n // G
    heads = H // G
    C = heads * dh
    Dn = D // n
    enc_local = enc.shape[0]
    Q = lax.axis_size("rep")
    part = Dn // Q

    def quarters(w):
        return w.reshape(Q, part, D)

    near_ins = dict(
        x=x,
        enc=enc,
        ffn_gain=ffn_gain.reshape(1, Dn),
        position_bias=position_bias.T,
        table=bucket_table.reshape(1, -1),
        self_gain=self_gain.reshape(1, Dn),
        cross_gain=cross_gain.reshape(1, Dn),
        cross_key=cross_key,
        cross_value=cross_value,
        cot=cot.reshape(pieces, T // pieces, D),
    )
    far_ins = dict(
        self_query=quarters(self_query),
        self_key=quarters(self_key),
        self_value=quarters(self_value),
        so=quarters(self_output),
        cq_w=quarters(cross_query),
        co=quarters(cross_output),
    )
    first = first_stage(G, R, Q, H, dh, near_ins, far_ins, 1)
    dn3, out_parts, d_gate, d_up, d_down = ffn_stage(
        G, R, Q, first.n3, first.cot_all, ffn_gate, ffn_up, ffn_down, 3
    )
    near_ins = dict(vars(first), x=x, cot=cot, dn3=dn3)
    del near_ins["wide"], near_ins["cot_all"], near_ins["n3"]
    far_ins = dict(
        wide=first.wide, out_parts=out_parts, d_gate_in=d_gate, d_up_in=d_up, d_down_in=d_down
    )
    back = back_stage(G, R, Q, H, dh, buckets, near_ins, far_ins, 5)

    near_ins = dict(
        d_gate=back.d_gate.reshape(ffn_gate.shape),
        d_up=back.d_up.reshape(ffn_up.shape),
        d_down=back.d_down.reshape(ffn_down.shape),
        d_x=back.d_x,
        out=back.out.reshape(T, D),
        d_w=back.d_w,
        d_ckv_w=back.d_ckv_w,
        d_wide0=back.d_wide0.reshape(Q, 1, part, D),
        d_wide1=back.d_wide1.reshape(Q, 1, part, D),
        d_wide2=back.d_wide2.reshape(Q, 1, part, D),
        d_enc=back.d_enc,
        tiny=back.tiny,
        self_query=self_query,
        self_key=self_key,
        self_value=self_value,
        cross_query=cross_query,
        self_gain=self_gain.reshape(1, Dn),
        cross_gain=cross_gain.reshape(1, Dn),
    )
    done = last_stage(Q, H, dh, buckets // n, near_ins)
    return (
        done.o_out[None],
        done.o_x[None],
        done.o_enc[None],
        done.o_g_self.reshape(Dn),
        done.o_g_cross.reshape(Dn),
        done.o_g_ffn.reshape(Dn),
        done.o_sq,
        done.o_sk,
        done.o_sv,
        done.o_so,
        done.o_bias,
        done.o_cq,
        done.o_ck,
        done.o_cv,
        done.o_co,
        done.o_gate,
        done.o_up,
        done.o_down,
    )


def solution(mesh):
    rows = P("rep", "fsdp", None)
    gain = P("fsdp")
    weight = P("fsdp", None)
    columns = P(None, "fsdp")
    args = (rows, rows, gain, gain, gain) + (weight,) * 4 + (P(), P()) + (weight,) * 4
    args += (columns, columns, weight, rows)
    outs = (rows, rows, rows, gain, gain, gain) + (weight,) * 9 + (columns, columns, weight)
    return jax.shard_map(
        functools.partial(shards, mesh.shape["fsdp"]),
        mesh=mesh,
        in_specs=args,
        out_specs=outs,
        check_vma=False,
    )
```
